128 devices in a mesh: row: 16 (over y, z), col: 8 (over x, core).
Axes of the slice: x: 4, y: 4, z: 4, core: 2. Of those that a mesh axis runs over, the one named last changes fastest.
Arguments:
- momentum: float32 [8192, 16384], P('row', 'col'), may hold values from -6 to 6
- grads: bfloat16 [2, 8192, 16384], P(None, 'row', 'col'), may hold values from -400 to 400
- basis: float32 [16384, 256], P('col'), may hold values from -0.046875 to 0.046875
Outputs:
- change: bfloat16 [8192, 16384], P('row', 'col')
- state: float32 [8192, 16384], P('row', 'col')
The draws below stay inside these ranges and needn't reach their ends.
All inputs are finite; a program needn't handle non-finite values.
Results may differ from the reference program's by a relative error of at most 0.0035.
Values sent between devices are 32-bit elements; how exact they have to be, the bound alone decides.
No kernel may reach another device: no remote copies, remote signals or barrier semaphores. Data moves between devices by JAX's collectives and lax.ppermute only.
A program may use at most 128 MiB of HBM per device.

```python
import jax
import jax.numpy as jnp
from jax import lax

ROWS = 8192
COLS = 16384
RANK = 256
STEPS = 2


def draw_grads(key, part):
    row_key = jax.random.fold_in(key, 11)
    col_key = jax.random.fold_in(key, 12)
    base_key = jax.random.fold_in(key, 13)
    row_scale = jnp.exp(jax.random.uniform(row_key, (1, ROWS, 1), jnp.float32, jnp.log(0.3), jnp.log(3.0)))
    col_scale = jnp.exp(jax.random.uniform(col_key, (1, 1, COLS), jnp.float32, jnp.log(0.3), jnp.log(3.0)))
    values = jax.random.normal(base_key, (STEPS, ROWS, COLS), jnp.float32) * row_scale * col_scale
    return jnp.clip(values, -400.0, 400.0).astype(jnp.bfloat16)


def shard_levels(key, dims, shards, least, high):
    gain = 1.0
    for dim, blocks in shards:
        draws = jax.random.uniform(jax.random.fold_in(jax.random.fold_in(key, 6), dim), (blocks,), jnp.float32, least / len(shards), high / len(shards))
        gain = gain * jnp.repeat(jnp.exp(draws), dims[dim] // blocks).reshape((-1,) + (1,) * (len(dims) - 1 - dim))
    return gain


def gaussian(stream_key, shape, deviation, limit, pieces=(), dtype=jnp.bfloat16):
    gain = shard_levels(stream_key, shape, pieces, -0.22, 0.18) if pieces else 1.0
    entries = jax.random.normal(stream_key, shape, jnp.float32) * deviation * gain
    return jnp.minimum(jnp.maximum(entries, -limit), limit).astype(dtype)


def setup_inputs(seed: int = 0) -> dict:
    arg_keys = jax.random.split(jax.random.key(seed), 4)
    return {
        "momentum": gaussian(arg_keys[0], (ROWS, COLS), 1.0, 6.0, ((0, 16), (1, 8)), jnp.float32),
        "grads": draw_grads(jax.random.fold_in(arg_keys[3], 71), 0),
        "basis": gaussian(arg_keys[2], (COLS, RANK), COLS ** -0.5, 0.046875, ((0, 8),), jnp.float32),
    }


keep_rate = 0.95
norm_eps = 1e-06

def reference(momentum, grads, basis):
    high = lax.Precision.HIGHEST
    factor = (ROWS * COLS / RANK) ** 0.5
    state = momentum
    right = basis
    change = jnp.zeros(momentum.shape, jnp.float32)
    for step in range(STEPS):
        buffer = state + grads[step].astype(jnp.float32)
        projected = jnp.dot(buffer.astype(jnp.float32), right.astype(jnp.float32), precision=high, preferred_element_type=jnp.float32)
        gram = jnp.dot(projected.T.astype(jnp.float32), projected.astype(jnp.float32), precision=high, preferred_element_type=jnp.float32)
        lower = jnp.linalg.cholesky(gram)
        ortho = jax.scipy.linalg.solve_triangular(lower, projected.T, lower=True).T
        raw = lax.dot_general(buffer.astype(jnp.float32), ortho.astype(jnp.float32), (((0,), (0,)), ((), ())), precision=high, preferred_element_type=jnp.float32)
        scale = lax.rsqrt(lax.optimization_barrier(jnp.sum(raw * raw, axis=0)) + norm_eps)
        right = raw * scale
        state = buffer - (1.0 - keep_rate) * jnp.dot(ortho.astype(jnp.float32), raw.T.astype(jnp.float32), precision=high, preferred_element_type=jnp.float32)
        change = change + factor * jnp.dot(ortho.astype(jnp.float32), right.T.astype(jnp.float32), precision=high, preferred_element_type=jnp.float32)
    return (change.astype(jnp.bfloat16), state)
```

```python
import functools

import jax
import jax.numpy as jnp
from jax import lax
from jax.experimental import pallas as pl
from jax.experimental.pallas import tpu as pltpu
from jax.sharding import PartitionSpec as P

KEEP_RATE = 0.95
NORM_EPS = 1e-06
STEPS = 2
LANES = 128
F32 = jnp.float32
BF16 = jnp.bfloat16
VMEM_LIMIT = 48 * 1024 * 1024
NN = (((1,), (0,)), ((), ()))
NT = (((1,), (1,)), ((), ()))


def split(x):
    high = x.astype(BF16)
    return high, (x - high.astype(F32)).astype(BF16)


def mm(a, b, dims):
    return lax.dot_general(a, b, dims, preferred_element_type=F32)


def dot3(a, b, dims):
    return mm(a[0], b[0], dims) + (mm(a[0], b[1], dims) + mm(a[1], b[0], dims))


def exact(a, b, dims):
    return lax.dot_general(
        a, b, dims, precision=lax.Precision.HIGHEST, preferred_element_type=F32
    )


def call(kernel, grid, in_specs, out_specs, out_shape, scratch, cost):
    return pl.pallas_call(
        kernel,
        grid=grid,
        in_specs=in_specs,
        out_specs=out_specs,
        out_shape=out_shape,
        scratch_shapes=scratch,
        compiler_params=pltpu.CompilerParams(vmem_limit_bytes=VMEM_LIMIT),
        cost_estimate=pl.CostEstimate(
            flops=cost, transcendentals=0, bytes_accessed=8 * 1024 * 1024
        ),
    )


def whole(shape):
    return pl.BlockSpec(shape, lambda i: (0,) * len(shape))


def first_kernel(m_ref, g_ref, v_ref, p_ref, vh, vl):
    @pl.when(pl.program_id(0) == 0)
    def _():
        vh[...], vl[...] = split(v_ref[...])

    b = split(m_ref[...] + g_ref[0].astype(F32))
    p_ref[...] = dot3(b, (vh[...], vl[...]), NN)


def first_projection(momentum, grads, basis):
    rows, cols = momentum.shape
    rank = basis.shape[1]
    bm = rows // 4
    return call(
        first_kernel,
        (4,),
        [
            pl.BlockSpec((bm, cols), lambda i: (i, 0)),
            pl.BlockSpec((1, bm, cols), lambda i: (0, i, 0)),
            whole(basis.shape),
        ],
        pl.BlockSpec((bm, rank), lambda i: (i, 0)),
        jax.ShapeDtypeStruct((rows, rank), F32),
        [pltpu.VMEM(basis.shape, BF16)] * 2,
        6 * rows * cols * rank,
    )(momentum, grads, basis)


def store_products(p, b, x_ref, pt, gram, blocks):
    rank = p.shape[1]
    share = rank // 16

    @pl.when(pl.program_id(0) == 0)
    def _():
        turned = p.T
        pt[0], pt[1] = split(turned)
        gram[...] = exact(turned, p, NN)

    r = dot3((pt[0], pt[1]), split(b), NN)
    for k in range(blocks):
        x_ref[k, :rank] = r[:, k * LANES : (k + 1) * LANES]
        first = pl.multiple_of((pl.program_id(0) * blocks + k) * share, share)
        for part in range(rank // LANES):
            x_ref[k, rank + part * share : rank + (part + 1) * share] = gram[
                pl.ds(first, share), part * LANES : (part + 1) * LANES
            ]


def raw_first_kernel(blocks, p_ref, m_ref, g_ref, x_ref, pt, gram):
    store_products(
        p_ref[...], m_ref[...] + g_ref[0].astype(F32), x_ref, pt, gram, blocks
    )


def raw_second_kernel(blocks, p_ref, rs_ref, b_ref, x_ref, pt, gram):
    store_products(p_ref[...] * rs_ref[:1], b_ref[...], x_ref, pt, gram, blocks)


def raw_products(kernel, p, small, bigs, big_specs, cols):
    rows, rank = p.shape
    blocks = 4
    steps = cols // LANES // blocks
    height = rank + rank * (rank // 16) // LANES
    return call(
        functools.partial(kernel, blocks),
        (steps,),
        [whole(p.shape)] + [whole(s.shape) for s in small] + big_specs(rows, blocks * LANES),
        pl.BlockSpec((blocks, height, LANES), lambda i: (i, 0, 0)),
        jax.ShapeDtypeStruct((cols // LANES, height, LANES), F32),
        [pltpu.VMEM((2, rank, rows), BF16), pltpu.VMEM((rank, rank), F32)],
        6 * rows * cols * rank,
    )(p, *small, *bigs)


def eliminated(m):
    n = m.shape[0]
    lane = lax.broadcasted_iota(jnp.int32, (8, n), 1)
    sub = lax.broadcasted_iota(jnp.int32, (8, n), 0)
    tiles = [m[8 * t : 8 * t + 8] for t in range(n // 8)]
    for j in range(n):
        t, r = divmod(j, 8)
        row = tiles[t][r : r + 1]
        inv = 1.0 / row[:, j : j + 1]
        here = lane == j
        scaled = jnp.where(here[:1], inv, row * inv)
        for s in range(t, n // 8):
            column = jnp.broadcast_to(tiles[s][:, j : j + 1], (8, n))
            new = jnp.where(here, 0.0, tiles[s]) - column * scaled
            if s == t:
                new = jnp.where(sub > r, new, tiles[s])
            tiles[s] = new
    m = jnp.concatenate(tiles, axis=0)
    i = lax.broadcasted_iota(jnp.int32, (n, n), 0)
    j = lax.broadcasted_iota(jnp.int32, (n, n), 1)
    pivots = jnp.sum(jnp.where(i == j, m, 0.0), axis=1, keepdims=True)
    unit = jnp.where(i > j, m, jnp.where(i == j, 1.0, 0.0))
    return unit * lax.rsqrt(pivots)


def cholesky_kernel(g_ref, w_ref, a, low):
    count, height, _ = g_ref.shape
    share = height // 2
    half = LANES
    for k in range(count):
        for part in range(2):
            a[k * share : (k + 1) * share, part * half : (part + 1) * half] = g_ref[
                k, part * share : (part + 1) * share
            ]

    def body(b, carry):
        first = pl.multiple_of(b * half, half)
        w = eliminated(a[pl.ds(first, half), pl.ds(first, half)])
        w_ref[pl.ds(first, half), pl.ds(first, half)] = w

        @pl.when(b == 0)
        def _():
            low[...] = exact(a[half:, :half], w, NT)
            a[half:, half:] -= exact(low[...], low[...], NT)

        return carry

    lax.fori_loop(0, 2, body, 0)
    w_ref[:half, half:] = jnp.zeros((half, half), F32)
    w_ref[half:, :half] = -exact(
        w_ref[half:, half:], exact(low[...], w_ref[:half, :half], NN), NN
    )


def inverse_factor(gram):
    rank = 2 * LANES
    return call(
        cholesky_kernel,
        (1,),
        [whole(gram.shape)],
        whole((rank, rank)),
        jax.ShapeDtypeStruct((rank, rank), F32),
        [pltpu.VMEM((rank, rank), F32), pltpu.VMEM((LANES, LANES), F32)],
        10**10,
    )(gram)


def assemble_raw(w_ref, x_ref, raw_ref):
    count = x_ref.shape[0]
    w = split(w_ref[...])
    for k in range(0, count, 4):
        block = jnp.concatenate([x_ref[k + q] for q in range(4)], axis=1)
        raw_ref[:, k * LANES : (k + 4) * LANES] = dot3(w, split(block), NN)


def squares_of(raw):
    return jnp.sum(raw * raw, axis=1, keepdims=True)


def middle_kernel(p_ref, w_ref, x_ref, m_ref, g_ref, q_ref, raw_ref, o_ref, rt, s_ref):
    bm = m_ref.shape[0]
    step = pl.program_id(0)

    @pl.when(step == 0)
    def _():
        assemble_raw(w_ref, x_ref, raw_ref)
        raw = raw_ref[...]
        rt[0], rt[1] = split(raw)
        s = dot3((rt[0], rt[1]), (rt[0], rt[1]), NT)
        s_ref[...] = s
        o_ref[...] = exact(p_ref[...], w_ref[...], NT)
        n = s.shape[0]
        i = lax.broadcasted_iota(jnp.int32, (n, n), 0)
        j = lax.broadcasted_iota(jnp.int32, (n, n), 1)
        squares = jnp.sum(jnp.where(i == j, s, 0.0), axis=0, keepdims=True)
        for half in range(2):
            q_ref[half, q_ref.shape[1] - 8 :] = jnp.broadcast_to(squares, (8, n))

    b = m_ref[...] + g_ref[0].astype(F32) + g_ref[1].astype(F32)
    q = dot3(split(b), (rt[0], rt[1]), NT)
    first = pl.multiple_of(step * bm, bm)
    o = o_ref[pl.ds(first, bm), :]
    q = q - (1.0 - KEEP_RATE) * exact(o, s_ref[...], NN)
    per_half = (q_ref.shape[1] - 8) // bm
    q_ref[step // per_half, pl.ds(pl.multiple_of((step % per_half) * bm, bm), bm), :] = q


def middle(p, w, x, momentum, grads):
    rows, cols = momentum.shape
    rank = p.shape[1]
    bm = rows // 4
    return call(
        middle_kernel,
        (4,),
        [
            whole(p.shape),
            whole(w.shape),
            whole(x.shape),
            pl.BlockSpec((bm, cols), lambda i: (i, 0)),
            pl.BlockSpec((2, bm, cols), lambda i: (0, i, 0)),
        ],
        [whole((2, rows // 2 + 8, rank)), whole((rank, cols)), whole((rows, rank))],
        [
            jax.ShapeDtypeStruct((2, rows // 2 + 8, rank), F32),
            jax.ShapeDtypeStruct((rank, cols), F32),
            jax.ShapeDtypeStruct((rows, rank), F32),
        ],
        [pltpu.VMEM((2, rank, cols), BF16), pltpu.VMEM((rank, rank), F32)],
        10 * rows * cols * rank,
    )(p, w, x, momentum, grads)


def update_kernel(o_ref, raw_ref, m_ref, g_ref, b_ref):
    b = m_ref[...] + g_ref[0].astype(F32) + g_ref[1].astype(F32)
    o = split((1.0 - KEEP_RATE) * o_ref[...])
    b_ref[...] = b - dot3(o, split(raw_ref[...]), NN)


def second_buffer(o, raw, momentum, grads):
    rows, cols = momentum.shape
    rank = o.shape[1]
    bn = cols // 4
    return call(
        update_kernel,
        (4,),
        [
            whole(o.shape),
            pl.BlockSpec((rank, bn), lambda i: (0, i)),
            pl.BlockSpec((rows, bn), lambda i: (0, i)),
            pl.BlockSpec((2, rows, bn), lambda i: (0, 0, i)),
        ],
        pl.BlockSpec((rows, bn), lambda i: (0, i)),
        jax.ShapeDtypeStruct((rows, cols), F32),
        [],
        6 * rows * cols * rank,
    )(o, raw, momentum, grads)


def change_kernel(factor, o_ref, rs_ref, raw_ref, c_ref):
    o = split(o_ref[...] * (factor * rs_ref[:1]))
    c_ref[...] = dot3(o, split(raw_ref[...]), NN)


def first_change(factor, o, rs, raw):
    rows, rank = o.shape
    cols = raw.shape[1]
    bn = cols // 4
    return call(
        functools.partial(change_kernel, factor),
        (4,),
        [whole(o.shape), whole(rs.shape), pl.BlockSpec((rank, bn), lambda i: (0, i))],
        pl.BlockSpec((rows, bn), lambda i: (0, i)),
        jax.ShapeDtypeStruct((rows, cols), F32),
        [],
        6 * rows * cols * rank,
    )(o, rs, raw)


def last_raw_kernel(p_ref, rs_ref, w_ref, x_ref, raw_ref, o_ref, sq_ref):
    assemble_raw(w_ref, x_ref, raw_ref)
    raw = raw_ref[...]
    o_ref[...] = exact(p_ref[...] * rs_ref[:1], w_ref[...], NT)
    n = raw.shape[0]
    i = lax.broadcasted_iota(jnp.int32, (n, n), 0)
    j = lax.broadcasted_iota(jnp.int32, (n, n), 1)
    squares = jnp.where(i == j, jnp.broadcast_to(squares_of(raw), (n, n)), 0.0)
    row = jnp.sum(squares, axis=0, keepdims=True)
    for k in range(sq_ref.shape[0]):
        sq_ref[k] = jnp.broadcast_to(row, (8, n))


def last_raw(p, rs, w, x, peers):
    rows, rank = p.shape
    cols = x.shape[0] * LANES
    return call(
        last_raw_kernel,
        (1,),
        [whole(p.shape), whole(rs.shape), whole(w.shape), whole(x.shape)],
        [whole((rank, cols)), whole((rows, rank)), whole((peers, 8, rank))],
        [
            jax.ShapeDtypeStruct((rank, cols), F32),
            jax.ShapeDtypeStruct((rows, rank), F32),
            jax.ShapeDtypeStruct((peers, 8, rank), F32),
        ],
        [],
        3 * rows * cols * rank,
    )(p, rs, w, x)


def state_kernel(o_ref, raw_ref, b_ref, s_ref):
    o = split((1.0 - KEEP_RATE) * o_ref[...])
    s_ref[...] = b_ref[...] - dot3(o, split(raw_ref[...]), NN)


def last_state(o, raw, b):
    rows, cols = b.shape
    rank = o.shape[1]
    bn = cols // 4
    return call(
        state_kernel,
        (4,),
        [
            whole(o.shape),
            pl.BlockSpec((rank, bn), lambda i: (0, i)),
            pl.BlockSpec((rows, bn), lambda i: (0, i)),
        ],
        pl.BlockSpec((rows, bn), lambda i: (0, i)),
        jax.ShapeDtypeStruct((rows, cols), F32),
        [],
        6 * rows * cols * rank,
    )(o, raw, b)


def last_change_kernel(factor, o_ref, sq_ref, raw_ref, c_ref, out_ref):
    total = sq_ref[0, :1]
    for k in range(1, sq_ref.shape[0]):
        total = total + sq_ref[k, :1]
    o = split(o_ref[...] * (factor * lax.rsqrt(total + NORM_EPS)))
    out_ref[...] = (c_ref[...] + dot3(o, split(raw_ref[...]), NN)).astype(BF16)


def last_change(factor, o, sq, raw, change):
    rows, cols = change.shape
    rank = o.shape[1]
    bn = cols // 4
    return call(
        functools.partial(last_change_kernel, factor),
        (4,),
        [
            whole(o.shape),
            whole(sq.shape),
            pl.BlockSpec((rank, bn), lambda i: (0, i)),
            pl.BlockSpec((rows, bn), lambda i: (0, i)),
        ],
        pl.BlockSpec((rows, bn), lambda i: (0, i)),
        jax.ShapeDtypeStruct((rows, cols), BF16),
        [],
        6 * rows * cols * rank,
    )(o, sq, raw, change)


def exchange(x, axis, groups=None):
    return lax.all_to_all(x, axis, 0, 0, axis_index_groups=groups, tiled=True)


def copies(x, count):
    return jnp.broadcast_to(x[None], (count, *x.shape))


def col_sum(halves, axis):
    count = lax.axis_size(axis)
    swap = [(k, k ^ 1) for k in range(count)]
    even = [k for k in range(count) if k % 2 == 0]
    groups = [even, [k + 1 for k in even]]
    core = lax.axis_index(axis) % 2
    mine = lax.dynamic_index_in_dim(halves, core, 0, keepdims=False)
    theirs = lax.dynamic_index_in_dim(halves, 1 - core, 0, keepdims=False)
    mine = mine + lax.ppermute(theirs, axis, swap)
    mine = exchange(copies(mine, len(even)), axis, groups).sum(axis=0)
    theirs = lax.ppermute(mine, axis, swap)
    return jnp.where(core == 0, jnp.stack([mine, theirs]), jnp.stack([theirs, mine]))


def row_total(products, rank, axis):
    count = lax.axis_size(axis)
    own = exchange(products, axis).sum(axis=0)
    gram = exchange(copies(own[rank:], count), axis)
    raw = exchange(copies(own[:rank], count), axis)
    return gram, raw


def shards(momentum, grads, basis):
    rows, cols = momentum.shape
    rank = basis.shape[1]
    factor = (rows * lax.axis_size("row") * cols * lax.axis_size("col") / rank) ** 0.5

    p1 = first_projection(momentum, grads, basis)
    p1 = col_sum(p1.reshape(2, rows // 2, rank), "col").reshape(rows, rank)
    x1 = raw_products(
        raw_first_kernel,
        p1,
        [],
        [momentum, grads],
        lambda r, n: [
            pl.BlockSpec((r, n), lambda i: (0, i)),
            pl.BlockSpec((1, r, n), lambda i: (0, 0, i)),
        ],
        cols,
    )
    gram1, x1 = row_total(x1, rank, "row")
    w1 = inverse_factor(gram1)
    q2, raw1, o1 = middle(p1, w1, x1, momentum, grads)
    b2 = second_buffer(o1, raw1, momentum, grads)
    q2 = col_sum(q2, "col")
    p2 = q2[:, : rows // 2].reshape(rows, rank)
    rs1 = lax.rsqrt(q2[0, rows // 2 :] + NORM_EPS)
    x2 = raw_products(
        raw_second_kernel,
        p2,
        [rs1],
        [b2],
        lambda r, n: [pl.BlockSpec((r, n), lambda i: (0, i))],
        cols,
    )
    change1 = first_change(factor, o1, rs1, raw1)
    gram2, x2 = row_total(x2, rank, "row")
    w2 = inverse_factor(gram2)
    raw2, o2, sq2 = last_raw(p2, rs1, w2, x2, lax.axis_size("col"))
    sq2 = exchange(sq2, "col")
    state = last_state(o2, raw2, b2)
    change = last_change(factor, o2, sq2, raw2, change1)
    return change, state


def solution(mesh):
    return jax.shard_map(
        shards,
        mesh=mesh,
        in_specs=(P("row", "col"), P(None, "row", "col"), P("col", None)),
        out_specs=(P("row", "col"), P("row", "col")),
        check_vma=False,
    )
```

```python
import functools

import jax
import jax.numpy as jnp
from jax import lax
from jax.experimental import pallas as pl
from jax.experimental.pallas import tpu as pltpu
from jax.sharding import PartitionSpec as P

KEEP_RATE = 0.95
NORM_EPS = 1e-06
LANES = 128
GRID = 4
F32 = jnp.float32
BF16 = jnp.bfloat16
VMEM_LIMIT = 48 * 1024 * 1024
NN = (((1,), (0,)), ((), ()))
NT = (((1,), (1,)), ((), ()))


def split(x):
    high = x.astype(BF16)
    return high, (x - high.astype(F32)).astype(BF16)


def mm(a, b, dims):
    return lax.dot_general(a, b, dims, preferred_element_type=F32)


def dot3(a, b, dims):
    return mm(a[0], b[0], dims) + (mm(a[0], b[1], dims) + mm(a[1], b[0], dims))


def exact(a, b, dims):
    return lax.dot_general(
        a, b, dims, precision=lax.Precision.HIGHEST, preferred_element_type=F32
    )


def call(kernel, grid, in_specs, out_specs, out_shape, scratch, cost):
    return pl.pallas_call(
        kernel,
        grid=grid,
        in_specs=in_specs,
        out_specs=out_specs,
        out_shape=out_shape,
        scratch_shapes=scratch,
        compiler_params=pltpu.CompilerParams(vmem_limit_bytes=VMEM_LIMIT),
        cost_estimate=pl.CostEstimate(
            flops=cost, transcendentals=0, bytes_accessed=8 * 1024 * 1024
        ),
    )


def whole(shape):
    return pl.BlockSpec(shape, lambda i: (0,) * len(shape))


def first_kernel(m_ref, g_ref, v_ref, p_ref):
    b = split(m_ref[...] + g_ref[0].astype(F32))
    part = dot3(b, split(v_ref[...]), NN)

    @pl.when(pl.program_id(0) == 0)
    def _():
        p_ref[...] = part

    @pl.when(pl.program_id(0) > 0)
    def _():
        p_ref[...] += part


def first_projection(momentum, grads, basis):
    rows, cols = momentum.shape
    rank = basis.shape[1]
    bn = cols // GRID
    return call(
        first_kernel,
        (GRID,),
        [
            pl.BlockSpec((rows, bn), lambda i: (0, i)),
            pl.BlockSpec((1, rows, bn), lambda i: (0, 0, i)),
            pl.BlockSpec((bn, rank), lambda i: (i, 0)),
        ],
        whole((rows, rank)),
        jax.ShapeDtypeStruct((rows, rank), F32),
        [],
        6 * rows * cols * rank,
    )(momentum, grads, basis)


def gram_kernel(n_ref, p_ref, pt_ref, c_ref, scratch):
    turned = p_ref[...].T
    scratch[...] = turned
    pt_ref[0], pt_ref[1] = split(turned)
    size = c_ref.shape[0]
    first = pl.multiple_of(n_ref[0] * size, size)
    c_ref[...] = exact(scratch[pl.ds(first, size), :], p_ref[...], NN)


def gram_part(p, index, parts):
    rows, rank = p.shape
    return call(
        gram_kernel,
        (1,),
        [pl.BlockSpec(memory_space=pltpu.SMEM), whole(p.shape)],
        [whole((2, rank, rows)), whole((rank // parts, rank))],
        [
            jax.ShapeDtypeStruct((2, rank, rows), BF16),
            jax.ShapeDtypeStruct((rank // parts, rank), F32),
        ],
        [pltpu.VMEM((rank, rows), F32)],
        2 * rows * rank * rank,
    )(index, p)


def store_products(pt_ref, b, x_ref):
    r = dot3((pt_ref[0], pt_ref[1]), split(b), NN)
    for k in range(x_ref.shape[0]):
        x_ref[k] = r[:, k * LANES : (k + 1) * LANES]


def raw_first_kernel(pt_ref, m_ref, g_ref, x_ref):
    store_products(pt_ref, m_ref[...] + g_ref[0].astype(F32), x_ref)


def raw_second_kernel(pt_ref, b_ref, x_ref):
    store_products(pt_ref, b_ref[...], x_ref)


def raw_products(kernel, pt, bigs):
    _, rank, rows = pt.shape
    cols = bigs[0].shape[1]
    bn = cols // GRID
    specs = [
        pl.BlockSpec((rows, bn), lambda i: (0, i)),
        pl.BlockSpec((1, rows, bn), lambda i: (0, 0, i)),
    ]
    return call(
        kernel,
        (GRID,),
        [whole(pt.shape)] + specs[: len(bigs)],
        pl.BlockSpec((bn // LANES, rank, LANES), lambda i: (i, 0, 0)),
        jax.ShapeDtypeStruct((cols // LANES, rank, LANES), F32),
        [],
        6 * rows * cols * rank,
    )(pt, *bigs)


def spread_kernel(x_ref, y_ref):
    count = x_ref.shape[0]
    total = x_ref[0]
    for k in range(1, count):
        total = total + x_ref[k]
    for k in range(count):
        y_ref[k] = total


def spread_sum(x):
    count, height, width = x.shape
    spec = pl.BlockSpec((count, height // 4, width), lambda i: (0, i, 0))
    return call(
        spread_kernel, (4,), [spec], spec, jax.ShapeDtypeStruct(x.shape, F32), [], count * height * width
    )(x)


def eliminated(m):
    n = m.shape[0]
    lane = lax.broadcasted_iota(jnp.int32, (8, n), 1)
    sub = lax.broadcasted_iota(jnp.int32, (8, n), 0)
    tiles = [m[8 * t : 8 * t + 8] for t in range(n // 8)]
    for j in range(n):
        t, r = divmod(j, 8)
        row = tiles[t][r : r + 1]
        inv = 1.0 / row[:, j : j + 1]
        here = lane == j
        scaled = jnp.where(here[:1], inv, row * inv)
        for s in range(t, n // 8):
            column = jnp.broadcast_to(tiles[s][:, j : j + 1], (8, n))
            new = jnp.where(here, 0.0, tiles[s]) - column * scaled
            if s == t:
                new = jnp.where(sub > r, new, tiles[s])
            tiles[s] = new
    m = jnp.concatenate(tiles, axis=0)
    i = lax.broadcasted_iota(jnp.int32, (n, n), 0)
    j = lax.broadcasted_iota(jnp.int32, (n, n), 1)
    pivots = jnp.sum(jnp.where(i == j, m, 0.0), axis=1, keepdims=True)
    unit = jnp.where(i > j, m, jnp.where(i == j, 1.0, 0.0))
    return unit * lax.rsqrt(pivots)


def cholesky_kernel(n_ref, *refs):
    pieces, (w_ref, a, low) = refs[:-3], refs[-3:]
    size = pieces[0].shape[0]
    count = len(pieces)
    for k, piece in enumerate(pieces):
        place = lax.rem(n_ref[0] + k, count)
        a[pl.ds(pl.multiple_of(place * size, size), size), :] = piece[...]
    half = LANES

    def body(b, carry):
        first = pl.multiple_of(b * half, half)
        w = eliminated(a[pl.ds(first, half), pl.ds(first, half)])
        w_ref[pl.ds(first, half), pl.ds(first, half)] = w

        @pl.when(b == 0)
        def _():
            low[...] = exact(a[half:, :half], w, NT)
            a[half:, half:] -= exact(low[...], low[...], NT)

        return carry

    lax.fori_loop(0, 2, body, 0)
    w_ref[:half, half:] = jnp.zeros((half, half), F32)
    w_ref[half:, :half] = -exact(
        w_ref[half:, half:], exact(low[...], w_ref[:half, :half], NN), NN
    )


def inverse_factor(pieces, index):
    rank = pieces[0].shape[1]
    return call(
        cholesky_kernel,
        (1,),
        [pl.BlockSpec(memory_space=pltpu.SMEM)] + [whole(q.shape) for q in pieces],
        whole((rank, rank)),
        jax.ShapeDtypeStruct((rank, rank), F32),
        [pltpu.VMEM((rank, rank), F32), pltpu.VMEM((LANES, LANES), F32)],
        10**10,
    )(index, *pieces)


def joined(x_ref):
    return jnp.concatenate([x_ref[k] for k in range(x_ref.shape[0])], axis=1)


def same(n):
    i = lax.broadcasted_iota(jnp.int32, (n, n), 0)
    return i == lax.broadcasted_iota(jnp.int32, (n, n), 1)


def middle_kernel(p_ref, w_ref, x_ref, m_ref, g_ref, q_ref, o_ref, q_sum, s_sum):
    step = pl.program_id(0)

    @pl.when(step == 0)
    def _():
        q_sum[...] = jnp.zeros_like(q_sum)
        s_sum[...] = jnp.zeros_like(s_sum)
        o_ref[...] = exact(p_ref[...], w_ref[...], NT)

    rt = split(joined(x_ref))
    b = m_ref[...] + g_ref[0].astype(F32) + g_ref[1].astype(F32)
    q_sum[...] += dot3(split(b), rt, NT)
    s_sum[...] += dot3(rt, rt, NT)

    @pl.when(step == pl.num_programs(0) - 1)
    def _():
        w = w_ref[...]
        s = exact(exact(w, s_sum[...], NN), w, NT)
        o = split((1.0 - KEEP_RATE) * o_ref[...])
        q = dot3(split(q_sum[...]), split(w), NT) - dot3(o, split(s), NN)
        n = s.shape[0]
        squares = jnp.sum(jnp.where(same(n), s, 0.0), axis=0, keepdims=True)
        height = q_ref.shape[1] - 8
        for k in range(q_ref.shape[0]):
            q_ref[k, :height] = q[k * height : (k + 1) * height]
            q_ref[k, height:] = jnp.broadcast_to(squares, (8, n))


def middle(p, w, x, momentum, grads):
    rows, cols = momentum.shape
    rank = p.shape[1]
    bn = cols // GRID
    shape = (4, rows // 4 + 8, rank)
    return call(
        middle_kernel,
        (GRID,),
        [
            whole(p.shape),
            whole(w.shape),
            pl.BlockSpec((bn // LANES, rank, LANES), lambda i: (i, 0, 0)),
            pl.BlockSpec((rows, bn), lambda i: (0, i)),
            pl.BlockSpec((2, rows, bn), lambda i: (0, 0, i)),
        ],
        [whole(shape), whole((rows, rank))],
        [jax.ShapeDtypeStruct(shape, F32), jax.ShapeDtypeStruct((rows, rank), F32)],
        [pltpu.VMEM((rows, rank), F32), pltpu.VMEM((rank, rank), F32)],
        10 * rows * cols * rank,
    )(p, w, x, momentum, grads)


def update_kernel(o_ref, w_ref, x_ref, m_ref, g_ref, raw_ref, b_ref):
    raw = dot3(split(w_ref[...]), split(joined(x_ref)), NN)
    raw_ref[...] = raw
    b = m_ref[...] + g_ref[0].astype(F32) + g_ref[1].astype(F32)
    o = split((1.0 - KEEP_RATE) * o_ref[...])
    b_ref[...] = b - dot3(o, split(raw), NN)


def second_buffer(o, w, x, momentum, grads):
    rows, cols = momentum.shape
    rank = o.shape[1]
    bn = cols // GRID
    return call(
        update_kernel,
        (GRID,),
        [
            whole(o.shape),
            whole(w.shape),
            pl.BlockSpec((bn // LANES, rank, LANES), lambda i: (i, 0, 0)),
            pl.BlockSpec((rows, bn), lambda i: (0, i)),
            pl.BlockSpec((2, rows, bn), lambda i: (0, 0, i)),
        ],
        [
            pl.BlockSpec((rank, bn), lambda i: (0, i)),
            pl.BlockSpec((rows, bn), lambda i: (0, i)),
        ],
        [
            jax.ShapeDtypeStruct((rank, cols), F32),
            jax.ShapeDtypeStruct((rows, cols), F32),
        ],
        [],
        9 * rows * cols * rank,
    )(o, w, x, momentum, grads)


def change_kernel(factor, o_ref, rs_ref, raw_ref, c_ref):
    o = split(o_ref[...] * (factor * rs_ref[:1]))
    c_ref[...] = dot3(o, split(raw_ref[...]), NN)


def first_change(factor, o, rs, raw):
    rows, rank = o.shape
    cols = raw.shape[1]
    bn = cols // GRID
    return call(
        functools.partial(change_kernel, factor),
        (GRID,),
        [whole(o.shape), whole(rs.shape), pl.BlockSpec((rank, bn), lambda i: (0, i))],
        pl.BlockSpec((rows, bn), lambda i: (0, i)),
        jax.ShapeDtypeStruct((rows, cols), F32),
        [],
        6 * rows * cols * rank,
    )(o, rs, raw)


def last_raw_kernel(p_ref, w_ref, x_ref, raw_ref, o_ref, sq_ref, total):
    step = pl.program_id(0)

    @pl.when(step == 0)
    def _():
        o_ref[...] = exact(p_ref[...], w_ref[...], NT)
        total[...] = jnp.zeros_like(total)

    raw = dot3(split(w_ref[...]), split(joined(x_ref)), NN)
    raw_ref[...] = raw
    total[...] += jnp.sum(raw * raw, axis=1, keepdims=True)

    @pl.when(step == pl.num_programs(0) - 1)
    def _():
        n = raw.shape[0]
        squares = jnp.where(same(n), jnp.broadcast_to(total[:, :1], (n, n)), 0.0)
        row = jnp.sum(squares, axis=0, keepdims=True)
        for k in range(sq_ref.shape[0]):
            sq_ref[k] = jnp.broadcast_to(row, (8, n))


def last_raw(p, w, x, peers):
    rows, rank = p.shape
    cols = x.shape[0] * LANES
    bn = cols // GRID
    return call(
        last_raw_kernel,
        (GRID,),
        [
            whole(p.shape),
            whole(w.shape),
            pl.BlockSpec((bn // LANES, rank, LANES), lambda i: (i, 0, 0)),
        ],
        [
            pl.BlockSpec((rank, bn), lambda i: (0, i)),
            whole((rows, rank)),
            whole((peers, 8, rank)),
        ],
        [
            jax.ShapeDtypeStruct((rank, cols), F32),
            jax.ShapeDtypeStruct((rows, rank), F32),
            jax.ShapeDtypeStruct((peers, 8, rank), F32),
        ],
        [pltpu.VMEM((rank, LANES), F32)],
        3 * rows * cols * rank,
    )(p, w, x)


def state_kernel(o_ref, raw_ref, b_ref, s_ref):
    o = split((1.0 - KEEP_RATE) * o_ref[...])
    s_ref[...] = b_ref[...] - dot3(o, split(raw_ref[...]), NN)


def last_state(o, raw, b):
    rows, cols = b.shape
    rank = o.shape[1]
    bn = cols // GRID
    return call(
        state_kernel,
        (GRID,),
        [
            whole(o.shape),
            pl.BlockSpec((rank, bn), lambda i: (0, i)),
            pl.BlockSpec((rows, bn), lambda i: (0, i)),
        ],
        pl.BlockSpec((rows, bn), lambda i: (0, i)),
        jax.ShapeDtypeStruct((rows, cols), F32),
        [],
        6 * rows * cols * rank,
    )(o, raw, b)


def last_change_kernel(factor, o_ref, sq_ref, raw_ref, c_ref, out_ref):
    total = sq_ref[0, :1]
    for k in range(1, sq_ref.shape[0]):
        total = total + sq_ref[k, :1]
    o = split(o_ref[...] * (factor * lax.rsqrt(total + NORM_EPS)))
    out_ref[...] = (c_ref[...] + dot3(o, split(raw_ref[...]), NN)).astype(BF16)


def last_change(factor, o, sq, raw, change):
    rows, cols = change.shape
    rank = o.shape[1]
    bn = cols // GRID
    return call(
        functools.partial(last_change_kernel, factor),
        (GRID,),
        [
            whole(o.shape),
            whole(sq.shape),
            pl.BlockSpec((rank, bn), lambda i: (0, i)),
            pl.BlockSpec((rows, bn), lambda i: (0, i)),
        ],
        pl.BlockSpec((rows, bn), lambda i: (0, i)),
        jax.ShapeDtypeStruct((rows, cols), BF16),
        [],
        6 * rows * cols * rank,
    )(o, sq, raw, change)


SIDE = 4


def row_permute(x, move):
    pairs = []
    for y in range(SIDE):
        for z in range(SIDE):
            to = move(y, z)
            pairs.append((SIDE * y + z, SIDE * to[0] + to[1]))
    return lax.ppermute(x, "row", pairs)


def chip_permute(x, move):
    pairs = [(2 * k + c, 2 * move(k) + c) for k in range(SIDE) for c in range(2)]
    return lax.ppermute(x, "col", pairs)


def core_permute(x):
    return lax.ppermute(x, "col", [(k, k ^ 1) for k in range(2 * SIDE)])


def near(k):
    return k ^ 1


def far(k):
    return SIDE - 1 - k


def col_sum(parts):
    core = lax.axis_index("col") % 2
    mine = lax.dynamic_slice_in_dim(parts, 2 * core, 2, 0)
    theirs = lax.dynamic_slice_in_dim(parts, 2 - 2 * core, 2, 0)
    mine = mine + core_permute(theirs)
    a, b = mine[0], mine[1]
    a, b = a + chip_permute(a, near), b + chip_permute(b, far)
    a, b = a + chip_permute(a, far), b + chip_permute(b, near)
    mine = jnp.stack([a, b])
    theirs = core_permute(mine)
    return jnp.where(
        core == 0, jnp.concatenate([mine, theirs]), jnp.concatenate([theirs, mine])
    )


def gram_sum(part):
    for move in (
        lambda y, z: (y, near(z)),
        lambda y, z: (y, far(z)),
        lambda y, z: (near(y), z),
        lambda y, z: (far(y), z),
    ):
        part = part + row_permute(part, move)
    core = lax.axis_index("col") % 2
    other = core_permute(part)
    chip = jnp.where(
        core == 0, jnp.concatenate([part, other]), jnp.concatenate([other, part])
    )
    return [chip] + [
        chip_permute(chip, lambda k, d=d: (k - d) % SIDE) for d in range(1, SIDE)
    ]


def exchange(x, axis):
    return lax.all_to_all(x, axis, 0, 0, tiled=True)


def row_total(products, part, chip):
    pieces = gram_sum(part)
    own = spread_sum(exchange(products, "row"))
    pieces, own = lax.optimization_barrier((pieces, own))
    total = exchange(own, "row")
    return total, inverse_factor(pieces, chip)


def shards(momentum, grads, basis):
    rows, cols = momentum.shape
    rank = basis.shape[1]
    peers = lax.axis_size("col")
    factor = (rows * lax.axis_size("row") * cols * peers / rank) ** 0.5
    place = lax.axis_index("col").astype(jnp.int32)
    chip, place = (place // 2)[None], place[None]

    p1 = first_projection(momentum, grads, basis)
    p1 = col_sum(p1.reshape(4, rows // 4, rank)).reshape(rows, rank)
    pt1, part1 = gram_part(p1, place, peers)
    x1 = raw_products(raw_first_kernel, pt1, [momentum, grads])
    x1, w1 = row_total(x1, part1, chip)
    q2, o1 = middle(p1, w1, x1, momentum, grads)
    raw1, b2 = second_buffer(o1, w1, x1, momentum, grads)
    q2 = col_sum(q2)
    rs1 = lax.rsqrt(q2[0, rows // 4 :] + NORM_EPS)
    p2 = q2[:, : rows // 4].reshape(rows, rank) * rs1[:1]
    pt2, part2 = gram_part(p2, place, peers)
    x2 = raw_products(raw_second_kernel, pt2, [b2])
    change1 = first_change(factor, o1, rs1, raw1)
    x2, w2 = row_total(x2, part2, chip)
    raw2, o2, sq2 = last_raw(p2, w2, x2, peers)
    sq2 = exchange(sq2, "col")
    state = last_state(o2, raw2, b2)
    change = last_change(factor, o2, sq2, raw2, change1)
    return change, state


def solution(mesh):
    return jax.shard_map(
        shards,
        mesh=mesh,
        in_specs=(P("row", "col"), P(None, "row", "col"), P("col", None)),
        out_specs=(P("row", "col"), P("row", "col")),
        check_vma=False,
    )
```

```python
import functools

import jax
import jax.numpy as jnp
from jax import lax
from jax.experimental import pallas as pl
from jax.experimental.pallas import tpu as pltpu
from jax.sharding import PartitionSpec as P

KEEP_RATE = 0.95
NORM_EPS = 1e-06
LANES = 128
GRID = 4
F32 = jnp.float32
BF16 = jnp.bfloat16
VMEM_LIMIT = 48 * 1024 * 1024
NN = (((1,), (0,)), ((), ()))
NT = (((1,), (1,)), ((), ()))


def split(x):
    high = x.astype(BF16)
    return high, (x - high.astype(F32)).astype(BF16)


def mm(a, b, dims):
    return lax.dot_general(a, b, dims, preferred_element_type=F32)


def dot3(a, b, dims):
    return mm(a[0], b[0], dims) + (mm(a[0], b[1], dims) + mm(a[1], b[0], dims))


def exact(a, b, dims):
    return lax.dot_general(
        a, b, dims, precision=lax.Precision.HIGHEST, preferred_element_type=F32
    )


def call(kernel, grid, in_specs, out_specs, out_shape, scratch, cost):
    return pl.pallas_call(
        kernel,
        grid=grid,
        in_specs=in_specs,
        out_specs=out_specs,
        out_shape=out_shape,
        scratch_shapes=scratch,
        compiler_params=pltpu.CompilerParams(vmem_limit_bytes=VMEM_LIMIT),
        cost_estimate=pl.CostEstimate(
            flops=cost, transcendentals=0, bytes_accessed=8 * 1024 * 1024
        ),
    )


def in_hbm(*arrays):
    return [pltpu.with_memory_space_constraint(a, pltpu.HBM) for a in arrays]


def whole(shape):
    return pl.BlockSpec(shape, lambda i: (0,) * len(shape))


def first_kernel(m_ref, g_ref, v_ref, p_ref):
    b = split(m_ref[...] + g_ref[0].astype(F32))
    part = dot3(b, split(v_ref[...]), NN)

    @pl.when(pl.program_id(0) == 0)
    def _():
        p_ref[...] = part

    @pl.when(pl.program_id(0) > 0)
    def _():
        p_ref[...] += part


def first_projection(momentum, grads, basis):
    rows, cols = momentum.shape
    rank = basis.shape[1]
    bn = cols // GRID
    return call(
        first_kernel,
        (GRID,),
        [
            pl.BlockSpec((rows, bn), lambda i: (0, i)),
            pl.BlockSpec((1, rows, bn), lambda i: (0, 0, i)),
            pl.BlockSpec((bn, rank), lambda i: (i, 0)),
        ],
        whole((rows, rank)),
        jax.ShapeDtypeStruct((rows, rank), F32),
        [],
        6 * rows * cols * rank,
    )(*in_hbm(momentum, grads, basis))


def gram_kernel(n_ref, p_ref, pt_ref, c_ref, t):
    turned = p_ref[...].T
    pt_ref[0], pt_ref[1] = split(turned)
    p, half = p_ref[...], LANES
    t[: 2 * half] = exact(turned, p[:, :half], NN)
    t[2 * half :] = exact(turned[half:], p[:, half:], NN)
    size = c_ref.shape[0]
    c_ref[...] = t[pl.ds(pl.multiple_of(n_ref[0] * size, size), size), :]


def gram_part(p, index, parts):
    rows, rank = p.shape
    height = 3 * LANES
    return call(
        gram_kernel,
        (1,),
        [pl.BlockSpec(memory_space=pltpu.SMEM), whole(p.shape)],
        [whole((2, rank, rows)), whole((height // parts, LANES))],
        [
            jax.ShapeDtypeStruct((2, rank, rows), BF16),
            jax.ShapeDtypeStruct((height // parts, LANES), F32),
        ],
        [pltpu.VMEM((height, LANES), F32)],
        2 * rows * rank * rank,
    )(index, p)


def store_products(pt_ref, c_ref, b, x_ref):
    rank = pt_ref.shape[1]
    r = dot3((pt_ref[0], pt_ref[1]), split(b), NN)
    for k in range(x_ref.shape[0]):
        x_ref[k, :rank] = r[:, k * LANES : (k + 1) * LANES]
        x_ref[k, rank:] = c_ref[...]


def raw_first_kernel(pt_ref, c_ref, m_ref, g_ref, x_ref):
    store_products(pt_ref, c_ref, m_ref[...] + g_ref[0].astype(F32), x_ref)


def raw_second_kernel(pt_ref, c_ref, b_ref, x_ref):
    store_products(pt_ref, c_ref, b_ref[...], x_ref)


def raw_products(kernel, pt, part, bigs):
    _, rank, rows = pt.shape
    cols = bigs[0].shape[1]
    bn = cols // GRID
    height = rank + part.shape[0]
    specs = [
        pl.BlockSpec((rows, bn), lambda i: (0, i)),
        pl.BlockSpec((1, rows, bn), lambda i: (0, 0, i)),
    ]
    return call(
        kernel,
        (GRID,),
        [whole(pt.shape), whole(part.shape)] + specs[: len(bigs)],
        pl.BlockSpec((bn // LANES, height, LANES), lambda i: (i, 0, 0)),
        pltpu.HBM((cols // LANES, height, LANES), F32),
        [],
        6 * rows * cols * rank,
    )(pt, part, *in_hbm(*bigs))


def spread_kernel(x_ref, *refs):
    tails, (y_ref, t_ref) = refs[:-2], refs[-2:]
    count = x_ref.shape[0]
    total = x_ref[0]
    for k in range(1, count):
        total = total + x_ref[k]
    for k in range(count):
        y_ref[k] = total

    @pl.when(pl.program_id(0) == 0)
    def _():
        for n, tail in enumerate(tails):
            size = tail.shape[1]
            total = tail[0]
            for k in range(1, count):
                total = total + tail[k]
            t_ref[n * size : (n + 1) * size] = total


def spread_sum(x, rank):
    count, height, width = x.shape
    size = 16
    steps = 4
    tails = [
        pl.BlockSpec((count, size, width), lambda i, n=n: (0, rank // size + n, 0))
        for n in range((height - rank) // size)
    ]
    spec = pl.BlockSpec((count, rank // steps, width), lambda i: (0, i, 0))
    return call(
        spread_kernel,
        (steps,),
        [spec] + tails,
        [spec, whole((height - rank, width))],
        [
            pltpu.HBM((count, rank, width), F32),
            jax.ShapeDtypeStruct((height - rank, width), F32),
        ],
        [],
        count * height * width,
    )(*[x] * (1 + len(tails)))


def eliminated(m):
    n = m.shape[0]
    lane = lax.broadcasted_iota(jnp.int32, (8, n), 1)
    sub = lax.broadcasted_iota(jnp.int32, (8, n), 0)
    tiles = [m[8 * t : 8 * t + 8] for t in range(n // 8)]
    for j in range(0, n, 2):
        t, r = divmod(j, 8)
        first, second = lane[:1] == j, lane[:1] == j + 1
        both = (lane >= j) & (lane < j + 2)
        row0, row1 = tiles[t][r : r + 1], tiles[t][r + 1 : r + 2]
        a, b = row0[:, j : j + 1], row0[:, j + 1 : j + 2]
        inv_a = 1.0 / a
        ratio = b * inv_a
        d = row1[:, j + 1 : j + 2] - b * ratio
        inv_d = 1.0 / d
        low = row1 - ratio * row0
        unit = jnp.where(first, -ratio, jnp.where(second, 1.0, low))
        use1 = unit * inv_d
        use0 = jnp.where(first, 1.0, jnp.where(second, 0.0, row0)) * inv_a - ratio * use1
        kept = jnp.where(first, -ratio, jnp.where(second, d, low))
        for s in range(t, n // 8):
            c0 = jnp.broadcast_to(tiles[s][:, j : j + 1], (8, n))
            c1 = jnp.broadcast_to(tiles[s][:, j + 1 : j + 2], (8, n))
            new = jnp.where(both, 0.0, tiles[s]) - c0 * use0 - c1 * use1
            if s == t:
                new = jnp.where(sub > r + 1, new, jnp.where(sub == r + 1, kept, tiles[s]))
            tiles[s] = new
    m = jnp.concatenate(tiles, axis=0)
    i = lax.broadcasted_iota(jnp.int32, (n, n), 0)
    j = lax.broadcasted_iota(jnp.int32, (n, n), 1)
    pivots = jnp.sum(jnp.where(i == j, m, 0.0), axis=1, keepdims=True)
    unit = jnp.where(i > j, m, jnp.where(i == j, 1.0, 0.0))
    return unit * lax.rsqrt(pivots)


def cholesky_kernel(n_ref, *refs):
    pieces, (w_ref, a, low) = refs[:-3], refs[-3:]
    size = pieces[0].shape[0]
    count = len(pieces)
    for k, piece in enumerate(pieces):
        place = lax.rem(n_ref[0] + k, count)
        a[pl.ds(pl.multiple_of(place * size, size), size), :] = piece[...]
    half = LANES

    def body(b, carry):
        w = eliminated(a[pl.ds(pl.multiple_of(2 * b * half, half), half), :])
        first = pl.multiple_of(b * half, half)
        w_ref[pl.ds(first, half), pl.ds(first, half)] = w

        @pl.when(b == 0)
        def _():
            low[...] = exact(a[half : 2 * half], w, NT)
            a[2 * half :] -= exact(low[...], low[...], NT)

        return carry

    lax.fori_loop(0, 2, body, 0)
    w_ref[:half, half:] = jnp.zeros((half, half), F32)
    w_ref[half:, :half] = -exact(
        w_ref[half:, half:], exact(low[...], w_ref[:half, :half], NN), NN
    )


def inverse_factor(pieces, index):
    rank = 2 * LANES
    return call(
        cholesky_kernel,
        (1,),
        [pl.BlockSpec(memory_space=pltpu.SMEM)] + [whole(q.shape) for q in pieces],
        whole((rank, rank)),
        jax.ShapeDtypeStruct((rank, rank), F32),
        [pltpu.VMEM((3 * LANES, LANES), F32), pltpu.VMEM((LANES, LANES), F32)],
        10**10,
    )(index, *pieces)


def joined(x_ref):
    return jnp.concatenate([x_ref[k] for k in range(x_ref.shape[0])], axis=1)


def same(n):
    i = lax.broadcasted_iota(jnp.int32, (n, n), 0)
    return i == lax.broadcasted_iota(jnp.int32, (n, n), 1)


def middle_kernel(p_ref, w_ref, x_ref, m_ref, g_ref, q_ref, o_ref, q_sum, s_sum):
    step = pl.program_id(0)

    @pl.when(step == 0)
    def _():
        q_sum[...] = jnp.zeros_like(q_sum)
        s_sum[...] = jnp.zeros_like(s_sum)
        o_ref[...] = exact(p_ref[...], w_ref[...], NT)

    rt = split(joined(x_ref))
    b = m_ref[...] + g_ref[0].astype(F32) + g_ref[1].astype(F32)
    q_sum[...] += dot3(split(b), rt, NT)
    s_sum[...] += dot3(rt, rt, NT)

    @pl.when(step == pl.num_programs(0) - 1)
    def _():
        w = w_ref[...]
        s = exact(exact(w, s_sum[...], NN), w, NT)
        o = split((1.0 - KEEP_RATE) * o_ref[...])
        q = dot3(split(q_sum[...]), split(w), NT) - dot3(o, split(s), NN)
        n = s.shape[0]
        squares = jnp.sum(jnp.where(same(n), s, 0.0), axis=0, keepdims=True)
        height = q_ref.shape[1] - 8
        for k in range(q_ref.shape[0]):
            q_ref[k, :height] = q[k * height : (k + 1) * height]
            q_ref[k, height:] = jnp.broadcast_to(squares, (8, n))


def middle(p, w, x, momentum, grads):
    rows, cols = momentum.shape
    rank = p.shape[1]
    bn = cols // GRID
    shape = (4, rows // 4 + 8, rank)
    return call(
        middle_kernel,
        (GRID,),
        [
            whole(p.shape),
            whole(w.shape),
            pl.BlockSpec((bn // LANES, rank, LANES), lambda i: (i, 0, 0)),
            pl.BlockSpec((rows, bn), lambda i: (0, i)),
            pl.BlockSpec((2, rows, bn), lambda i: (0, 0, i)),
        ],
        [whole(shape), whole((rows, rank))],
        [jax.ShapeDtypeStruct(shape, F32), jax.ShapeDtypeStruct((rows, rank), F32)],
        [pltpu.VMEM((rows, rank), F32), pltpu.VMEM((rank, rank), F32)],
        10 * rows * cols * rank,
    )(p, w, x, *in_hbm(momentum, grads))


def update_kernel(o_ref, w_ref, x_ref, m_ref, g_ref, raw_ref, b_ref):
    raw = dot3(split(w_ref[...]), split(joined(x_ref)), NN)
    raw_ref[...] = raw
    b = m_ref[...] + g_ref[0].astype(F32) + g_ref[1].astype(F32)
    o = split((1.0 - KEEP_RATE) * o_ref[...])
    b_ref[...] = b - dot3(o, split(raw), NN)


def second_buffer(o, w, x, momentum, grads):
    rows, cols = momentum.shape
    rank = o.shape[1]
    bn = cols // GRID
    return call(
        update_kernel,
        (GRID,),
        [
            whole(o.shape),
            whole(w.shape),
            pl.BlockSpec((bn // LANES, rank, LANES), lambda i: (i, 0, 0)),
            pl.BlockSpec((rows, bn), lambda i: (0, i)),
            pl.BlockSpec((2, rows, bn), lambda i: (0, 0, i)),
        ],
        [
            pl.BlockSpec((rank, bn), lambda i: (0, i)),
            pl.BlockSpec((rows, bn), lambda i: (0, i)),
        ],
        [pltpu.HBM((rank, cols), F32), pltpu.HBM((rows, cols), F32)],
        [],
        9 * rows * cols * rank,
    )(o, w, x, *in_hbm(momentum, grads))


def change_kernel(factor, o_ref, rs_ref, raw_ref, c_ref):
    o = split(o_ref[...] * (factor * rs_ref[:1]))
    c_ref[...] = dot3(o, split(raw_ref[...]), NN)


def first_change(factor, o, rs, raw):
    rows, rank = o.shape
    cols = raw.shape[1]
    bn = cols // GRID
    return call(
        functools.partial(change_kernel, factor),
        (GRID,),
        [whole(o.shape), whole(rs.shape), pl.BlockSpec((rank, bn), lambda i: (0, i))],
        pl.BlockSpec((rows, bn), lambda i: (0, i)),
        pltpu.HBM((rows, cols), F32),
        [],
        6 * rows * cols * rank,
    )(o, rs, *in_hbm(raw))


def last_raw_kernel(p_ref, w_ref, x_ref, raw_ref, o_ref, sq_ref, total):
    step = pl.program_id(0)

    @pl.when(step == 0)
    def _():
        o_ref[...] = exact(p_ref[...], w_ref[...], NT)
        total[...] = jnp.zeros_like(total)

    raw = dot3(split(w_ref[...]), split(joined(x_ref)), NN)
    raw_ref[...] = raw
    total[...] += jnp.sum(raw * raw, axis=1, keepdims=True)

    @pl.when(step == pl.num_programs(0) - 1)
    def _():
        n = raw.shape[0]
        squares = jnp.where(same(n), jnp.broadcast_to(total[:, :1], (n, n)), 0.0)
        row = jnp.sum(squares, axis=0, keepdims=True)
        for k in range(sq_ref.shape[0]):
            sq_ref[k] = jnp.broadcast_to(row, (8, n))


def last_raw(p, w, x, peers):
    rows, rank = p.shape
    cols = x.shape[0] * LANES
    bn = cols // GRID
    return call(
        last_raw_kernel,
        (GRID,),
        [
            whole(p.shape),
            whole(w.shape),
            pl.BlockSpec((bn // LANES, rank, LANES), lambda i: (i, 0, 0)),
        ],
        [
            pl.BlockSpec((rank, bn), lambda i: (0, i)),
            whole((rows, rank)),
            whole((peers, 8, rank)),
        ],
        [
            jax.ShapeDtypeStruct((rank, cols), F32),
            jax.ShapeDtypeStruct((rows, rank), F32),
            jax.ShapeDtypeStruct((peers, 8, rank), F32),
        ],
        [pltpu.VMEM((rank, LANES), F32)],
        3 * rows * cols * rank,
    )(p, w, *in_hbm(x))


def state_kernel(o_ref, raw_ref, b_ref, s_ref):
    o = split((1.0 - KEEP_RATE) * o_ref[...])
    s_ref[...] = b_ref[...] - dot3(o, split(raw_ref[...]), NN)


def last_state(o, raw, b):
    rows, cols = b.shape
    rank = o.shape[1]
    bn = cols // GRID
    return call(
        state_kernel,
        (GRID,),
        [
            whole(o.shape),
            pl.BlockSpec((rank, bn), lambda i: (0, i)),
            pl.BlockSpec((rows, bn), lambda i: (0, i)),
        ],
        pl.BlockSpec((rows, bn), lambda i: (0, i)),
        jax.ShapeDtypeStruct((rows, cols), F32),
        [],
        6 * rows * cols * rank,
    )(o, raw, *in_hbm(b))


def last_change_kernel(factor, o_ref, sq_ref, raw_ref, c_ref, out_ref):
    total = sq_ref[0, :1]
    for k in range(1, sq_ref.shape[0]):
        total = total + sq_ref[k, :1]
    o = split(o_ref[...] * (factor * lax.rsqrt(total + NORM_EPS)))
    out_ref[...] = (c_ref[...] + dot3(o, split(raw_ref[...]), NN)).astype(BF16)


def last_change(factor, o, sq, raw, change):
    rows, cols = change.shape
    rank = o.shape[1]
    bn = cols // GRID
    return call(
        functools.partial(last_change_kernel, factor),
        (GRID,),
        [
            whole(o.shape),
            whole(sq.shape),
            pl.BlockSpec((rank, bn), lambda i: (0, i)),
            pl.BlockSpec((rows, bn), lambda i: (0, i)),
        ],
        pl.BlockSpec((rows, bn), lambda i: (0, i)),
        jax.ShapeDtypeStruct((rows, cols), BF16),
        [],
        6 * rows * cols * rank,
    )(o, sq, raw, *in_hbm(change))


SIDE = 4


def chip_permute(x, move):
    pairs = [(2 * k + c, 2 * move(k) + c) for k in range(SIDE) for c in range(2)]
    return lax.ppermute(x, "col", pairs)


def core_permute(x):
    return lax.ppermute(x, "col", [(k, k ^ 1) for k in range(2 * SIDE)])


def near(k):
    return k ^ 1


def far(k):
    return SIDE - 1 - k


def col_sum(parts):
    core = lax.axis_index("col") % 2
    mine = lax.dynamic_slice_in_dim(parts, 2 * core, 2, 0)
    theirs = lax.dynamic_slice_in_dim(parts, 2 - 2 * core, 2, 0)
    mine = mine + core_permute(theirs)
    a, b = mine[0], mine[1]
    a, b = a + chip_permute(a, near), b + chip_permute(b, far)
    a, b = a + chip_permute(a, far), b + chip_permute(b, near)
    mine = jnp.stack([a, b])
    theirs = core_permute(mine)
    return jnp.where(
        core == 0, jnp.concatenate([mine, theirs]), jnp.concatenate([theirs, mine])
    )


def by_chip(part):
    core = lax.axis_index("col") % 2
    other = core_permute(part)
    chip = jnp.where(
        core == 0, jnp.concatenate([part, other]), jnp.concatenate([other, part])
    )
    return [chip] + [
        chip_permute(chip, lambda k, d=d: (k - d) % SIDE) for d in range(1, SIDE)
    ]


def exchange(x, axis):
    return lax.all_to_all(x, axis, 0, 0, tiled=True)


def row_total(products, rank, chip, beside):
    got, beside = lax.optimization_barrier((exchange(products, "row"), beside))
    own, part = spread_sum(got, rank)
    total = exchange(own, "row")
    return total, inverse_factor(by_chip(part), chip), beside


def shards(momentum, grads, basis):
    rows, cols = momentum.shape
    rank = basis.shape[1]
    peers = lax.axis_size("col")
    factor = (rows * lax.axis_size("row") * cols * peers / rank) ** 0.5
    place = lax.axis_index("col").astype(jnp.int32)
    chip, place = (place // 2)[None], place[None]

    p1 = first_projection(momentum, grads, basis)
    p1 = col_sum(p1.reshape(4, rows // 4, rank)).reshape(rows, rank)
    pt1, part1 = gram_part(p1, place, peers)
    x1 = raw_products(raw_first_kernel, pt1, part1, [momentum, grads])
    x1, w1, _ = row_total(x1, rank, chip, [])
    q2, o1 = middle(p1, w1, x1, momentum, grads)
    raw1, b2 = second_buffer(o1, w1, x1, momentum, grads)
    q2 = col_sum(q2)
    rs1 = lax.rsqrt(q2[0, rows // 4 :] + NORM_EPS)
    p2 = q2[:, : rows // 4].reshape(rows, rank) * rs1[:1]
    pt2, part2 = gram_part(p2, place, peers)
    x2 = raw_products(raw_second_kernel, pt2, part2, [b2])
    change1 = first_change(factor, o1, rs1, raw1)
    x2, w2, change1 = row_total(x2, rank, chip, change1)
    raw2, o2, sq2 = last_raw(p2, w2, x2, peers)
    sq2 = exchange(sq2, "col")
    state = last_state(o2, raw2, b2)
    change = last_change(factor, o2, sq2, raw2, change1)
    return change, state


def solution(mesh):
    return jax.shard_map(
        shards,
        mesh=mesh,
        in_specs=(P("row", "col"), P(None, "row", "col"), P("col", None)),
        out_specs=(P("row", "col"), P("row", "col")),
        check_vma=False,
    )
```

```python
import functools

import jax
import jax.numpy as jnp
from jax import lax
from jax.experimental import pallas as pl
from jax.experimental.pallas import tpu as pltpu
from jax.sharding import PartitionSpec as P

KEEP_RATE = 0.95
NORM_EPS = 1e-06
LANES = 128
CHUNKS = 4
F32 = jnp.float32
BF16 = jnp.bfloat16
VMEM_LIMIT = 20 * 1024 * 1024
NN = (((1,), (0,)), ((), ()))
NT = (((1,), (1,)), ((), ()))


def split(x):
    high = x.astype(BF16)
    return high, (x - high.astype(F32)).astype(BF16)


def mm(a, b, dims):
    return lax.dot_general(a, b, dims, preferred_element_type=F32)


def dot3(a, b, dims):
    return mm(a[0], b[0], dims) + (mm(a[0], b[1], dims) + mm(a[1], b[0], dims))


def exact(a, b, dims):
    return lax.dot_general(
        a, b, dims, precision=lax.Precision.HIGHEST, preferred_element_type=F32
    )


def call(kernel, in_specs, out_shape, out_specs, scratch, cost):
    return pl.pallas_call(
        kernel,
        in_specs=in_specs,
        out_specs=out_specs,
        out_shape=out_shape,
        scratch_shapes=scratch,
        compiler_params=pltpu.CompilerParams(vmem_limit_bytes=VMEM_LIMIT),
        cost_estimate=pl.CostEstimate(
            flops=cost, transcendentals=0, bytes_accessed=8 * 1024 * 1024
        ),
    )


VM = pl.BlockSpec(memory_space=pltpu.VMEM)
SM = pl.BlockSpec(memory_space=pltpu.SMEM)
ANY = pl.BlockSpec(memory_space=pl.ANY)


def in_hbm(*arrays):
    return [pltpu.with_memory_space_constraint(a, pltpu.HBM) for a in arrays]


def pair(shape):
    return jax.ShapeDtypeStruct((2, *shape), BF16)


def pair_in_hbm(shape):
    return pltpu.HBM((2, *shape), BF16)


def dma(*shape):
    return pltpu.SemaphoreType.DMA(shape)


def fetch(moves, sems):
    copies = [
        [pltpu.make_async_copy(a, b, sems.at[k, n]) for n, (a, b) in enumerate(block)]
        for k, block in enumerate(moves)
    ]
    for block in copies:
        for copy in block:
            copy.start()

    def wait(k):
        for copy in copies[k]:
            copy.wait()

    return wait


def columns(k, width):
    return slice(k * width, (k + 1) * width)


def same(n):
    i = lax.broadcasted_iota(jnp.int32, (n, n), 0)
    return i == lax.broadcasted_iota(jnp.int32, (n, n), 1)


def buffer_moves(m_ref, g_ref, m, g):
    width = m.shape[1] // CHUNKS
    moves = []
    for k in range(CHUNKS):
        c = columns(k, width)
        moves.append([(m_ref.at[:, c], m.at[:, c])])
        for n in range(g.shape[0]):
            moves[k].append((g_ref.at[n, :, c], g.at[n, :, c]))
    return moves


def buffer_block(m, g, c):
    b = m[:, c]
    for n in range(g.shape[0]):
        b = b + g[n, :, c].astype(F32)
    return b


def first_kernel(m_ref, g_ref, v_ref, p_ref, m, g, v, sems):
    width = m.shape[1] // CHUNKS
    moves = buffer_moves(m_ref, g_ref, m, g)
    for k in range(CHUNKS):
        c = columns(k, width)
        moves[k].append((v_ref.at[c], v.at[c]))
    wait = fetch(moves, sems)
    for k in range(CHUNKS):
        c = columns(k, width)
        wait(k)
        part = dot3(split(buffer_block(m, g, c)), split(v[c]), NN)
        if k == 0:
            p_ref[...] = part
        else:
            p_ref[...] += part


def first_projection(momentum, grads, basis):
    rows, cols = momentum.shape
    rank = basis.shape[1]
    return call(
        first_kernel,
        [ANY] * 3,
        jax.ShapeDtypeStruct((rows, rank), F32),
        VM,
        [
            pltpu.VMEM((rows, cols), F32),
            pltpu.VMEM((1, rows, cols), BF16),
            pltpu.VMEM((cols, rank), F32),
            dma(CHUNKS, 3),
        ],
        6 * rows * cols * rank,
    )(*in_hbm(momentum, grads, basis))


def store_products(n_ref, mine_ref, theirs_ref, scaled, block, x_ref, p_ref, rs_ref, parts, x, t, sems):
    core = lax.rem(n_ref[0], 2)
    parts[pl.ds(2 * core, 2)] = mine_ref[...]
    parts[pl.ds(2 - 2 * core, 2)] = theirs_ref[...]
    rows, rank = p_ref.shape
    height = rows // 4
    p = jnp.concatenate([parts[k, :height] for k in range(4)], axis=0)
    if scaled:
        rs = lax.rsqrt(parts[0, height : height + 8] + NORM_EPS)
        p = p * rs[:1]
    else:
        rs = jnp.ones(rs_ref.shape, F32)
    rs_ref[...] = rs
    p_ref[...] = p
    turned, half = p.T, LANES
    t[: 2 * half] = exact(turned, p[:, :half], NN)
    t[2 * half :] = exact(turned[half:], p[:, half:], NN)
    size = x_ref.shape[1] - rank
    share = t[pl.ds(pl.multiple_of(n_ref[0] * size, size), size), :]
    pt = split(turned)
    blocks = x_ref.shape[0] // CHUNKS
    copies = []
    for k in range(CHUNKS):
        r = dot3(pt, block(k), NN)
        for q in range(blocks):
            x[k * blocks + q, :rank] = r[:, columns(q, LANES)]
            x[k * blocks + q, rank:] = share
        here = columns(k, blocks)
        copies.append(pltpu.make_async_copy(x.at[here], x_ref.at[here], sems.at[k]))
        copies[k].start()
    for copy in copies:
        copy.wait()


def first_products_kernel(
    n_ref, mine_ref, theirs_ref, m_ref, g_ref, x_ref, p_ref, rs_ref, *scratch
):
    parts, x, t, sent, came, m, g = scratch
    wait = fetch(buffer_moves(m_ref, g_ref, m, g), came)

    def block(k):
        wait(k)
        return split(buffer_block(m, g, columns(k, m.shape[1] // CHUNKS)))

    store_products(
        n_ref, mine_ref, theirs_ref, False, block, x_ref, p_ref, rs_ref, parts, x, t, sent
    )


def pair_moves(b_ref, b):
    width = b.shape[2] // CHUNKS
    return [
        [(b_ref.at[:, :, columns(k, width)], b.at[:, :, columns(k, width)])]
        for k in range(CHUNKS)
    ]


def second_products_kernel(
    n_ref, mine_ref, theirs_ref, b_ref, x_ref, p_ref, rs_ref, *scratch
):
    parts, x, t, sent, came, b = scratch
    wait = fetch(pair_moves(b_ref, b), came)

    def block(k):
        wait(k)
        c = columns(k, b.shape[2] // CHUNKS)
        return b[0, :, c], b[1, :, c]

    store_products(
        n_ref, mine_ref, theirs_ref, True, block, x_ref, p_ref, rs_ref, parts, x, t, sent
    )


def products(kernel, place, mine, theirs, bigs, held, peers):
    rows, cols = bigs[0].shape[-2:]
    _, height, rank = mine.shape
    shape = (cols // LANES, rank + 3 * LANES // peers, LANES)
    return call(
        kernel,
        [SM, VM, VM] + [ANY] * len(bigs),
        [
            pltpu.HBM(shape, F32),
            jax.ShapeDtypeStruct((rows, rank), F32),
            jax.ShapeDtypeStruct((8, rank), F32),
        ],
        [ANY, VM, VM],
        [
            pltpu.VMEM((4, height, rank), F32),
            pltpu.VMEM(shape, F32),
            pltpu.VMEM((3 * LANES, LANES), F32),
            dma(CHUNKS),
            dma(CHUNKS, len(bigs)),
        ]
        + held,
        6 * rows * cols * rank,
    )(place, mine, theirs, *in_hbm(*bigs))


def spread_kernel(x_ref, y_ref, t_ref, y, sems):
    count = x_ref.shape[0]
    rank = y.shape[0]
    total = x_ref[0]
    for k in range(1, count):
        total = total + x_ref[k]
    y[...] = total[:rank]
    copies = [
        pltpu.make_async_copy(y, y_ref.at[k], sems.at[k]) for k in range(count)
    ]
    for copy in copies:
        copy.start()
    t_ref[...] = total[rank:]
    for copy in copies:
        copy.wait()


def spread_sum(x, rank):
    count, height, width = x.shape
    return call(
        spread_kernel,
        [VM],
        [
            pltpu.HBM((count, rank, width), F32),
            jax.ShapeDtypeStruct((height - rank, width), F32),
        ],
        [ANY, VM],
        [pltpu.VMEM((rank, width), F32), pltpu.SemaphoreType.DMA((count,))],
        count * height * width,
    )(x)


def eliminated(m):
    n = m.shape[0]
    eye = same(n)
    across = lax.rsqrt(jnp.sum(jnp.where(eye, m, 0.0), axis=0, keepdims=True))
    down = lax.rsqrt(jnp.sum(jnp.where(eye, m, 0.0), axis=1, keepdims=True))
    m = m * down * across
    lane = lax.broadcasted_iota(jnp.int32, (8, n), 1)
    sub = lax.broadcasted_iota(jnp.int32, (8, n), 0)
    tiles = [m[8 * t : 8 * t + 8] for t in range(n // 8)]
    for j in range(0, n, 2):
        t, r = divmod(j, 8)
        first, second = lane[:1] == j, lane[:1] == j + 1
        both = (lane >= j) & (lane < j + 2)
        c0 = [jnp.broadcast_to(x[:, j : j + 1], (8, n)) for x in tiles[t:]]
        c1 = [jnp.broadcast_to(x[:, j + 1 : j + 2], (8, n)) for x in tiles[t:]]
        row0, row1 = tiles[t][r : r + 1], tiles[t][r + 1 : r + 2]
        a, b = c0[0][r : r + 1], c0[0][r + 1 : r + 2]
        d = c1[0][r + 1 : r + 2]
        inv_a = 1.0 / a
        inv_d = a * (1.0 / (a * d - b * b))
        ratio = b * inv_a
        low = row1 - ratio * row0
        use1 = jnp.where(first, -ratio, jnp.where(second, 1.0, low)) * inv_d
        use0 = jnp.where(first, 1.0, jnp.where(second, 0.0, row0)) * inv_a - ratio * use1
        kept = jnp.where(first, -ratio, low)
        for s in range(t, n // 8):
            new = jnp.where(both, 0.0, tiles[s]) - c0[s - t] * use0 - c1[s - t] * use1
            if s == t:
                new = jnp.where(sub > r + 1, new, jnp.where(sub == r + 1, kept, tiles[s]))
            tiles[s] = new
    m = jnp.concatenate(tiles, axis=0)
    i = lax.broadcasted_iota(jnp.int32, (n, n), 0)
    j = lax.broadcasted_iota(jnp.int32, (n, n), 1)
    pivots = jnp.sum(jnp.where(eye, m, 0.0), axis=1, keepdims=True)
    unit = jnp.where(i > j, m, jnp.where(eye, 1.0, 0.0))
    return unit * lax.rsqrt(pivots) * across


def cholesky_kernel(n_ref, *refs):
    pieces, (w_ref, a, low) = refs[:-3], refs[-3:]
    size = pieces[0].shape[0]
    count = len(pieces)
    for k, piece in enumerate(pieces):
        place = lax.rem(n_ref[0] // 2 + k, count)
        a[pl.ds(pl.multiple_of(place * size, size), size), :] = piece[...]
    half = LANES

    def body(b, carry):
        w = eliminated(a[pl.ds(pl.multiple_of(2 * b * half, half), half), :])
        first = pl.multiple_of(b * half, half)
        w_ref[pl.ds(first, half), pl.ds(first, half)] = w

        @pl.when(b == 0)
        def _():
            low[...] = exact(a[half : 2 * half], w, NT)
            a[2 * half :] -= exact(low[...], low[...], NT)

        return carry

    lax.fori_loop(0, 2, body, 0)
    w_ref[:half, half:] = jnp.zeros((half, half), F32)
    w_ref[half:, :half] = -exact(
        w_ref[half:, half:], exact(low[...], w_ref[:half, :half], NN), NN
    )


def inverse_factor(pieces, place):
    rank = 2 * LANES
    return call(
        cholesky_kernel,
        [SM] + [VM] * len(pieces),
        jax.ShapeDtypeStruct((rank, rank), F32),
        VM,
        [pltpu.VMEM((3 * LANES, LANES), F32), pltpu.VMEM((LANES, LANES), F32)],
        10**10,
    )(place, *pieces)


def middle_kernel(p_ref, w_ref, x_ref, m_ref, g_ref, q_ref, o_ref, rt_ref, m, g, q_sum, sems):
    wait = fetch(buffer_moves(m_ref, g_ref, m, g), sems)
    for k in range(x_ref.shape[0]):
        c = columns(k, LANES)
        rt_ref[0, :, c], rt_ref[1, :, c] = split(x_ref[k])
    rt = (rt_ref[0], rt_ref[1])
    w = w_ref[...]
    ortho = exact(p_ref[...], w, NT)
    o_ref[...] = ortho
    s = exact(exact(w, dot3(rt, rt, NT), NN), w, NT)
    width = m.shape[1] // CHUNKS
    for k in range(CHUNKS):
        c = columns(k, width)
        wait(k)
        part = dot3(
            split(buffer_block(m, g, c)), (rt_ref[0, :, c], rt_ref[1, :, c]), NT
        )
        if k == 0:
            q_sum[...] = part
        else:
            q_sum[...] += part
    q = dot3(split(q_sum[...]), split(w), NT) - dot3(
        split((1.0 - KEEP_RATE) * ortho), split(s), NN
    )
    n = s.shape[0]
    squares = jnp.sum(jnp.where(same(n), s, 0.0), axis=0, keepdims=True)
    height = q_ref.shape[1] - 8
    for k in range(q_ref.shape[0]):
        q_ref[k, :height] = q[columns(k, height)]
        q_ref[k, height:] = jnp.broadcast_to(squares, (8, n))


def middle(p, w, x, momentum, grads):
    rows, cols = momentum.shape
    rank = p.shape[1]
    return call(
        middle_kernel,
        [VM] * 3 + [ANY] * 2,
        [
            jax.ShapeDtypeStruct((4, rows // 4 + 8, rank), F32),
            jax.ShapeDtypeStruct((rows, rank), F32),
            pair((rank, cols)),
        ],
        [VM] * 3,
        [
            pltpu.VMEM((rows, cols), F32),
            pltpu.VMEM(grads.shape, BF16),
            pltpu.VMEM((rows, rank), F32),
            dma(CHUNKS, 3),
        ],
        10 * rows * cols * rank,
    )(p, w, x, *in_hbm(momentum, grads))


def update_kernel(
    o_ref, w_ref, rt_ref, m_ref, g_ref, raw_ref, b_ref, m, g, raw, b, came, sent
):
    wait = fetch(buffer_moves(m_ref, g_ref, m, g), came)
    o = split((1.0 - KEEP_RATE) * o_ref[...])
    w = split(w_ref[...])
    width = m.shape[1] // CHUNKS
    copies = []
    for k in range(CHUNKS):
        c = columns(k, width)
        now = split(dot3(w, (rt_ref[0, :, c], rt_ref[1, :, c]), NN))
        raw[0, :, c], raw[1, :, c] = now
        wait(k)
        b[0, :, c], b[1, :, c] = split(buffer_block(m, g, c) - dot3(o, now, NN))
        for n, (source, target) in enumerate(((raw, raw_ref), (b, b_ref))):
            copy = pltpu.make_async_copy(
                source.at[:, :, c], target.at[:, :, c], sent.at[k, n]
            )
            copy.start()
            copies.append(copy)
    for copy in copies:
        copy.wait()


def second_buffer(o, w, rt, momentum, grads):
    rows, cols = momentum.shape
    rank = o.shape[1]
    return call(
        update_kernel,
        [VM] * 3 + [ANY] * 2,
        [pair_in_hbm((rank, cols)), pair_in_hbm((rows, cols))],
        [ANY] * 2,
        [
            pltpu.VMEM((rows, cols), F32),
            pltpu.VMEM(grads.shape, BF16),
            pltpu.VMEM((2, rank, cols), BF16),
            pltpu.VMEM((2, rows, cols), BF16),
            dma(CHUNKS, 3),
            dma(CHUNKS, 2),
        ],
        9 * rows * cols * rank,
    )(o, w, rt, *in_hbm(momentum, grads))


def write_out(value, out_ref, buffer, sems):
    width = buffer.shape[1] // CHUNKS
    copies = []
    for k in range(CHUNKS):
        c = columns(k, width)
        buffer[:, c] = value(k, c).astype(buffer.dtype)
        copies.append(
            pltpu.make_async_copy(buffer.at[:, c], out_ref.at[:, c], sems.at[k])
        )
        copies[k].start()
    for copy in copies:
        copy.wait()


def change_kernel(factor, o_ref, rs_ref, raw_ref, c_ref, raw, buffer, came, sent):
    wait = fetch(pair_moves(raw_ref, raw), came)
    o = split(o_ref[...] * (factor * rs_ref[:1]))

    def value(k, c):
        wait(k)
        return dot3(o, (raw[0, :, c], raw[1, :, c]), NN)

    write_out(value, c_ref, buffer, sent)


def first_change(factor, o, rs, raw):
    rows, rank = o.shape
    cols = raw.shape[2]
    return call(
        functools.partial(change_kernel, factor),
        [VM, VM, ANY],
        pltpu.HBM((rows, cols), F32),
        ANY,
        [
            pltpu.VMEM(raw.shape, BF16),
            pltpu.VMEM((rows, cols), F32),
            dma(CHUNKS, 1),
            dma(CHUNKS),
        ],
        6 * rows * cols * rank,
    )(o, rs, *in_hbm(raw))


def last_raw_kernel(p_ref, w_ref, x_ref, raw_ref, o_ref, sq_ref):
    blocks = x_ref.shape[0] // CHUNKS
    o_ref[...] = exact(p_ref[...], w_ref[...], NT)
    w = split(w_ref[...])
    n = w_ref.shape[0]
    total = jnp.zeros((n, 1), F32)
    for k in range(CHUNKS):
        c = columns(k, blocks * LANES)
        block = jnp.concatenate([x_ref[k * blocks + q] for q in range(blocks)], axis=1)
        raw = dot3(w, split(block), NN)
        raw_ref[0, :, c], raw_ref[1, :, c] = split(raw)
        total = total + jnp.sum(raw * raw, axis=1, keepdims=True)
    squares = jnp.where(same(n), jnp.broadcast_to(total, (n, n)), 0.0)
    row = jnp.sum(squares, axis=0, keepdims=True)
    for k in range(sq_ref.shape[0]):
        sq_ref[k] = jnp.broadcast_to(row, (8, n))


def last_raw(p, w, x, peers):
    rows, rank = p.shape
    cols = x.shape[0] * LANES
    return call(
        last_raw_kernel,
        [VM] * 3,
        [
            pair((rank, cols)),
            jax.ShapeDtypeStruct((rows, rank), F32),
            jax.ShapeDtypeStruct((peers, 8, rank), F32),
        ],
        [VM] * 3,
        [],
        3 * rows * cols * rank,
    )(p, w, x)


def state_kernel(o_ref, raw_ref, b_ref, s_ref, b, buffer, came, sent):
    wait = fetch(pair_moves(b_ref, b), came)
    o = split((1.0 - KEEP_RATE) * o_ref[...])

    def value(k, c):
        part = dot3(o, (raw_ref[0, :, c], raw_ref[1, :, c]), NN)
        wait(k)
        return b[0, :, c].astype(F32) + b[1, :, c].astype(F32) - part

    write_out(value, s_ref, buffer, sent)


def last_state(o, raw, b):
    _, rows, cols = b.shape
    rank = o.shape[1]
    return call(
        state_kernel,
        [VM, VM, ANY],
        pltpu.HBM((rows, cols), F32),
        ANY,
        [
            pltpu.VMEM(b.shape, BF16),
            pltpu.VMEM((rows, cols), F32),
            dma(CHUNKS, 1),
            dma(CHUNKS),
        ],
        6 * rows * cols * rank,
    )(o, raw, *in_hbm(b))


def last_change_kernel(
    factor, o_ref, sq_ref, raw_ref, c_ref, out_ref, held, buffer, came, sent
):
    width = held.shape[1] // CHUNKS
    wait = fetch(
        [
            [(c_ref.at[:, columns(k, width)], held.at[:, columns(k, width)])]
            for k in range(CHUNKS)
        ],
        came,
    )
    total = sq_ref[0, :1]
    for k in range(1, sq_ref.shape[0]):
        total = total + sq_ref[k, :1]
    o = split(o_ref[...] * (factor * lax.rsqrt(total + NORM_EPS)))

    def value(k, c):
        part = dot3(o, (raw_ref[0, :, c], raw_ref[1, :, c]), NN)
        wait(k)
        return held[:, c] + part

    write_out(value, out_ref, buffer, sent)


def last_change(factor, o, sq, raw, change):
    rows, cols = change.shape
    rank = o.shape[1]
    return call(
        functools.partial(last_change_kernel, factor),
        [VM, VM, VM, ANY],
        pltpu.HBM((rows, cols), BF16),
        ANY,
        [
            pltpu.VMEM((rows, cols), F32),
            pltpu.VMEM((rows, cols), BF16),
            dma(CHUNKS, 1),
            dma(CHUNKS),
        ],
        6 * rows * cols * rank,
    )(o, sq, raw, *in_hbm(change))


SIDE = 4


def chip_permute(x, move):
    pairs = [(2 * k + c, 2 * move(k) + c) for k in range(SIDE) for c in range(2)]
    return lax.ppermute(x, "col", pairs)


def core_permute(x):
    return lax.ppermute(x, "col", [(k, k ^ 1) for k in range(2 * SIDE)])


def near(k):
    return k ^ 1


def far(k):
    return SIDE - 1 - k


def col_sum(parts, beside):
    core = lax.axis_index("col") % 2
    mine = lax.dynamic_slice_in_dim(parts, 2 * core, 2, 0)
    theirs = lax.dynamic_slice_in_dim(parts, 2 - 2 * core, 2, 0)
    mine = mine + core_permute(theirs)
    a, b = mine[0], mine[1]
    near_a, far_b, beside = lax.optimization_barrier(
        (chip_permute(a, near), chip_permute(b, far), beside)
    )
    a, b = a + near_a, b + far_b
    a, b = a + chip_permute(a, far), b + chip_permute(b, near)
    mine = jnp.stack([a, b])
    return mine, core_permute(mine), beside


def by_chip(part):
    core = lax.axis_index("col") % 2
    other = core_permute(part)
    chip = jnp.where(
        core == 0, jnp.concatenate([part, other]), jnp.concatenate([other, part])
    )
    return [chip] + [
        chip_permute(chip, lambda k, d=d: (k - d) % SIDE) for d in range(1, SIDE)
    ]


def exchange(x, axis):
    return lax.all_to_all(x, axis, 0, 0, tiled=True)


def row_total(blocks, rank, place, beside):
    got, beside = lax.optimization_barrier((exchange(blocks, "row"), beside))
    own, part = spread_sum(got, rank)
    total = exchange(own, "row")
    return total, inverse_factor(by_chip(part), place), beside


def shards(momentum, grads, basis):
    rows, cols = momentum.shape
    rank = basis.shape[1]
    peers = lax.axis_size("col")
    factor = (rows * lax.axis_size("row") * cols * peers / rank) ** 0.5
    place = lax.axis_index("col").astype(jnp.int32)[None]

    held = [pltpu.VMEM((rows, cols), F32), pltpu.VMEM((1, rows, cols), BF16)]
    part = first_projection(momentum, grads, basis)
    mine, theirs, _ = col_sum(part.reshape(4, rows // 4, rank), [])
    x1, p1, _ = products(
        first_products_kernel, place, mine, theirs, [momentum, grads], held, peers
    )
    x1, w1, _ = row_total(x1, rank, place, [])
    part, o1, rt1 = middle(p1, w1, x1, momentum, grads)
    mine, theirs, (raw1, buffer) = col_sum(
        part, second_buffer(o1, w1, rt1, momentum, grads)
    )
    held = [pltpu.VMEM((2, rows, cols), BF16)]
    x2, p2, rs1 = products(
        second_products_kernel, place, mine, theirs, [buffer], held, peers
    )
    x2, w2, change1 = row_total(x2, rank, place, first_change(factor, o1, rs1, raw1))
    raw2, o2, sq2 = last_raw(p2, w2, x2, peers)
    sq2 = exchange(sq2, "col")
    state = last_state(o2, raw2, buffer)
    change = last_change(factor, o2, sq2, raw2, change1)
    return change, state


def solution(mesh):
    return jax.shard_map(
        shards,
        mesh=mesh,
        in_specs=(P("row", "col"), P(None, "row", "col"), P("col", None)),
        out_specs=(P("row", "col"), P("row", "col")),
        check_vma=False,
    )
```

```python
import functools

import jax
import jax.numpy as jnp
from jax import lax
from jax.experimental import pallas as pl
from jax.experimental.pallas import tpu as pltpu
from jax.sharding import PartitionSpec as P

KEEP_RATE = 0.95
NORM_EPS = 1e-06
LANES = 128
CHUNKS = 4
F32 = jnp.float32
BF16 = jnp.bfloat16
VMEM_LIMIT = 20 * 1024 * 1024
NN = (((1,), (0,)), ((), ()))
NT = (((1,), (1,)), ((), ()))


def split(x):
    high = x.astype(BF16)
    return high, (x - high.astype(F32)).astype(BF16)


def mm(a, b, dims):
    return lax.dot_general(a, b, dims, preferred_element_type=F32)


def dot3(a, b, dims):
    return mm(a[0], b[0], dims) + (mm(a[0], b[1], dims) + mm(a[1], b[0], dims))


def exact(a, b, dims):
    return lax.dot_general(
        a, b, dims, precision=lax.Precision.HIGHEST, preferred_element_type=F32
    )


def call(kernel, in_specs, out_shape, out_specs, scratch, cost):
    return pl.pallas_call(
        kernel,
        in_specs=in_specs,
        out_specs=out_specs,
        out_shape=out_shape,
        scratch_shapes=scratch,
        compiler_params=pltpu.CompilerParams(vmem_limit_bytes=VMEM_LIMIT),
        cost_estimate=pl.CostEstimate(
            flops=cost, transcendentals=0, bytes_accessed=8 * 1024 * 1024
        ),
    )


VM = pl.BlockSpec(memory_space=pltpu.VMEM)
SM = pl.BlockSpec(memory_space=pltpu.SMEM)
ANY = pl.BlockSpec(memory_space=pl.ANY)


def in_hbm(*arrays):
    return [pltpu.with_memory_space_constraint(a, pltpu.HBM) for a in arrays]


def pair(shape):
    return jax.ShapeDtypeStruct((2, *shape), BF16)


def pair_in_hbm(shape):
    return pltpu.HBM((2, *shape), BF16)


def dma(*shape):
    return pltpu.SemaphoreType.DMA(shape)


def fetch(moves, sems):
    def copies(k):
        return [
            pltpu.make_async_copy(a, b, sems.at[k, n]) for n, (a, b) in enumerate(moves(k))
        ]

    for k in range(CHUNKS):
        for copy in copies(k):
            copy.start()

    def wait(k):
        for copy in copies(k):
            copy.wait()

    return wait


def send(moves, sems):
    def copies(k):
        return [
            pltpu.make_async_copy(a, b, sems.at[k, n]) for n, (a, b) in enumerate(moves(k))
        ]

    def start(k):
        for copy in copies(k):
            copy.start()

    def finish():
        for k in range(CHUNKS):
            for copy in copies(k):
                copy.wait()

    return start, finish


def columns(k, width):
    if isinstance(k, int):
        return pl.ds(k * width, width)
    return pl.ds(pl.multiple_of(k * width, width), width)


def each(block, count=CHUNKS):
    lax.fori_loop(0, count, lambda k, _: (block(k), 0)[1], 0)


def same(n):
    i = lax.broadcasted_iota(jnp.int32, (n, n), 0)
    return i == lax.broadcasted_iota(jnp.int32, (n, n), 1)


def buffer_moves(m_ref, g_ref, m, g):
    width = m.shape[1] // CHUNKS

    def moves(k):
        c = columns(k, width)
        pairs = [(m_ref.at[:, c], m.at[:, c])]
        for n in range(g.shape[0]):
            pairs.append((g_ref.at[n, :, c], g.at[n, :, c]))
        return pairs

    return moves


def buffer_block(m, g, c):
    b = m[:, c]
    for n in range(g.shape[0]):
        b = b + g[n, :, c].astype(F32)
    return b


def first_kernel(m_ref, g_ref, v_ref, p_ref, m, g, v, sems):
    width = m.shape[1] // CHUNKS
    moves = buffer_moves(m_ref, g_ref, m, g)
    wait = fetch(
        lambda k: moves(k) + [(v_ref.at[columns(k, width)], v.at[columns(k, width)])], sems
    )
    p_ref[...] = jnp.zeros_like(p_ref)

    def block(k):
        c = columns(k, width)
        wait(k)
        p_ref[...] += dot3(split(buffer_block(m, g, c)), split(v[c]), NN)

    each(block)


def first_projection(momentum, grads, basis):
    rows, cols = momentum.shape
    rank = basis.shape[1]
    return call(
        first_kernel,
        [ANY] * 3,
        jax.ShapeDtypeStruct((rows, rank), F32),
        VM,
        [
            pltpu.VMEM((rows, cols), F32),
            pltpu.VMEM((1, rows, cols), BF16),
            pltpu.VMEM((cols, rank), F32),
            dma(CHUNKS, 3),
        ],
        6 * rows * cols * rank,
    )(*in_hbm(momentum, grads, basis))


def store_products(inputs, outputs, scratch, block, scaled, direct):
    n_ref, mine_ref, theirs_ref = inputs
    x_ref, p_ref, rs_ref = outputs
    parts, t, shares, pair_of_p = scratch[:4]
    held, sems = (None, None) if direct else scratch[4:]
    core = lax.rem(n_ref[0], 2)
    parts[pl.ds(2 * core, 2)] = mine_ref[...]
    parts[pl.ds(2 - 2 * core, 2)] = theirs_ref[...]
    rows, rank = p_ref.shape
    height = rows // 4
    p = jnp.concatenate([parts[k, :height] for k in range(4)], axis=0)
    if scaled:
        rs = lax.rsqrt(parts[0, height : height + 8] + NORM_EPS)
        p = p * rs[:1]
    else:
        rs = jnp.ones(rs_ref.shape, F32)
    rs_ref[...] = rs
    p_ref[...] = p
    turned, half = p.T, LANES
    t[: 2 * half] = exact(turned, p[:, :half], NN)
    t[2 * half :] = exact(turned[half:], p[:, half:], NN)
    size = x_ref.shape[1] - rank
    share = t[pl.ds(pl.multiple_of(n_ref[0] * size, size), size), :]
    pt = split(turned)
    blocks = x_ref.shape[0] // CHUNKS
    shares[...] = share
    pair_of_p[0], pair_of_p[1] = pt
    x = x_ref if direct else held

    def fill(k):
        r = dot3((pair_of_p[0], pair_of_p[1]), block(k), NN)
        for q in range(blocks):
            x[k * blocks + q, :rank] = r[:, q * LANES : (q + 1) * LANES]
            x[k * blocks + q, rank:] = shares[...]
        if not direct:
            start(k)

    if not direct:
        start, finish = send(
            lambda k: [(held.at[columns(k, blocks)], x_ref.at[columns(k, blocks)])], sems
        )
    each(fill)
    if not direct:
        finish()


def first_products_kernel(
    n_ref, mine_ref, theirs_ref, m_ref, g_ref, x_ref, p_ref, rs_ref, m, g, came, *scratch
):
    wait = fetch(buffer_moves(m_ref, g_ref, m, g), came)

    def block(k):
        wait(k)
        return split(buffer_block(m, g, columns(k, m.shape[1] // CHUNKS)))

    store_products(
        (n_ref, mine_ref, theirs_ref), (x_ref, p_ref, rs_ref), scratch, block, False, True
    )


def pair_moves(b_ref, b):
    width = b.shape[2] // CHUNKS

    def moves(k):
        c = columns(k, width)
        return [(b_ref.at[:, :, c], b.at[:, :, c])]

    return moves


def second_products_kernel(
    n_ref, mine_ref, theirs_ref, b_ref, x_ref, p_ref, rs_ref, b, came, *scratch
):
    wait = fetch(pair_moves(b_ref, b), came)

    def block(k):
        wait(k)
        c = columns(k, b.shape[2] // CHUNKS)
        return b[0, :, c], b[1, :, c]

    store_products(
        (n_ref, mine_ref, theirs_ref), (x_ref, p_ref, rs_ref), scratch, block, True, False
    )


def products(kernel, place, mine, theirs, bigs, held, peers, direct):
    rows, cols = bigs[0].shape[-2:]
    _, height, rank = mine.shape
    tail = 3 * LANES // peers
    shape = (cols // LANES, rank + tail, LANES)
    return call(
        kernel,
        [SM, VM, VM] + [ANY] * len(bigs),
        [
            jax.ShapeDtypeStruct(shape, F32) if direct else pltpu.HBM(shape, F32),
            jax.ShapeDtypeStruct((rows, rank), F32),
            jax.ShapeDtypeStruct((8, rank), F32),
        ],
        [VM if direct else ANY, VM, VM],
        held
        + [
            dma(CHUNKS, len(bigs)),
            pltpu.VMEM((4, height, rank), F32),
            pltpu.VMEM((3 * LANES, LANES), F32),
            pltpu.VMEM((tail, LANES), F32),
            pltpu.VMEM((2, rank, rows), BF16),
        ]
        + ([] if direct else [pltpu.VMEM(shape, F32), dma(CHUNKS, 1)]),
        6 * rows * cols * rank,
    )(place, mine, theirs, *in_hbm(*bigs))


def spread_kernel(x_ref, y_ref, t_ref, y, sems):
    count = x_ref.shape[0]
    rank = y.shape[0]
    total = x_ref[0]
    for k in range(1, count):
        total = total + x_ref[k]
    y[...] = total[:rank]
    copies = [
        pltpu.make_async_copy(y, y_ref.at[k], sems.at[k]) for k in range(count)
    ]
    for copy in copies:
        copy.start()
    t_ref[...] = total[rank:]
    for copy in copies:
        copy.wait()


def spread_sum(x, rank):
    count, height, width = x.shape
    return call(
        spread_kernel,
        [VM],
        [
            pltpu.HBM((count, rank, width), F32),
            jax.ShapeDtypeStruct((height - rank, width), F32),
        ],
        [ANY, VM],
        [pltpu.VMEM((rank, width), F32), pltpu.SemaphoreType.DMA((count,))],
        count * height * width,
    )(x)


def eliminated(m):
    n = m.shape[0]
    eye = same(n)
    across = lax.rsqrt(jnp.sum(jnp.where(eye, m, 0.0), axis=0, keepdims=True))
    down = lax.rsqrt(jnp.sum(jnp.where(eye, m, 0.0), axis=1, keepdims=True))
    m = m * down * across
    lane = lax.broadcasted_iota(jnp.int32, (8, n), 1)
    sub = lax.broadcasted_iota(jnp.int32, (8, n), 0)
    tiles = [m[8 * t : 8 * t + 8] for t in range(n // 8)]
    for j in range(0, n, 2):
        t, r = divmod(j, 8)
        first, second = lane[:1] == j, lane[:1] == j + 1
        both = (lane >= j) & (lane < j + 2)
        c0 = [jnp.broadcast_to(x[:, j : j + 1], (8, n)) for x in tiles[t:]]
        c1 = [jnp.broadcast_to(x[:, j + 1 : j + 2], (8, n)) for x in tiles[t:]]
        row0, row1 = tiles[t][r : r + 1], tiles[t][r + 1 : r + 2]
        a, b = c0[0][r : r + 1], c0[0][r + 1 : r + 2]
        d = c1[0][r + 1 : r + 2]
        inv_a = 1.0 / a
        inv_d = a * (1.0 / (a * d - b * b))
        ratio = b * inv_a
        low = row1 - ratio * row0
        use1 = jnp.where(first, -ratio, jnp.where(second, 1.0, low)) * inv_d
        use0 = jnp.where(first, 1.0, jnp.where(second, 0.0, row0)) * inv_a - ratio * use1
        kept = jnp.where(first, -ratio, low)
        for s in range(t, n // 8):
            new = jnp.where(both, 0.0, tiles[s]) - c0[s - t] * use0 - c1[s - t] * use1
            if s == t:
                new = jnp.where(sub > r + 1, new, jnp.where(sub == r + 1, kept, tiles[s]))
            tiles[s] = new
    m = jnp.concatenate(tiles, axis=0)
    i = lax.broadcasted_iota(jnp.int32, (n, n), 0)
    j = lax.broadcasted_iota(jnp.int32, (n, n), 1)
    pivots = jnp.sum(jnp.where(eye, m, 0.0), axis=1, keepdims=True)
    unit = jnp.where(i > j, m, jnp.where(eye, 1.0, 0.0))
    return unit * lax.rsqrt(pivots) * across


def cholesky_kernel(n_ref, p_ref, *refs):
    pieces, (w_ref, o_ref, a, low) = refs[:-4], refs[-4:]
    size = pieces[0].shape[0]
    count = len(pieces)
    for k, piece in enumerate(pieces):
        place = lax.rem(n_ref[0] // 2 + k, count)
        a[pl.ds(pl.multiple_of(place * size, size), size), :] = piece[...]
    half = LANES

    def body(b, carry):
        w = eliminated(a[pl.ds(pl.multiple_of(2 * b * half, half), half), :])
        first = pl.multiple_of(b * half, half)
        w_ref[pl.ds(first, half), pl.ds(first, half)] = w

        @pl.when(b == 0)
        def _():
            low[...] = exact(a[half : 2 * half], w, NT)
            a[2 * half :] -= exact(low[...], low[...], NT)

        return carry

    lax.fori_loop(0, 2, body, 0)
    w_ref[:half, half:] = jnp.zeros((half, half), F32)
    w_ref[half:, :half] = -exact(
        w_ref[half:, half:], exact(low[...], w_ref[:half, :half], NN), NN
    )
    o_ref[...] = exact(p_ref[...], w_ref[...], NT)


def inverse_factor(pieces, place, p):
    rank = p.shape[1]
    return call(
        cholesky_kernel,
        [SM, VM] + [VM] * len(pieces),
        [jax.ShapeDtypeStruct((rank, rank), F32), jax.ShapeDtypeStruct(p.shape, F32)],
        [VM, VM],
        [pltpu.VMEM((3 * LANES, LANES), F32), pltpu.VMEM((LANES, LANES), F32)],
        10**10,
    )(place, p, *pieces)


def middle_kernel(o_ref, w_ref, x_ref, m_ref, g_ref, q_ref, rt_ref, m, g, q_sum, s_ref, sems):
    wait = fetch(buffer_moves(m_ref, g_ref, m, g), sems)

    def turn(k):
        c = columns(k, LANES)
        rt_ref[0, :, c], rt_ref[1, :, c] = split(x_ref[k])

    each(turn, x_ref.shape[0])
    rt = (rt_ref[0], rt_ref[1])
    w = w_ref[...]
    s_ref[...] = exact(exact(w, dot3(rt, rt, NT), NN), w, NT)
    width = m.shape[1] // CHUNKS
    q_sum[...] = jnp.zeros_like(q_sum)

    def block(k):
        c = columns(k, width)
        wait(k)
        q_sum[...] += dot3(
            split(buffer_block(m, g, c)), (rt_ref[0, :, c], rt_ref[1, :, c]), NT
        )

    each(block)
    s = s_ref[...]
    q = dot3(split(q_sum[...]), split(w_ref[...]), NT) - dot3(
        split((1.0 - KEEP_RATE) * o_ref[...]), split(s), NN
    )
    n = s.shape[0]
    squares = jnp.sum(jnp.where(same(n), s, 0.0), axis=0, keepdims=True)
    height = q_ref.shape[1] - 8
    for k in range(q_ref.shape[0]):
        q_ref[k, :height] = q[k * height : (k + 1) * height]
        q_ref[k, height:] = jnp.broadcast_to(squares, (8, n))


def middle(o, w, x, momentum, grads):
    rows, cols = momentum.shape
    rank = o.shape[1]
    return call(
        middle_kernel,
        [VM] * 3 + [ANY] * 2,
        [jax.ShapeDtypeStruct((4, rows // 4 + 8, rank), F32), pair((rank, cols))],
        [VM] * 2,
        [
            pltpu.VMEM((rows, cols), F32),
            pltpu.VMEM(grads.shape, BF16),
            pltpu.VMEM((rows, rank), F32),
            pltpu.VMEM((rank, rank), F32),
            dma(CHUNKS, 3),
        ],
        10 * rows * cols * rank,
    )(o, w, x, *in_hbm(momentum, grads))


def update_kernel(
    o_ref, w_ref, rt_ref, m_ref, g_ref, raw_ref, b_ref, m, g, raw, b, came, sent
):
    wait = fetch(buffer_moves(m_ref, g_ref, m, g), came)
    o = split((1.0 - KEEP_RATE) * o_ref[...])
    w = split(w_ref[...])
    width = m.shape[1] // CHUNKS
    start, finish = send(
        lambda k: [
            (a.at[:, :, columns(k, width)], r.at[:, :, columns(k, width)])
            for a, r in ((raw, raw_ref), (b, b_ref))
        ],
        sent,
    )

    def block(k):
        c = columns(k, width)
        now = split(dot3(w, (rt_ref[0, :, c], rt_ref[1, :, c]), NN))
        raw[0, :, c], raw[1, :, c] = now
        wait(k)
        b[0, :, c], b[1, :, c] = split(buffer_block(m, g, c) - dot3(o, now, NN))
        start(k)

    each(block)
    finish()


def second_buffer(o, w, rt, momentum, grads):
    rows, cols = momentum.shape
    rank = o.shape[1]
    return call(
        update_kernel,
        [VM] * 3 + [ANY] * 2,
        [pair_in_hbm((rank, cols)), pair_in_hbm((rows, cols))],
        [ANY] * 2,
        [
            pltpu.VMEM((rows, cols), F32),
            pltpu.VMEM(grads.shape, BF16),
            pltpu.VMEM((2, rank, cols), BF16),
            pltpu.VMEM((2, rows, cols), BF16),
            dma(CHUNKS, 3),
            dma(CHUNKS, 2),
        ],
        9 * rows * cols * rank,
    )(o, w, rt, *in_hbm(momentum, grads))


def write_out(value, out_ref, buffer, sems):
    width = buffer.shape[1] // CHUNKS
    start, finish = send(
        lambda k: [(buffer.at[:, columns(k, width)], out_ref.at[:, columns(k, width)])], sems
    )

    def block(k):
        c = columns(k, width)
        buffer[:, c] = value(k, c).astype(buffer.dtype)
        start(k)

    each(block)
    finish()


def change_kernel(factor, o_ref, rs_ref, raw_ref, c_ref, raw, buffer, came, sent):
    wait = fetch(pair_moves(raw_ref, raw), came)
    o = split(o_ref[...] * (factor * rs_ref[:1]))

    def value(k, c):
        wait(k)
        return dot3(o, (raw[0, :, c], raw[1, :, c]), NN)

    write_out(value, c_ref, buffer, sent)


def first_change(factor, o, rs, raw):
    rows, rank = o.shape
    cols = raw.shape[2]
    return call(
        functools.partial(change_kernel, factor),
        [VM, VM, ANY],
        pltpu.HBM((rows, cols), F32),
        ANY,
        [
            pltpu.VMEM(raw.shape, BF16),
            pltpu.VMEM((rows, cols), F32),
            dma(CHUNKS, 1),
            dma(CHUNKS, 1),
        ],
        6 * rows * cols * rank,
    )(o, rs, *in_hbm(raw))


def last_raw_kernel(w_ref, x_ref, raw_ref, sq_ref, total):
    blocks = x_ref.shape[0] // CHUNKS
    n = w_ref.shape[0]
    total[...] = jnp.zeros_like(total)

    def block(k):
        c = columns(k, blocks * LANES)
        part = jnp.concatenate([x_ref[k * blocks + q] for q in range(blocks)], axis=1)
        raw = dot3(split(w_ref[...]), split(part), NN)
        raw_ref[0, :, c], raw_ref[1, :, c] = split(raw)
        total[...] += jnp.sum(raw * raw, axis=1, keepdims=True)

    each(block)
    squares = jnp.where(same(n), jnp.broadcast_to(total[:, :1], (n, n)), 0.0)
    row = jnp.sum(squares, axis=0, keepdims=True)
    for k in range(sq_ref.shape[0]):
        sq_ref[k] = jnp.broadcast_to(row, (8, n))


def last_raw(w, x, peers):
    rank = w.shape[0]
    cols = x.shape[0] * LANES
    return call(
        last_raw_kernel,
        [VM] * 2,
        [pair((rank, cols)), jax.ShapeDtypeStruct((peers, 8, rank), F32)],
        [VM] * 2,
        [pltpu.VMEM((rank, LANES), F32)],
        6 * rank * cols * rank,
    )(w, *in_hbm(x))


def state_kernel(o_ref, raw_ref, b_ref, s_ref, b, buffer, came, sent):
    wait = fetch(pair_moves(b_ref, b), came)
    o = split((1.0 - KEEP_RATE) * o_ref[...])

    def value(k, c):
        part = dot3(o, (raw_ref[0, :, c], raw_ref[1, :, c]), NN)
        wait(k)
        return b[0, :, c].astype(F32) + b[1, :, c].astype(F32) - part

    write_out(value, s_ref, buffer, sent)


def last_state(o, raw, b):
    _, rows, cols = b.shape
    rank = o.shape[1]
    return call(
        state_kernel,
        [VM, VM, ANY],
        pltpu.HBM((rows, cols), F32),
        ANY,
        [
            pltpu.VMEM(b.shape, BF16),
            pltpu.VMEM((rows, cols), F32),
            dma(CHUNKS, 1),
            dma(CHUNKS, 1),
        ],
        6 * rows * cols * rank,
    )(o, raw, *in_hbm(b))


def last_change_kernel(
    factor, o_ref, sq_ref, raw_ref, c_ref, out_ref, held, buffer, came, sent
):
    width = held.shape[1] // CHUNKS
    wait = fetch(
        lambda k: [(c_ref.at[:, columns(k, width)], held.at[:, columns(k, width)])], came
    )
    total = sq_ref[0, :1]
    for k in range(1, sq_ref.shape[0]):
        total = total + sq_ref[k, :1]
    o = split(o_ref[...] * (factor * lax.rsqrt(total + NORM_EPS)))

    def value(k, c):
        part = dot3(o, (raw_ref[0, :, c], raw_ref[1, :, c]), NN)
        wait(k)
        return held[:, c] + part

    write_out(value, out_ref, buffer, sent)


def last_change(factor, o, sq, raw, change):
    rows, cols = change.shape
    rank = o.shape[1]
    return call(
        functools.partial(last_change_kernel, factor),
        [VM, VM, VM, ANY],
        pltpu.HBM((rows, cols), BF16),
        ANY,
        [
            pltpu.VMEM((rows, cols), F32),
            pltpu.VMEM((rows, cols), BF16),
            dma(CHUNKS, 1),
            dma(CHUNKS, 1),
        ],
        6 * rows * cols * rank,
    )(o, sq, raw, *in_hbm(change))


SIDE = 4


def chip_permute(x, move):
    pairs = [(2 * k + c, 2 * move(k) + c) for k in range(SIDE) for c in range(2)]
    return lax.ppermute(x, "col", pairs)


def core_permute(x):
    return lax.ppermute(x, "col", [(k, k ^ 1) for k in range(2 * SIDE)])


def near(k):
    return k ^ 1


def far(k):
    return SIDE - 1 - k


def col_sum(parts, beside):
    core = lax.axis_index("col") % 2
    mine = lax.dynamic_slice_in_dim(parts, 2 * core, 2, 0)
    theirs = lax.dynamic_slice_in_dim(parts, 2 - 2 * core, 2, 0)
    mine = mine + core_permute(theirs)
    a, b = mine[0], mine[1]
    near_a, far_b, beside = lax.optimization_barrier(
        (chip_permute(a, near), chip_permute(b, far), beside)
    )
    a, b = a + near_a, b + far_b
    a, b = a + chip_permute(a, far), b + chip_permute(b, near)
    mine = jnp.stack([a, b])
    return mine, core_permute(mine), beside


def by_chip(part):
    core = lax.axis_index("col") % 2
    other = core_permute(part)
    chip = jnp.where(
        core == 0, jnp.concatenate([part, other]), jnp.concatenate([other, part])
    )
    return [chip] + [
        chip_permute(chip, lambda k, d=d: (k - d) % SIDE) for d in range(1, SIDE)
    ]


def exchange(x, axis):
    return lax.all_to_all(x, axis, 0, 0, tiled=True)


def row_total(blocks, p, place, beside):
    got, beside = lax.optimization_barrier((exchange(blocks, "row"), beside))
    own, part = spread_sum(got, p.shape[1])
    total = exchange(own, "row")
    return total, *inverse_factor(by_chip(part), place, p), beside


def shards(momentum, grads, basis):
    rows, cols = momentum.shape
    rank = basis.shape[1]
    peers = lax.axis_size("col")
    factor = (rows * lax.axis_size("row") * cols * peers / rank) ** 0.5
    place = lax.axis_index("col").astype(jnp.int32)[None]

    held = [pltpu.VMEM((rows, cols), F32), pltpu.VMEM((1, rows, cols), BF16)]
    part = first_projection(momentum, grads, basis)
    mine, theirs, _ = col_sum(part.reshape(4, rows // 4, rank), [])
    x1, p1, _ = products(
        first_products_kernel, place, mine, theirs, [momentum, grads], held, peers, True
    )
    x1, w1, o1, _ = row_total(x1, p1, place, [])
    part, rt1 = middle(o1, w1, x1, momentum, grads)
    mine, theirs, (raw1, buffer) = col_sum(
        part, second_buffer(o1, w1, rt1, momentum, grads)
    )
    held = [pltpu.VMEM((2, rows, cols), BF16)]
    x2, p2, rs1 = products(
        second_products_kernel, place, mine, theirs, [buffer], held, peers, False
    )
    change1 = first_change(factor, o1, rs1, raw1)
    x2, w2, o2, change1 = row_total(x2, p2, place, change1)
    raw2, sq2 = last_raw(w2, x2, peers)
    sq2 = exchange(sq2, "col")
    state = last_state(o2, raw2, buffer)
    change = last_change(factor, o2, sq2, raw2, change1)
    return change, state


def solution(mesh):
    return jax.shard_map(
        shards,
        mesh=mesh,
        in_specs=(P("row", "col"), P(None, "row", "col"), P("col", None)),
        out_specs=(P("row", "col"), P("row", "col")),
        check_vma=False,
    )
```

```python
import functools

import jax
import jax.numpy as jnp
from jax import lax
from jax.experimental import pallas as pl
from jax.experimental.pallas import tpu as pltpu
from jax.sharding import PartitionSpec as P

KEEP_RATE = 0.95
NORM_EPS = 1e-06
LANES = 128
CHUNKS = 4
F32 = jnp.float32
BF16 = jnp.bfloat16
VMEM_LIMIT = 20 * 1024 * 1024
NN = (((1,), (0,)), ((), ()))
NT = (((1,), (1,)), ((), ()))


def split(x):
    high = x.astype(BF16)
    return high, (x - high.astype(F32)).astype(BF16)


def mm(a, b, dims):
    return lax.dot_general(a, b, dims, preferred_element_type=F32)


def dot3(a, b, dims):
    return mm(a[0], b[0], dims) + (mm(a[0], b[1], dims) + mm(a[1], b[0], dims))


def exact(a, b, dims):
    return lax.dot_general(
        a, b, dims, precision=lax.Precision.HIGHEST, preferred_element_type=F32
    )


def call(kernel, in_specs, out_shape, out_specs, scratch, cost, aliases=None):
    return pl.pallas_call(
        kernel,
        in_specs=in_specs,
        out_specs=out_specs,
        out_shape=out_shape,
        scratch_shapes=scratch,
        input_output_aliases=aliases or {},
        compiler_params=pltpu.CompilerParams(vmem_limit_bytes=VMEM_LIMIT),
        cost_estimate=pl.CostEstimate(
            flops=cost, transcendentals=0, bytes_accessed=8 * 1024 * 1024
        ),
    )


VM = pl.BlockSpec(memory_space=pltpu.VMEM)
SM = pl.BlockSpec(memory_space=pltpu.SMEM)
ANY = pl.BlockSpec(memory_space=pl.ANY)


def in_hbm(*arrays):
    return [pltpu.with_memory_space_constraint(a, pltpu.HBM) for a in arrays]


def pair(shape):
    return jax.ShapeDtypeStruct((2, *shape), BF16)


def pair_in_hbm(shape):
    return pltpu.HBM((2, *shape), BF16)


def dma(*shape):
    return pltpu.SemaphoreType.DMA(shape)


def fetch(moves, sems, count=CHUNKS):
    def copies(k):
        return [
            pltpu.make_async_copy(a, b, sems.at[k, n]) for n, (a, b) in enumerate(moves(k))
        ]

    for k in range(count):
        for copy in copies(k):
            copy.start()

    def wait(k):
        for copy in copies(k):
            copy.wait()

    return wait


def send(moves, sems, count=CHUNKS):
    def copies(k):
        return [
            pltpu.make_async_copy(a, b, sems.at[k, n]) for n, (a, b) in enumerate(moves(k))
        ]

    def start(k):
        for copy in copies(k):
            copy.start()

    def finish():
        for k in range(count):
            for copy in copies(k):
                copy.wait()

    return start, finish


def columns(k, width):
    if isinstance(k, int):
        return pl.ds(k * width, width)
    return pl.ds(pl.multiple_of(k * width, width), width)


def each(block, count=CHUNKS):
    lax.fori_loop(0, count, lambda k, _: (block(k), 0)[1], 0)


def same(n):
    i = lax.broadcasted_iota(jnp.int32, (n, n), 0)
    return i == lax.broadcasted_iota(jnp.int32, (n, n), 1)


def buffer_moves(m_ref, g_ref, m, g):
    width = m.shape[1] // CHUNKS

    def moves(k):
        c = columns(k, width)
        pairs = [(m_ref.at[:, c], m.at[:, c])]
        for n in range(g.shape[0]):
            pairs.append((g_ref.at[n, :, c], g.at[n, :, c]))
        return pairs

    return moves


def buffer_block(m, g, c):
    b = m[:, c]
    for n in range(g.shape[0]):
        b = b + g[n, :, c].astype(F32)
    return b


def first_kernel(m_ref, g_ref, v_ref, p_ref, m, g, v, sems):
    width = m.shape[1] // CHUNKS
    moves = buffer_moves(m_ref, g_ref, m, g)
    wait = fetch(
        lambda k: moves(k) + [(v_ref.at[columns(k, width)], v.at[columns(k, width)])], sems
    )
    p_ref[...] = jnp.zeros_like(p_ref)

    def block(k):
        c = columns(k, width)
        wait(k)
        p_ref[...] += dot3(split(buffer_block(m, g, c)), split(v[c]), NN)

    each(block)


def first_projection(momentum, grads, basis):
    rows, cols = momentum.shape
    rank = basis.shape[1]
    return call(
        first_kernel,
        [ANY] * 3,
        jax.ShapeDtypeStruct((rows, rank), F32),
        VM,
        [
            pltpu.VMEM((rows, cols), F32),
            pltpu.VMEM((1, rows, cols), BF16),
            pltpu.VMEM((cols, rank), F32),
            dma(CHUNKS, 3),
        ],
        6 * rows * cols * rank,
    )(*in_hbm(momentum, grads, basis))


def store_products(inputs, outputs, scratch, block, scaled):
    n_ref, mine_ref, theirs_ref = inputs
    x_ref, p_ref, rs_ref = outputs
    parts, t, shares, pair_of_p = scratch
    core = lax.rem(n_ref[0], 2)
    parts[pl.ds(2 * core, 2)] = mine_ref[...]
    parts[pl.ds(2 - 2 * core, 2)] = theirs_ref[...]
    rows, rank = p_ref.shape
    height = rows // 4
    p = jnp.concatenate([parts[k, :height] for k in range(4)], axis=0)
    if scaled:
        rs = lax.rsqrt(parts[0, height : height + 8] + NORM_EPS)
        p = p * rs[:1]
    else:
        rs = jnp.ones(rs_ref.shape, F32)
    rs_ref[...] = rs
    p_ref[...] = p
    turned, half = p.T, LANES
    t[: 2 * half] = exact(turned, p[:, :half], NN)
    t[2 * half :] = exact(turned[half:], p[:, half:], NN)
    size = x_ref.shape[1] - rank
    share = t[pl.ds(pl.multiple_of(n_ref[0] * size, size), size), :]
    pt = split(turned)
    blocks = x_ref.shape[0] // CHUNKS
    shares[...] = share
    pair_of_p[0], pair_of_p[1] = pt

    def fill(k):
        r = dot3((pair_of_p[0], pair_of_p[1]), block(k), NN)
        for q in range(blocks):
            x_ref[k * blocks + q, :rank] = r[:, q * LANES : (q + 1) * LANES]
            x_ref[k * blocks + q, rank:] = shares[...]

    each(fill)


def first_products_kernel(
    n_ref, mine_ref, theirs_ref, m_ref, g_ref, x_ref, p_ref, rs_ref, m, g, came, *scratch
):
    wait = fetch(buffer_moves(m_ref, g_ref, m, g), came)

    def block(k):
        wait(k)
        return split(buffer_block(m, g, columns(k, m.shape[1] // CHUNKS)))

    store_products(
        (n_ref, mine_ref, theirs_ref), (x_ref, p_ref, rs_ref), scratch, block, False
    )


def pair_moves(b_ref, b):
    width = b.shape[2] // CHUNKS

    def moves(k):
        c = columns(k, width)
        return [(b_ref.at[:, :, c], b.at[:, :, c])]

    return moves


def second_products_kernel(
    n_ref, mine_ref, theirs_ref, b_ref, x_ref, p_ref, rs_ref, b, came, *scratch
):
    wait = fetch(pair_moves(b_ref, b), came)

    def block(k):
        wait(k)
        c = columns(k, b.shape[2] // CHUNKS)
        return b[0, :, c], b[1, :, c]

    store_products(
        (n_ref, mine_ref, theirs_ref), (x_ref, p_ref, rs_ref), scratch, block, True
    )


def products(kernel, place, mine, theirs, bigs, held, peers):
    rows, cols = bigs[0].shape[-2:]
    _, height, rank = mine.shape
    tail = 3 * LANES // peers
    shape = (cols // LANES, rank + tail, LANES)
    return call(
        kernel,
        [SM, VM, VM] + [ANY] * len(bigs),
        [
            jax.ShapeDtypeStruct(shape, F32),
            jax.ShapeDtypeStruct((rows, rank), F32),
            jax.ShapeDtypeStruct((8, rank), F32),
        ],
        [VM, VM, VM],
        held
        + [
            dma(CHUNKS, len(bigs)),
            pltpu.VMEM((4, height, rank), F32),
            pltpu.VMEM((3 * LANES, LANES), F32),
            pltpu.VMEM((tail, LANES), F32),
            pltpu.VMEM((2, rank, rows), BF16),
        ],
        6 * rows * cols * rank,
    )(place, mine, theirs, *in_hbm(*bigs))


def spread_kernel(x_ref, y_ref, t_ref, y, sems):
    count = x_ref.shape[0]
    rank = y.shape[0]
    total = x_ref[0]
    for k in range(1, count):
        total = total + x_ref[k]
    y[...] = total[:rank]
    copies = [
        pltpu.make_async_copy(y, y_ref.at[k], sems.at[k]) for k in range(count)
    ]
    for copy in copies:
        copy.start()
    t_ref[...] = total[rank:]
    for copy in copies:
        copy.wait()


def spread_sum(x, rank):
    count, height, width = x.shape
    return call(
        spread_kernel,
        [VM],
        [
            pltpu.HBM((count, rank, width), F32),
            jax.ShapeDtypeStruct((height - rank, width), F32),
        ],
        [ANY, VM],
        [pltpu.VMEM((rank, width), F32), pltpu.SemaphoreType.DMA((count,))],
        count * height * width,
    )(x)


def eliminated(m):
    n = m.shape[0]
    eye = same(n)
    across = lax.rsqrt(jnp.sum(jnp.where(eye, m, 0.0), axis=0, keepdims=True))
    down = lax.rsqrt(jnp.sum(jnp.where(eye, m, 0.0), axis=1, keepdims=True))
    m = m * down * across
    lane = lax.broadcasted_iota(jnp.int32, (8, n), 1)
    sub = lax.broadcasted_iota(jnp.int32, (8, n), 0)
    tiles = [m[8 * t : 8 * t + 8] for t in range(n // 8)]
    for j in range(0, n, 2):
        t, r = divmod(j, 8)
        first, second = lane[:1] == j, lane[:1] == j + 1
        both = (lane >= j) & (lane < j + 2)
        c0 = [jnp.broadcast_to(x[:, j : j + 1], (8, n)) for x in tiles[t:]]
        c1 = [jnp.broadcast_to(x[:, j + 1 : j + 2], (8, n)) for x in tiles[t:]]
        row0, row1 = tiles[t][r : r + 1], tiles[t][r + 1 : r + 2]
        a, b = c0[0][r : r + 1], c0[0][r + 1 : r + 2]
        d = c1[0][r + 1 : r + 2]
        inv_a = 1.0 / a
        inv_d = a * (1.0 / (a * d - b * b))
        ratio = b * inv_a
        low = row1 - ratio * row0
        use1 = jnp.where(first, -ratio, jnp.where(second, 1.0, low)) * inv_d
        use0 = jnp.where(first, 1.0, jnp.where(second, 0.0, row0)) * inv_a - ratio * use1
        kept = jnp.where(first, -ratio, low)
        for s in range(t, n // 8):
            new = jnp.where(both, 0.0, tiles[s]) - c0[s - t] * use0 - c1[s - t] * use1
            if s == t:
                new = jnp.where(sub > r + 1, new, jnp.where(sub == r + 1, kept, tiles[s]))
            tiles[s] = new
    m = jnp.concatenate(tiles, axis=0)
    i = lax.broadcasted_iota(jnp.int32, (n, n), 0)
    j = lax.broadcasted_iota(jnp.int32, (n, n), 1)
    pivots = jnp.sum(jnp.where(eye, m, 0.0), axis=1, keepdims=True)
    unit = jnp.where(i > j, m, jnp.where(eye, 1.0, 0.0))
    return unit * lax.rsqrt(pivots) * across


def cholesky_kernel(n_ref, p_ref, *refs):
    pieces, (w_ref, o_ref, a, low) = refs[:-4], refs[-4:]
    size = pieces[0].shape[0]
    count = len(pieces)
    for k, piece in enumerate(pieces):
        place = lax.rem(n_ref[0] // 2 + k, count)
        a[pl.ds(pl.multiple_of(place * size, size), size), :] = piece[...]
    half = LANES

    def body(b, carry):
        w = eliminated(a[pl.ds(pl.multiple_of(2 * b * half, half), half), :])
        first = pl.multiple_of(b * half, half)
        w_ref[pl.ds(first, half), pl.ds(first, half)] = w

        @pl.when(b == 0)
        def _():
            low[...] = exact(a[half : 2 * half], w, NT)
            a[2 * half :] -= exact(low[...], low[...], NT)

        return carry

    lax.fori_loop(0, 2, body, 0)
    w_ref[:half, half:] = jnp.zeros((half, half), F32)
    w_ref[half:, :half] = -exact(
        w_ref[half:, half:], exact(low[...], w_ref[:half, :half], NN), NN
    )
    o_ref[...] = exact(p_ref[...], w_ref[...], NT)


def inverse_factor(pieces, place, p):
    rank = p.shape[1]
    return call(
        cholesky_kernel,
        [SM, VM] + [VM] * len(pieces),
        [jax.ShapeDtypeStruct((rank, rank), F32), jax.ShapeDtypeStruct(p.shape, F32)],
        [VM, VM],
        [pltpu.VMEM((3 * LANES, LANES), F32), pltpu.VMEM((LANES, LANES), F32)],
        10**10,
    )(place, p, *pieces)


def middle_kernel(o_ref, w_ref, x_ref, m_ref, g_ref, q_ref, rt_ref, m, g, q_sum, s_ref, sems):
    wait = fetch(buffer_moves(m_ref, g_ref, m, g), sems)

    def turn(k):
        c = columns(k, LANES)
        rt_ref[0, :, c], rt_ref[1, :, c] = split(x_ref[k])

    each(turn, x_ref.shape[0])
    rt = (rt_ref[0], rt_ref[1])
    w = w_ref[...]
    s_ref[...] = exact(exact(w, dot3(rt, rt, NT), NN), w, NT)
    width = m.shape[1] // CHUNKS
    q_sum[...] = jnp.zeros_like(q_sum)

    def block(k):
        c = columns(k, width)
        wait(k)
        q_sum[...] += dot3(
            split(buffer_block(m, g, c)), (rt_ref[0, :, c], rt_ref[1, :, c]), NT
        )

    each(block)
    s = s_ref[...]
    q = dot3(split(q_sum[...]), split(w_ref[...]), NT) - dot3(
        split((1.0 - KEEP_RATE) * o_ref[...]), split(s), NN
    )
    n = s.shape[0]
    squares = jnp.sum(jnp.where(same(n), s, 0.0), axis=0, keepdims=True)
    height = q_ref.shape[1] - 8
    for k in range(q_ref.shape[0]):
        q_ref[k, :height] = q[k * height : (k + 1) * height]
        q_ref[k, height:] = jnp.broadcast_to(squares, (8, n))


def middle(o, w, x, momentum, grads):
    rows, cols = momentum.shape
    rank = o.shape[1]
    return call(
        middle_kernel,
        [VM] * 3 + [ANY] * 2,
        [jax.ShapeDtypeStruct((4, rows // 4 + 8, rank), F32), pair((rank, cols))],
        [VM] * 2,
        [
            pltpu.VMEM((rows, cols), F32),
            pltpu.VMEM(grads.shape, BF16),
            pltpu.VMEM((rows, rank), F32),
            pltpu.VMEM((rank, rank), F32),
            dma(CHUNKS, 3),
        ],
        10 * rows * cols * rank,
    )(o, w, x, *in_hbm(momentum, grads))


def update_kernel(half, o_ref, w_ref, rt_ref, m_ref, g_ref, *refs):
    raw_ref, b_ref, m, g, raw, b, came, sent = refs[-8:]
    count = CHUNKS // 2
    width = m.shape[1] // count
    base = half * m.shape[1]

    def placed(k):
        if isinstance(k, int):
            return pl.ds(base + k * width, width)
        return pl.ds(pl.multiple_of(base + k * width, width), width)

    def moves(k):
        c, there = columns(k, width), placed(k)
        return [
            (m_ref.at[:, there], m.at[:, c]),
            (g_ref.at[0, :, there], g.at[0, :, c]),
            (g_ref.at[1, :, there], g.at[1, :, c]),
        ]

    wait = fetch(moves, came, count)
    start, finish = send(
        lambda k: [
            (raw.at[:, :, columns(k, width)], raw_ref.at[:, :, placed(k)]),
            (b.at[:, :, columns(k, width)], b_ref.at[:, :, placed(k)]),
        ],
        sent,
        count,
    )
    o = split((1.0 - KEEP_RATE) * o_ref[...])
    w = split(w_ref[...])

    def block(k):
        c, there = columns(k, width), placed(k)
        now = split(dot3(w, (rt_ref[0, :, there], rt_ref[1, :, there]), NN))
        raw[0, :, c], raw[1, :, c] = now
        wait(k)
        b[0, :, c], b[1, :, c] = split(buffer_block(m, g, c) - dot3(o, now, NN))
        start(k)

    each(block, count)
    finish()


def second_buffer(half, o, w, rt, momentum, grads, begun):
    rows, cols = momentum.shape
    rank = o.shape[1]
    part = cols // 2
    return call(
        functools.partial(update_kernel, half),
        [VM] * 3 + [ANY] * (2 + len(begun)),
        [pair_in_hbm((rank, cols)), pair_in_hbm((rows, cols))],
        [ANY] * 2,
        [
            pltpu.VMEM((rows, part), F32),
            pltpu.VMEM((2, rows, part), BF16),
            pltpu.VMEM((2, rank, part), BF16),
            pltpu.VMEM((2, rows, part), BF16),
            dma(CHUNKS // 2, 3),
            dma(CHUNKS // 2, 2),
        ],
        5 * rows * cols * rank,
        {5: 0, 6: 1} if begun else None,
    )(o, w, rt, *in_hbm(momentum, grads), *in_hbm(*begun))


def write_out(value, out_ref, buffer, sems):
    width = buffer.shape[1] // CHUNKS
    start, finish = send(
        lambda k: [(buffer.at[:, columns(k, width)], out_ref.at[:, columns(k, width)])], sems
    )

    def block(k):
        c = columns(k, width)
        buffer[:, c] = value(k, c).astype(buffer.dtype)
        start(k)

    each(block)
    finish()


def last_raw_kernel(
    o_ref, w_ref, x_ref, b_ref, raw_ref, sq_ref, s_ref, x, b, buffer, total, came, sent
):
    blocks = x_ref.shape[0] // CHUNKS
    bring = pair_moves(b_ref, b)
    wait = fetch(
        lambda k: [(x_ref.at[columns(k, blocks)], x.at[columns(k, blocks)])] + bring(k),
        came,
    )
    total[...] = jnp.zeros_like(total)
    o = split((1.0 - KEEP_RATE) * o_ref[...])
    w = split(w_ref[...])

    def value(k, c):
        wait(k)
        part = jnp.concatenate([x[k * blocks + q] for q in range(blocks)], axis=1)
        raw = dot3(w, split(part), NN)
        now = split(raw)
        raw_ref[0, :, c], raw_ref[1, :, c] = now
        total[...] += jnp.sum(raw * raw, axis=1, keepdims=True)
        return b[0, :, c].astype(F32) + b[1, :, c].astype(F32) - dot3(o, now, NN)

    write_out(value, s_ref, buffer, sent)
    n = w_ref.shape[0]
    squares = jnp.where(same(n), jnp.broadcast_to(total[:, :1], (n, n)), 0.0)
    row = jnp.sum(squares, axis=0, keepdims=True)
    for k in range(sq_ref.shape[0]):
        sq_ref[k] = jnp.broadcast_to(row, (8, n))


def last_raw(o, w, x, b, peers):
    _, rows, cols = b.shape
    rank = w.shape[0]
    return call(
        last_raw_kernel,
        [VM, VM, ANY, ANY],
        [
            pair((rank, cols)),
            jax.ShapeDtypeStruct((peers, 8, rank), F32),
            pltpu.HBM((rows, cols), F32),
        ],
        [VM, VM, ANY],
        [
            pltpu.VMEM(x.shape, F32),
            pltpu.VMEM(b.shape, BF16),
            pltpu.VMEM((rows, cols), F32),
            pltpu.VMEM((rank, LANES), F32),
            dma(CHUNKS, 2),
            dma(CHUNKS, 1),
        ],
        9 * rows * cols * rank,
    )(o, w, *in_hbm(x), *in_hbm(b))


def change_kernel(
    factor, o1_ref, rs_ref, raw1_ref, o_ref, sq_ref, raw_ref, out_ref, raw1, buffer, came, sent
):
    wait = fetch(pair_moves(raw1_ref, raw1), came)
    total = sq_ref[0, :1]
    for k in range(1, sq_ref.shape[0]):
        total = total + sq_ref[k, :1]
    o = split(o_ref[...] * (factor * lax.rsqrt(total + NORM_EPS)))
    o1 = split(o1_ref[...] * (factor * rs_ref[:1]))

    def value(k, c):
        wait(k)
        return dot3(o1, (raw1[0, :, c], raw1[1, :, c]), NN) + dot3(
            o, (raw_ref[0, :, c], raw_ref[1, :, c]), NN
        )

    write_out(value, out_ref, buffer, sent)


def both_changes(factor, o1, rs, raw1, o, sq, raw):
    rows, rank = o.shape
    cols = raw.shape[2]
    return call(
        functools.partial(change_kernel, factor),
        [VM, VM, ANY, VM, VM, VM],
        pltpu.HBM((rows, cols), BF16),
        ANY,
        [
            pltpu.VMEM(raw1.shape, BF16),
            pltpu.VMEM((rows, cols), BF16),
            dma(CHUNKS, 1),
            dma(CHUNKS, 1),
        ],
        12 * rows * cols * rank,
    )(o1, rs, *in_hbm(raw1), o, sq, raw)


SIDE = 4


def chip_permute(x, move):
    pairs = [(2 * k + c, 2 * move(k) + c) for k in range(SIDE) for c in range(2)]
    return lax.ppermute(x, "col", pairs)


def core_permute(x):
    return lax.ppermute(x, "col", [(k, k ^ 1) for k in range(2 * SIDE)])


def near(k):
    return k ^ 1


def far(k):
    return SIDE - 1 - k


def col_sum(parts, beside):
    core = lax.axis_index("col") % 2
    mine = lax.dynamic_slice_in_dim(parts, 2 * core, 2, 0)
    theirs = lax.dynamic_slice_in_dim(parts, 2 - 2 * core, 2, 0)
    mine = mine + core_permute(theirs)
    a, b, done = mine[0], mine[1], []
    for half, moves in enumerate(((near, far), (far, near))):
        from_a, from_b, done = lax.optimization_barrier(
            (chip_permute(a, moves[0]), chip_permute(b, moves[1]), beside(half, done))
        )
        a, b = a + from_a, b + from_b
    mine = jnp.stack([a, b])
    return mine, core_permute(mine), done


def by_chip(part):
    core = lax.axis_index("col") % 2
    other = core_permute(part)
    chip = jnp.where(
        core == 0, jnp.concatenate([part, other]), jnp.concatenate([other, part])
    )
    return [chip] + [
        chip_permute(chip, lambda k, d=d: (k - d) % SIDE) for d in range(1, SIDE)
    ]


def exchange(x, axis):
    return lax.all_to_all(x, axis, 0, 0, tiled=True)


def row_total(blocks, p, place):
    own, part = spread_sum(exchange(blocks, "row"), p.shape[1])
    total = exchange(own, "row")
    return total, *inverse_factor(by_chip(part), place, p)


def shards(momentum, grads, basis):
    rows, cols = momentum.shape
    rank = basis.shape[1]
    peers = lax.axis_size("col")
    factor = (rows * lax.axis_size("row") * cols * peers / rank) ** 0.5
    place = lax.axis_index("col").astype(jnp.int32)[None]

    held = [pltpu.VMEM((rows, cols), F32), pltpu.VMEM((1, rows, cols), BF16)]
    part = first_projection(momentum, grads, basis)
    mine, theirs, _ = col_sum(part.reshape(4, rows // 4, rank), lambda half, done: [])
    x1, p1, _ = products(
        first_products_kernel, place, mine, theirs, [momentum, grads], held, peers
    )
    x1, w1, o1 = row_total(x1, p1, place)
    part, rt1 = middle(o1, w1, x1, momentum, grads)
    mine, theirs, (raw1, buffer) = col_sum(
        part,
        lambda half, done: second_buffer(half, o1, w1, rt1, momentum, grads, done),
    )
    held = [pltpu.VMEM((2, rows, cols), BF16)]
    x2, p2, rs1 = products(
        second_products_kernel, place, mine, theirs, [buffer], held, peers
    )
    x2, w2, o2 = row_total(x2, p2, place)
    raw2, sq2, state = last_raw(o2, w2, x2, buffer, peers)
    sq2 = exchange(sq2, "col")
    change = both_changes(factor, o1, rs1, raw1, o2, sq2, raw2)
    return change, state


def solution(mesh):
    return jax.shard_map(
        shards,
        mesh=mesh,
        in_specs=(P("row", "col"), P(None, "row", "col"), P("col", None)),
        out_specs=(P("row", "col"), P("row", "col")),
        check_vma=False,
    )
```

```python
import functools

import jax
import jax.numpy as jnp
from jax import lax
from jax.experimental import pallas as pl
from jax.experimental.pallas import tpu as pltpu
from jax.sharding import PartitionSpec as P

KEEP_RATE = 0.95
NORM_EPS = 1e-06
LANES = 128
CHUNKS = 4
F32 = jnp.float32
BF16 = jnp.bfloat16
VMEM_LIMIT = 20 * 1024 * 1024
NN = (((1,), (0,)), ((), ()))
NT = (((1,), (1,)), ((), ()))


def split(x):
    high = x.astype(BF16)
    return high, (x - high.astype(F32)).astype(BF16)


def mm(a, b, dims):
    return lax.dot_general(a, b, dims, preferred_element_type=F32)


def dot3(a, b, dims):
    return mm(a[0], b[0], dims) + (mm(a[0], b[1], dims) + mm(a[1], b[0], dims))


def exact(a, b, dims):
    return lax.dot_general(
        a, b, dims, precision=lax.Precision.HIGHEST, preferred_element_type=F32
    )


def call(kernel, in_specs, out_shape, out_specs, scratch, cost, aliases=None):
    return pl.pallas_call(
        kernel,
        in_specs=in_specs,
        out_specs=out_specs,
        out_shape=out_shape,
        scratch_shapes=scratch,
        input_output_aliases=aliases or {},
        compiler_params=pltpu.CompilerParams(vmem_limit_bytes=VMEM_LIMIT),
        cost_estimate=pl.CostEstimate(
            flops=cost, transcendentals=0, bytes_accessed=8 * 1024 * 1024
        ),
    )


VM = pl.BlockSpec(memory_space=pltpu.VMEM)
SM = pl.BlockSpec(memory_space=pltpu.SMEM)
ANY = pl.BlockSpec(memory_space=pl.ANY)


def in_hbm(*arrays):
    return [pltpu.with_memory_space_constraint(a, pltpu.HBM) for a in arrays]


def pair(shape):
    return jax.ShapeDtypeStruct((2, *shape), BF16)


def pair_in_hbm(shape):
    return pltpu.HBM((2, *shape), BF16)


def dma(*shape):
    return pltpu.SemaphoreType.DMA(shape)


def fetch(moves, sems, count=CHUNKS):
    def copies(k):
        return [
            pltpu.make_async_copy(a, b, sems.at[k, n]) for n, (a, b) in enumerate(moves(k))
        ]

    for k in range(count):
        for copy in copies(k):
            copy.start()

    def wait(k):
        for copy in copies(k):
            copy.wait()

    return wait


def send(moves, sems, count=CHUNKS):
    def copies(k):
        return [
            pltpu.make_async_copy(a, b, sems.at[k, n]) for n, (a, b) in enumerate(moves(k))
        ]

    def start(k):
        for copy in copies(k):
            copy.start()

    def finish():
        for k in range(count):
            for copy in copies(k):
                copy.wait()

    return start, finish


def columns(k, width):
    if isinstance(k, int):
        return pl.ds(k * width, width)
    return pl.ds(pl.multiple_of(k * width, width), width)


def each(block, count=CHUNKS):
    lax.fori_loop(0, count, lambda k, _: (block(k), 0)[1], 0)


def same(n):
    i = lax.broadcasted_iota(jnp.int32, (n, n), 0)
    return i == lax.broadcasted_iota(jnp.int32, (n, n), 1)


def buffer_moves(m_ref, g_ref, m, g):
    width = m.shape[1] // CHUNKS

    def moves(k):
        c = columns(k, width)
        pairs = [(m_ref.at[:, c], m.at[:, c])]
        for n in range(g.shape[0]):
            pairs.append((g_ref.at[n, :, c], g.at[n, :, c]))
        return pairs

    return moves


def buffer_block(m, g, c):
    b = m[:, c]
    for n in range(g.shape[0]):
        b = b + g[n, :, c].astype(F32)
    return b


def first_kernel(m_ref, g_ref, v_ref, p_ref, m, g, v, sems):
    width = m.shape[1] // CHUNKS
    moves = buffer_moves(m_ref, g_ref, m, g)
    wait = fetch(
        lambda k: moves(k) + [(v_ref.at[columns(k, width)], v.at[columns(k, width)])], sems
    )
    p_ref[...] = jnp.zeros_like(p_ref)

    def block(k):
        c = columns(k, width)
        wait(k)
        p_ref[...] += dot3(split(buffer_block(m, g, c)), split(v[c]), NN)

    each(block)


def first_projection(momentum, grads, basis):
    rows, cols = momentum.shape
    rank = basis.shape[1]
    return call(
        first_kernel,
        [ANY] * 3,
        jax.ShapeDtypeStruct((rows, rank), F32),
        VM,
        [
            pltpu.VMEM((rows, cols), F32),
            pltpu.VMEM((1, rows, cols), BF16),
            pltpu.VMEM((cols, rank), F32),
            dma(CHUNKS, 3),
        ],
        6 * rows * cols * rank,
    )(*in_hbm(momentum, grads, basis))


def store_products(inputs, outputs, scratch, block, scaled):
    n_ref, mine_ref, theirs_ref = inputs
    x_ref, p_ref, rs_ref = outputs
    parts, t, shares, pair_of_p = scratch
    core = lax.rem(n_ref[0], 2)
    parts[pl.ds(2 * core, 2)] = mine_ref[...]
    parts[pl.ds(2 - 2 * core, 2)] = theirs_ref[...]
    rows, rank = p_ref.shape
    height = rows // 4
    p = jnp.concatenate([parts[k, :height] for k in range(4)], axis=0)
    if scaled:
        rs = lax.rsqrt(parts[0, height : height + 8] + NORM_EPS)
        p = p * rs[:1]
    else:
        rs = jnp.ones(rs_ref.shape, F32)
    rs_ref[...] = rs
    p_ref[...] = p
    turned, half = p.T, LANES
    t[: 2 * half] = exact(turned, p[:, :half], NN)
    t[2 * half :] = exact(turned[half:], p[:, half:], NN)
    size = x_ref.shape[1] - rank
    share = t[pl.ds(pl.multiple_of(n_ref[0] * size, size), size), :]
    pt = split(turned)
    blocks = x_ref.shape[0] // CHUNKS
    shares[...] = share
    pair_of_p[0], pair_of_p[1] = pt

    def fill(k):
        r = dot3((pair_of_p[0], pair_of_p[1]), block(k), NN)
        for q in range(blocks):
            x_ref[k * blocks + q, :rank] = r[:, q * LANES : (q + 1) * LANES]
            x_ref[k * blocks + q, rank:] = shares[...]

    each(fill)


def first_products_kernel(
    n_ref, mine_ref, theirs_ref, m_ref, g_ref, x_ref, p_ref, rs_ref, m, g, came, *scratch
):
    wait = fetch(buffer_moves(m_ref, g_ref, m, g), came)

    def block(k):
        wait(k)
        return split(buffer_block(m, g, columns(k, m.shape[1] // CHUNKS)))

    store_products(
        (n_ref, mine_ref, theirs_ref), (x_ref, p_ref, rs_ref), scratch, block, False
    )


def pair_moves(b_ref, b):
    width = b.shape[2] // CHUNKS

    def moves(k):
        c = columns(k, width)
        return [(b_ref.at[:, :, c], b.at[:, :, c])]

    return moves


def second_products_kernel(
    n_ref, mine_ref, theirs_ref, b_ref, x_ref, p_ref, rs_ref, b, came, *scratch
):
    wait = fetch(pair_moves(b_ref, b), came)

    def block(k):
        wait(k)
        c = columns(k, b.shape[2] // CHUNKS)
        return b[0, :, c], b[1, :, c]

    store_products(
        (n_ref, mine_ref, theirs_ref), (x_ref, p_ref, rs_ref), scratch, block, True
    )


def products(kernel, place, mine, theirs, bigs, held, peers):
    rows, cols = bigs[0].shape[-2:]
    _, height, rank = mine.shape
    tail = 3 * LANES // peers
    shape = (cols // LANES, rank + tail, LANES)
    return call(
        kernel,
        [SM, VM, VM] + [ANY] * len(bigs),
        [
            jax.ShapeDtypeStruct(shape, F32),
            jax.ShapeDtypeStruct((rows, rank), F32),
            jax.ShapeDtypeStruct((8, rank), F32),
        ],
        [VM, VM, VM],
        held
        + [
            dma(CHUNKS, len(bigs)),
            pltpu.VMEM((4, height, rank), F32),
            pltpu.VMEM((3 * LANES, LANES), F32),
            pltpu.VMEM((tail, LANES), F32),
            pltpu.VMEM((2, rank, rows), BF16),
        ],
        6 * rows * cols * rank,
    )(place, mine, theirs, *in_hbm(*bigs))


def spread_kernel(x_ref, y_ref, t_ref, y, sems):
    count = x_ref.shape[0]
    rank = y.shape[0]
    total = x_ref[0]
    for k in range(1, count):
        total = total + x_ref[k]
    y[...] = total[:rank]
    copies = [
        pltpu.make_async_copy(y, y_ref.at[k], sems.at[k]) for k in range(count)
    ]
    for copy in copies:
        copy.start()
    t_ref[...] = total[rank:]
    for copy in copies:
        copy.wait()


def spread_sum(x, rank):
    count, height, width = x.shape
    return call(
        spread_kernel,
        [VM],
        [
            pltpu.HBM((count, rank, width), F32),
            jax.ShapeDtypeStruct((height - rank, width), F32),
        ],
        [ANY, VM],
        [pltpu.VMEM((rank, width), F32), pltpu.SemaphoreType.DMA((count,))],
        count * height * width,
    )(x)


def two_columns(a, b, d, row0, row1, first, second):
    inv = 1.0 / (a * d - b * b)
    i00, i01, i11 = d * inv, -b * inv, a * inv
    e0 = jnp.where(first, 1.0, jnp.where(second, 0.0, row0))
    e1 = jnp.where(first, 0.0, jnp.where(second, 1.0, row1))
    ratio = b / a
    kept = jnp.where(first, -ratio, row1 - ratio * row0)
    return (i00, i01, i11), i00 * e0 + i01 * e1, i01 * e0 + i11 * e1, kept


def eliminated(m):
    n = m.shape[0]
    eye = same(n)
    across = lax.rsqrt(jnp.sum(jnp.where(eye, m, 0.0), axis=0, keepdims=True))
    down = lax.rsqrt(jnp.sum(jnp.where(eye, m, 0.0), axis=1, keepdims=True))
    m = m * down * across
    lane = lax.broadcasted_iota(jnp.int32, (8, n), 1)
    sub = lax.broadcasted_iota(jnp.int32, (8, n), 0)
    tiles = [m[8 * t : 8 * t + 8] for t in range(n // 8)]
    for j in range(0, n, 4):
        t, r = divmod(j, 8)
        here = [lane[:1] == j + k for k in range(4)]
        left, right = here[0] | here[1], here[2] | here[3]
        all_four = (lane >= j) & (lane < j + 4)
        c = [
            [jnp.broadcast_to(x[:, j + k : j + k + 1], (8, n)) for x in tiles[t:]]
            for k in range(4)
        ]
        rows = [tiles[t][r + k : r + k + 1] for k in range(4)]

        def at(k, l):
            return c[l][0][r + k : r + k + 1]

        (i00, i01, i11), use0, use1, kept1 = two_columns(
            at(0, 0), at(1, 0), at(1, 1), rows[0], rows[1], here[0], here[1]
        )
        f2, g2 = i00 * at(2, 0) + i01 * at(2, 1), i01 * at(2, 0) + i11 * at(2, 1)
        f3, g3 = i00 * at(3, 0) + i01 * at(3, 1), i01 * at(3, 0) + i11 * at(3, 1)
        row2 = jnp.where(left, 0.0, rows[2]) - at(2, 0) * use0 - at(2, 1) * use1
        row3 = jnp.where(left, 0.0, rows[3]) - at(3, 0) * use0 - at(3, 1) * use1
        _, use2, use3, kept3 = two_columns(
            at(2, 2) - at(2, 0) * f2 - at(2, 1) * g2,
            at(3, 2) - at(3, 0) * f2 - at(3, 1) * g2,
            at(3, 3) - at(3, 0) * f3 - at(3, 1) * g3,
            row2,
            row3,
            here[2],
            here[3],
        )
        use0, use1 = jnp.where(right, 0.0, use0), jnp.where(right, 0.0, use1)
        for s in range(t, n // 8):
            c0, c1, c2, c3 = (c[k][s - t] for k in range(4))
            c2 = c2 - c0 * f2 - c1 * g2
            c3 = c3 - c0 * f3 - c1 * g3
            new = jnp.where(all_four, 0.0, tiles[s]) - c0 * use0 - c1 * use1
            new = new - c2 * use2 - c3 * use3
            if s == t:
                own = jnp.where(sub == r + 1, kept1, tiles[s])
                own = jnp.where(sub == r + 2, row2, own)
                own = jnp.where(sub == r + 3, kept3, own)
                new = jnp.where(sub > r + 3, new, own)
            tiles[s] = new
    m = jnp.concatenate(tiles, axis=0)
    i = lax.broadcasted_iota(jnp.int32, (n, n), 0)
    j = lax.broadcasted_iota(jnp.int32, (n, n), 1)
    pivots = jnp.sum(jnp.where(eye, m, 0.0), axis=1, keepdims=True)
    unit = jnp.where(i > j, m, jnp.where(eye, 1.0, 0.0))
    return unit * lax.rsqrt(pivots) * across


def cholesky_kernel(n_ref, p_ref, *refs):
    pieces, (w_ref, o_ref, a, low) = refs[:-4], refs[-4:]
    size = pieces[0].shape[0]
    count = len(pieces)
    for k, piece in enumerate(pieces):
        place = lax.rem(n_ref[0] // 2 + k, count)
        a[pl.ds(pl.multiple_of(place * size, size), size), :] = piece[...]
    half = LANES

    def body(b, carry):
        w = eliminated(a[pl.ds(pl.multiple_of(2 * b * half, half), half), :])
        first = pl.multiple_of(b * half, half)
        w_ref[pl.ds(first, half), pl.ds(first, half)] = w

        @pl.when(b == 0)
        def _():
            low[...] = exact(a[half : 2 * half], w, NT)
            a[2 * half :] -= exact(low[...], low[...], NT)

        return carry

    lax.fori_loop(0, 2, body, 0)
    w_ref[:half, half:] = jnp.zeros((half, half), F32)
    w_ref[half:, :half] = -exact(
        w_ref[half:, half:], exact(low[...], w_ref[:half, :half], NN), NN
    )
    o_ref[...] = exact(p_ref[...], w_ref[...], NT)


def inverse_factor(pieces, place, p):
    rank = p.shape[1]
    return call(
        cholesky_kernel,
        [SM, VM] + [VM] * len(pieces),
        [jax.ShapeDtypeStruct((rank, rank), F32), jax.ShapeDtypeStruct(p.shape, F32)],
        [VM, VM],
        [pltpu.VMEM((3 * LANES, LANES), F32), pltpu.VMEM((LANES, LANES), F32)],
        10**10,
    )(place, p, *pieces)


def ahead_kernel(after_ref, m_ref, g_ref, a_ref, m, g, a, came, sent):
    del after_ref
    width = m.shape[1] // CHUNKS
    wait = fetch(buffer_moves(m_ref, g_ref, m, g), came)
    start, finish = send(
        lambda k: [(a.at[:, :, columns(k, width)], a_ref.at[:, :, columns(k, width)])], sent
    )

    def block(k):
        c = columns(k, width)
        wait(k)
        a[0, :, c], a[1, :, c] = split(buffer_block(m, g, c))
        start(k)

    each(block)
    finish()


def buffer_ahead(after, momentum, grads):
    rows, cols = momentum.shape
    return call(
        ahead_kernel,
        [VM] + [ANY] * 2,
        pair_in_hbm((rows, cols)),
        ANY,
        [
            pltpu.VMEM((rows, cols), F32),
            pltpu.VMEM(grads.shape, BF16),
            pltpu.VMEM((2, rows, cols), BF16),
            dma(CHUNKS, 3),
            dma(CHUNKS, 1),
        ],
        8 * rows * cols,
    )(after, *in_hbm(momentum, grads))


def middle_kernel(o_ref, w_ref, x_ref, a_ref, q_ref, rt_ref, a, q_sum, s_ref, sems):
    wait = fetch(pair_moves(a_ref, a), sems)

    def turn(k):
        c = columns(k, LANES)
        rt_ref[0, :, c], rt_ref[1, :, c] = split(x_ref[k])

    each(turn, x_ref.shape[0])
    rt = (rt_ref[0], rt_ref[1])
    w = w_ref[...]
    s_ref[...] = exact(exact(w, dot3(rt, rt, NT), NN), w, NT)
    width = a.shape[2] // CHUNKS
    q_sum[...] = jnp.zeros_like(q_sum)

    def block(k):
        c = columns(k, width)
        wait(k)
        q_sum[...] += dot3(
            (a[0, :, c], a[1, :, c]), (rt_ref[0, :, c], rt_ref[1, :, c]), NT
        )

    each(block)
    s = s_ref[...]
    q = dot3(split(q_sum[...]), split(w_ref[...]), NT) - dot3(
        split((1.0 - KEEP_RATE) * o_ref[...]), split(s), NN
    )
    n = s.shape[0]
    squares = jnp.sum(jnp.where(same(n), s, 0.0), axis=0, keepdims=True)
    height = q_ref.shape[1] - 8
    for k in range(q_ref.shape[0]):
        q_ref[k, :height] = q[k * height : (k + 1) * height]
        q_ref[k, height:] = jnp.broadcast_to(squares, (8, n))


def middle(o, w, x, ahead):
    _, rows, cols = ahead.shape
    rank = o.shape[1]
    return call(
        middle_kernel,
        [VM] * 3 + [ANY],
        [jax.ShapeDtypeStruct((4, rows // 4 + 8, rank), F32), pair((rank, cols))],
        [VM] * 2,
        [
            pltpu.VMEM((2, rows, cols), BF16),
            pltpu.VMEM((rows, rank), F32),
            pltpu.VMEM((rank, rank), F32),
            dma(CHUNKS, 1),
        ],
        10 * rows * cols * rank,
    )(o, w, x, *in_hbm(ahead))


def update_kernel(half, o_ref, w_ref, rt_ref, a_ref, *refs):
    raw_ref, b_ref, a, raw, b, came, sent = refs[-7:]
    count = CHUNKS // 2
    width = a.shape[2] // count
    base = half * a.shape[2]

    def placed(k):
        if isinstance(k, int):
            return pl.ds(base + k * width, width)
        return pl.ds(pl.multiple_of(base + k * width, width), width)

    def moves(k):
        return [(a_ref.at[:, :, placed(k)], a.at[:, :, columns(k, width)])]

    wait = fetch(moves, came, count)
    start, finish = send(
        lambda k: [
            (raw.at[:, :, columns(k, width)], raw_ref.at[:, :, placed(k)]),
            (b.at[:, :, columns(k, width)], b_ref.at[:, :, placed(k)]),
        ],
        sent,
        count,
    )
    o = split((1.0 - KEEP_RATE) * o_ref[...])
    w = split(w_ref[...])

    def block(k):
        c, there = columns(k, width), placed(k)
        now = split(dot3(w, (rt_ref[0, :, there], rt_ref[1, :, there]), NN))
        raw[0, :, c], raw[1, :, c] = now
        wait(k)
        b[0, :, c], b[1, :, c] = split(
            a[0, :, c].astype(F32) + a[1, :, c].astype(F32) - dot3(o, now, NN)
        )
        start(k)

    each(block, count)
    finish()


def second_buffer(half, o, w, rt, ahead, begun):
    _, rows, cols = ahead.shape
    rank = o.shape[1]
    part = cols // 2
    return call(
        functools.partial(update_kernel, half),
        [VM] * 3 + [ANY] * (1 + len(begun)),
        [pair_in_hbm((rank, cols)), pair_in_hbm((rows, cols))],
        [ANY] * 2,
        [
            pltpu.VMEM((2, rows, part), BF16),
            pltpu.VMEM((2, rank, part), BF16),
            pltpu.VMEM((2, rows, part), BF16),
            dma(CHUNKS // 2, 1),
            dma(CHUNKS // 2, 2),
        ],
        5 * rows * cols * rank,
        {4: 0, 5: 1} if begun else None,
    )(o, w, rt, *in_hbm(ahead), *in_hbm(*begun))


def write_out(value, out_ref, buffer, sems):
    width = buffer.shape[1] // CHUNKS
    start, finish = send(
        lambda k: [(buffer.at[:, columns(k, width)], out_ref.at[:, columns(k, width)])], sems
    )

    def block(k):
        c = columns(k, width)
        buffer[:, c] = value(k, c).astype(buffer.dtype)
        start(k)

    each(block)
    finish()


def first_change_kernel(
    factor, after_ref, o_ref, rs_ref, raw_ref, c_ref, raw, buffer, came, sent
):
    del after_ref
    wait = fetch(pair_moves(raw_ref, raw), came)
    o = split(o_ref[...] * (factor * rs_ref[:1]))

    def value(k, c):
        wait(k)
        return dot3(o, (raw[0, :, c], raw[1, :, c]), NN)

    write_out(value, c_ref, buffer, sent)


def first_change(factor, after, o, rs, raw):
    rows, rank = o.shape
    cols = raw.shape[2]
    return call(
        functools.partial(first_change_kernel, factor),
        [VM, VM, VM, ANY],
        pltpu.HBM((rows, cols), F32),
        ANY,
        [
            pltpu.VMEM(raw.shape, BF16),
            pltpu.VMEM((rows, cols), F32),
            dma(CHUNKS, 1),
            dma(CHUNKS, 1),
        ],
        6 * rows * cols * rank,
    )(after, o, rs, *in_hbm(raw))


def last_raw_kernel(w_ref, x_ref, raw_ref, sq_ref, x, total, came):
    blocks = x_ref.shape[0] // CHUNKS
    wait = fetch(
        lambda k: [(x_ref.at[columns(k, blocks)], x.at[columns(k, blocks)])], came
    )
    total[...] = jnp.zeros_like(total)
    w = split(w_ref[...])

    def block(k):
        c = columns(k, blocks * LANES)
        wait(k)
        part = jnp.concatenate([x[k * blocks + q] for q in range(blocks)], axis=1)
        raw = dot3(w, split(part), NN)
        raw_ref[0, :, c], raw_ref[1, :, c] = split(raw)
        total[...] += jnp.sum(raw * raw, axis=1, keepdims=True)

    each(block)
    n = w_ref.shape[0]
    squares = jnp.where(same(n), jnp.broadcast_to(total[:, :1], (n, n)), 0.0)
    row = jnp.sum(squares, axis=0, keepdims=True)
    for k in range(sq_ref.shape[0]):
        sq_ref[k] = jnp.broadcast_to(row, (8, n))


def last_raw(w, x, peers):
    rank = w.shape[0]
    cols = x.shape[0] * LANES
    return call(
        last_raw_kernel,
        [VM, ANY],
        [pair((rank, cols)), jax.ShapeDtypeStruct((peers, 8, rank), F32)],
        [VM] * 2,
        [
            pltpu.VMEM(x.shape, F32),
            pltpu.VMEM((rank, LANES), F32),
            dma(CHUNKS, 1),
        ],
        6 * rank * cols * rank,
    )(w, *in_hbm(x))


def state_kernel(o_ref, raw_ref, b_ref, s_ref, b, buffer, came, sent):
    wait = fetch(pair_moves(b_ref, b), came)
    o = split((1.0 - KEEP_RATE) * o_ref[...])

    def value(k, c):
        wait(k)
        b_now = b[0, :, c].astype(F32) + b[1, :, c].astype(F32)
        return b_now - dot3(o, (raw_ref[0, :, c], raw_ref[1, :, c]), NN)

    write_out(value, s_ref, buffer, sent)


def last_state(o, raw, b):
    _, rows, cols = b.shape
    return call(
        state_kernel,
        [VM, VM, ANY],
        pltpu.HBM((rows, cols), F32),
        ANY,
        [
            pltpu.VMEM(b.shape, BF16),
            pltpu.VMEM((rows, cols), F32),
            dma(CHUNKS, 1),
            dma(CHUNKS, 1),
        ],
        6 * rows * cols * o.shape[1],
    )(o, raw, *in_hbm(b))


def last_change_kernel(
    factor, o_ref, sq_ref, raw_ref, c_ref, out_ref, held, buffer, came, sent
):
    width = held.shape[1] // CHUNKS
    wait = fetch(
        lambda k: [(c_ref.at[:, columns(k, width)], held.at[:, columns(k, width)])], came
    )
    total = sq_ref[0, :1]
    for k in range(1, sq_ref.shape[0]):
        total = total + sq_ref[k, :1]
    o = split(o_ref[...] * (factor * lax.rsqrt(total + NORM_EPS)))

    def value(k, c):
        wait(k)
        return held[:, c] + dot3(o, (raw_ref[0, :, c], raw_ref[1, :, c]), NN)

    write_out(value, out_ref, buffer, sent)


def last_change(factor, o, sq, raw, change):
    rows, cols = change.shape
    return call(
        functools.partial(last_change_kernel, factor),
        [VM, VM, VM, ANY],
        pltpu.HBM((rows, cols), BF16),
        ANY,
        [
            pltpu.VMEM((rows, cols), F32),
            pltpu.VMEM((rows, cols), BF16),
            dma(CHUNKS, 1),
            dma(CHUNKS, 1),
        ],
        6 * rows * cols * o.shape[1],
    )(o, sq, raw, *in_hbm(change))


SIDE = 4


def chip_permute(x, move):
    pairs = [(2 * k + c, 2 * move(k) + c) for k in range(SIDE) for c in range(2)]
    return lax.ppermute(x, "col", pairs)


def core_permute(x):
    return lax.ppermute(x, "col", [(k, k ^ 1) for k in range(2 * SIDE)])


def near(k):
    return k ^ 1


def far(k):
    return SIDE - 1 - k


def col_sum(parts, beside):
    core = lax.axis_index("col") % 2
    mine = lax.dynamic_slice_in_dim(parts, 2 * core, 2, 0)
    theirs = lax.dynamic_slice_in_dim(parts, 2 - 2 * core, 2, 0)
    mine = mine + core_permute(theirs)
    a, b, done = mine[0], mine[1], []
    for half, moves in enumerate(((near, far), (far, near))):
        from_a, from_b, done = lax.optimization_barrier(
            (chip_permute(a, moves[0]), chip_permute(b, moves[1]), beside(half, done))
        )
        a, b = a + from_a, b + from_b
    mine = jnp.stack([a, b])
    return mine, core_permute(mine), done


def by_chip(part):
    core = lax.axis_index("col") % 2
    other = core_permute(part)
    chip = jnp.where(
        core == 0, jnp.concatenate([part, other]), jnp.concatenate([other, part])
    )
    return [chip] + [
        chip_permute(chip, lambda k, d=d: (k - d) % SIDE) for d in range(1, SIDE)
    ]


def exchange(x, axis):
    return lax.all_to_all(x, axis, 0, 0, tiled=True)


def row_total(blocks, p, place, beside):
    own, part = spread_sum(exchange(blocks, "row"), p.shape[1])
    total, extra = lax.optimization_barrier((exchange(own, "row"), beside(part)))
    return total, *inverse_factor(by_chip(part), place, p), extra


def shards(momentum, grads, basis):
    rows, cols = momentum.shape
    rank = basis.shape[1]
    peers = lax.axis_size("col")
    factor = (rows * lax.axis_size("row") * cols * peers / rank) ** 0.5
    place = lax.axis_index("col").astype(jnp.int32)[None]

    held = [pltpu.VMEM((rows, cols), F32), pltpu.VMEM((1, rows, cols), BF16)]
    part = first_projection(momentum, grads, basis)
    mine, theirs, _ = col_sum(part.reshape(4, rows // 4, rank), lambda half, done: [])
    x1, p1, _ = products(
        first_products_kernel, place, mine, theirs, [momentum, grads], held, peers
    )
    x1, w1, o1, ahead = row_total(
        x1, p1, place, lambda part: buffer_ahead(part, momentum, grads)
    )
    part, rt1 = middle(o1, w1, x1, ahead)
    mine, theirs, (raw1, buffer) = col_sum(
        part, lambda half, done: second_buffer(half, o1, w1, rt1, ahead, done)
    )
    held = [pltpu.VMEM((2, rows, cols), BF16)]
    x2, p2, rs1 = products(
        second_products_kernel, place, mine, theirs, [buffer], held, peers
    )
    x2, w2, o2, change1 = row_total(
        x2, p2, place, lambda part: first_change(factor, part, o1, rs1, raw1)
    )
    raw2, sq2 = last_raw(w2, x2, peers)
    sq2, state = lax.optimization_barrier(
        (exchange(sq2, "col"), last_state(o2, raw2, buffer))
    )
    change = last_change(factor, o2, sq2, raw2, change1)
    return change, state


def solution(mesh):
    return jax.shard_map(
        shards,
        mesh=mesh,
        in_specs=(P("row", "col"), P(None, "row", "col"), P("col", None)),
        out_specs=(P("row", "col"), P("row", "col")),
        check_vma=False,
    )
```

```python
import functools

import jax
import jax.numpy as jnp
from jax import lax
from jax.experimental import pallas as pl
from jax.experimental.pallas import tpu as pltpu
from jax.sharding import PartitionSpec as P

KEEP_RATE = 0.95
NORM_EPS = 1e-06
LANES = 128
CHUNKS = 4
F32 = jnp.float32
BF16 = jnp.bfloat16
VMEM_LIMIT = 20 * 1024 * 1024
NN = (((1,), (0,)), ((), ()))
NT = (((1,), (1,)), ((), ()))


def split(x):
    high = x.astype(BF16)
    return high, (x - high.astype(F32)).astype(BF16)


def mm(a, b, dims):
    return lax.dot_general(a, b, dims, preferred_element_type=F32)


def dot3(a, b, dims):
    return mm(a[0], b[0], dims) + (mm(a[0], b[1], dims) + mm(a[1], b[0], dims))


def exact(a, b, dims):
    return lax.dot_general(
        a, b, dims, precision=lax.Precision.HIGHEST, preferred_element_type=F32
    )


def call(kernel, in_specs, out_shape, out_specs, scratch, cost, aliases=None):
    return pl.pallas_call(
        kernel,
        in_specs=in_specs,
        out_specs=out_specs,
        out_shape=out_shape,
        scratch_shapes=scratch,
        input_output_aliases=aliases or {},
        compiler_params=pltpu.CompilerParams(vmem_limit_bytes=VMEM_LIMIT),
        cost_estimate=pl.CostEstimate(
            flops=cost, transcendentals=0, bytes_accessed=8 * 1024 * 1024
        ),
    )


VM = pl.BlockSpec(memory_space=pltpu.VMEM)
SM = pl.BlockSpec(memory_space=pltpu.SMEM)
ANY = pl.BlockSpec(memory_space=pl.ANY)


def in_hbm(*arrays):
    return [pltpu.with_memory_space_constraint(a, pltpu.HBM) for a in arrays]


def pair(shape):
    return jax.ShapeDtypeStruct((2, *shape), BF16)


def pair_in_hbm(shape):
    return pltpu.HBM((2, *shape), BF16)


def dma(*shape):
    return pltpu.SemaphoreType.DMA(shape)


def fetch(moves, sems, count=CHUNKS):
    def copies(k):
        return [
            pltpu.make_async_copy(a, b, sems.at[k, n]) for n, (a, b) in enumerate(moves(k))
        ]

    for k in range(count):
        for copy in copies(k):
            copy.start()

    def wait(k):
        for copy in copies(k):
            copy.wait()

    return wait


def send(moves, sems, count=CHUNKS):
    def copies(k):
        return [
            pltpu.make_async_copy(a, b, sems.at[k, n]) for n, (a, b) in enumerate(moves(k))
        ]

    def start(k):
        for copy in copies(k):
            copy.start()

    def finish():
        for k in range(count):
            for copy in copies(k):
                copy.wait()

    return start, finish


def columns(k, width):
    if isinstance(k, int):
        return pl.ds(k * width, width)
    return pl.ds(pl.multiple_of(k * width, width), width)


def each(block, count=CHUNKS):
    lax.fori_loop(0, count, lambda k, _: (block(k), 0)[1], 0)


def same(n):
    i = lax.broadcasted_iota(jnp.int32, (n, n), 0)
    return i == lax.broadcasted_iota(jnp.int32, (n, n), 1)


def buffer_moves(m_ref, g_ref, m, g):
    width = m.shape[1] // CHUNKS

    def moves(k):
        c = columns(k, width)
        pairs = [(m_ref.at[:, c], m.at[:, c])]
        for n in range(g.shape[0]):
            pairs.append((g_ref.at[n, :, c], g.at[n, :, c]))
        return pairs

    return moves


def buffer_block(m, g, c):
    b = m[:, c]
    for n in range(g.shape[0]):
        b = b + g[n, :, c].astype(F32)
    return b


def first_kernel(m_ref, g_ref, v_ref, p_ref, m, g, v, sems):
    width = m.shape[1] // CHUNKS
    moves = buffer_moves(m_ref, g_ref, m, g)
    wait = fetch(
        lambda k: moves(k) + [(v_ref.at[columns(k, width)], v.at[columns(k, width)])], sems
    )
    p_ref[...] = jnp.zeros_like(p_ref)

    def block(k):
        c = columns(k, width)
        wait(k)
        p_ref[...] += dot3(split(buffer_block(m, g, c)), split(v[c]), NN)

    each(block)


def first_projection(momentum, grads, basis):
    rows, cols = momentum.shape
    rank = basis.shape[1]
    return call(
        first_kernel,
        [ANY] * 3,
        jax.ShapeDtypeStruct((rows, rank), F32),
        VM,
        [
            pltpu.VMEM((rows, cols), F32),
            pltpu.VMEM((1, rows, cols), BF16),
            pltpu.VMEM((cols, rank), F32),
            dma(CHUNKS, 3),
        ],
        6 * rows * cols * rank,
    )(*in_hbm(momentum, grads, basis))


def store_products(inputs, outputs, scratch, block, scaled):
    n_ref, mine_ref, theirs_ref = inputs
    x_ref, p_ref, rs_ref = outputs
    parts, t, shares, pair_of_p = scratch
    core = lax.rem(n_ref[0], 2)
    parts[pl.ds(2 * core, 2)] = mine_ref[...]
    parts[pl.ds(2 - 2 * core, 2)] = theirs_ref[...]
    rows, rank = p_ref.shape
    height = rows // 4
    p = jnp.concatenate([parts[k, :height] for k in range(4)], axis=0)
    if scaled:
        rs = lax.rsqrt(parts[0, height : height + 8] + NORM_EPS)
        p = p * rs[:1]
    else:
        rs = jnp.ones(rs_ref.shape, F32)
    rs_ref[...] = rs
    p_ref[...] = p
    turned, half = p.T, LANES
    gram = exact(turned, p, NN)
    t[: 2 * half] = gram[:, :half]
    t[2 * half :] = gram[half:, half:]
    size = x_ref.shape[1] - rank
    share = t[pl.ds(pl.multiple_of(n_ref[0] * size, size), size), :]
    pt = split(turned)
    blocks = x_ref.shape[0] // CHUNKS
    shares[...] = share
    pair_of_p[0], pair_of_p[1] = pt

    def fill(k):
        r = dot3((pair_of_p[0], pair_of_p[1]), block(k), NN)
        for q in range(blocks):
            x_ref[k * blocks + q, :rank] = r[:, q * LANES : (q + 1) * LANES]
            x_ref[k * blocks + q, rank:] = shares[...]

    each(fill)


def first_products_kernel(
    n_ref, mine_ref, theirs_ref, m_ref, g_ref, x_ref, p_ref, rs_ref, m, g, came, *scratch
):
    wait = fetch(buffer_moves(m_ref, g_ref, m, g), came)

    def block(k):
        wait(k)
        return split(buffer_block(m, g, columns(k, m.shape[1] // CHUNKS)))

    store_products(
        (n_ref, mine_ref, theirs_ref), (x_ref, p_ref, rs_ref), scratch, block, False
    )


def pair_moves(b_ref, b):
    width = b.shape[2] // CHUNKS

    def moves(k):
        c = columns(k, width)
        return [(b_ref.at[:, :, c], b.at[:, :, c])]

    return moves


def second_products_kernel(
    n_ref, mine_ref, theirs_ref, b_ref, x_ref, p_ref, rs_ref, b, came, *scratch
):
    wait = fetch(pair_moves(b_ref, b), came)

    def block(k):
        wait(k)
        c = columns(k, b.shape[2] // CHUNKS)
        return b[0, :, c], b[1, :, c]

    store_products(
        (n_ref, mine_ref, theirs_ref), (x_ref, p_ref, rs_ref), scratch, block, True
    )


def products(kernel, place, mine, theirs, bigs, held, peers):
    rows, cols = bigs[0].shape[-2:]
    _, height, rank = mine.shape
    tail = 3 * LANES // peers
    shape = (cols // LANES, rank + tail, LANES)
    return call(
        kernel,
        [SM, VM, VM] + [ANY] * len(bigs),
        [
            jax.ShapeDtypeStruct(shape, F32),
            jax.ShapeDtypeStruct((rows, rank), F32),
            jax.ShapeDtypeStruct((8, rank), F32),
        ],
        [VM, VM, VM],
        held
        + [
            dma(CHUNKS, len(bigs)),
            pltpu.VMEM((4, height, rank), F32),
            pltpu.VMEM((3 * LANES, LANES), F32),
            pltpu.VMEM((tail, LANES), F32),
            pltpu.VMEM((2, rank, rows), BF16),
        ],
        6 * rows * cols * rank,
    )(place, mine, theirs, *in_hbm(*bigs))


def spread_kernel(x_ref, y_ref, t_ref, y, sems):
    count = x_ref.shape[0]
    rank = y.shape[0]
    total = x_ref[0]
    for k in range(1, count):
        total = total + x_ref[k]
    y[...] = total[:rank]
    copies = [
        pltpu.make_async_copy(y, y_ref.at[k], sems.at[k]) for k in range(count)
    ]
    for copy in copies:
        copy.start()
    t_ref[...] = total[rank:]
    for copy in copies:
        copy.wait()


def spread_sum(x, rank):
    count, height, width = x.shape
    return call(
        spread_kernel,
        [VM],
        [
            pltpu.HBM((count, rank, width), F32),
            jax.ShapeDtypeStruct((height - rank, width), F32),
        ],
        [ANY, VM],
        [pltpu.VMEM((rank, width), F32), pltpu.SemaphoreType.DMA((count,))],
        count * height * width,
    )(x)


def two_columns(a, b, d, row0, row1, first, second):
    inv = 1.0 / (a * d - b * b)
    i00, i01, i11 = d * inv, -b * inv, a * inv
    e0 = jnp.where(first, 1.0, jnp.where(second, 0.0, row0))
    e1 = jnp.where(first, 0.0, jnp.where(second, 1.0, row1))
    ratio = b / a
    kept = jnp.where(first, -ratio, row1 - ratio * row0)
    return (i00, i01, i11), i00 * e0 + i01 * e1, i01 * e0 + i11 * e1, kept


def eliminated(m):
    n = m.shape[0]
    eye = same(n)
    across = lax.rsqrt(jnp.sum(jnp.where(eye, m, 0.0), axis=0, keepdims=True))
    down = lax.rsqrt(jnp.sum(jnp.where(eye, m, 0.0), axis=1, keepdims=True))
    m = m * down * across
    lane = lax.broadcasted_iota(jnp.int32, (8, n), 1)
    sub = lax.broadcasted_iota(jnp.int32, (8, n), 0)
    tiles = [m[8 * t : 8 * t + 8] for t in range(n // 8)]
    for j in range(0, n, 4):
        t, r = divmod(j, 8)
        here = [lane[:1] == j + k for k in range(4)]
        left, right = here[0] | here[1], here[2] | here[3]
        all_four = (lane >= j) & (lane < j + 4)
        c = [
            [jnp.broadcast_to(x[:, j + k : j + k + 1], (8, n)) for x in tiles[t:]]
            for k in range(4)
        ]
        rows = [tiles[t][r + k : r + k + 1] for k in range(4)]

        def at(k, l):
            return c[l][0][r + k : r + k + 1]

        (i00, i01, i11), use0, use1, kept1 = two_columns(
            at(0, 0), at(1, 0), at(1, 1), rows[0], rows[1], here[0], here[1]
        )
        f2, g2 = i00 * at(2, 0) + i01 * at(2, 1), i01 * at(2, 0) + i11 * at(2, 1)
        f3, g3 = i00 * at(3, 0) + i01 * at(3, 1), i01 * at(3, 0) + i11 * at(3, 1)
        row2 = jnp.where(left, 0.0, rows[2]) - at(2, 0) * use0 - at(2, 1) * use1
        row3 = jnp.where(left, 0.0, rows[3]) - at(3, 0) * use0 - at(3, 1) * use1
        _, use2, use3, kept3 = two_columns(
            at(2, 2) - at(2, 0) * f2 - at(2, 1) * g2,
            at(3, 2) - at(3, 0) * f2 - at(3, 1) * g2,
            at(3, 3) - at(3, 0) * f3 - at(3, 1) * g3,
            row2,
            row3,
            here[2],
            here[3],
        )
        use0, use1 = jnp.where(right, 0.0, use0), jnp.where(right, 0.0, use1)
        for s in range(t, n // 8):
            c0, c1, c2, c3 = (c[k][s - t] for k in range(4))
            c2 = c2 - c0 * f2 - c1 * g2
            c3 = c3 - c0 * f3 - c1 * g3
            new = jnp.where(all_four, 0.0, tiles[s]) - c0 * use0 - c1 * use1
            new = new - c2 * use2 - c3 * use3
            if s == t:
                own = jnp.where(sub == r + 1, kept1, tiles[s])
                own = jnp.where(sub == r + 2, row2, own)
                own = jnp.where(sub == r + 3, kept3, own)
                new = jnp.where(sub > r + 3, new, own)
            tiles[s] = new
    m = jnp.concatenate(tiles, axis=0)
    i = lax.broadcasted_iota(jnp.int32, (n, n), 0)
    j = lax.broadcasted_iota(jnp.int32, (n, n), 1)
    pivots = jnp.sum(jnp.where(eye, m, 0.0), axis=1, keepdims=True)
    unit = jnp.where(i > j, m, jnp.where(eye, 1.0, 0.0))
    return unit * lax.rsqrt(pivots) * across


def cholesky_kernel(n_ref, p_ref, *refs):
    pieces, (w_ref, o_ref, a, low) = refs[:-4], refs[-4:]
    size = pieces[0].shape[0]
    count = len(pieces)
    for k, piece in enumerate(pieces):
        place = lax.rem(n_ref[0] // 2 + k, count)
        a[pl.ds(pl.multiple_of(place * size, size), size), :] = piece[...]
    half = LANES

    def body(b, carry):
        w = eliminated(a[pl.ds(pl.multiple_of(2 * b * half, half), half), :])
        first = pl.multiple_of(b * half, half)
        w_ref[pl.ds(first, half), pl.ds(first, half)] = w

        @pl.when(b == 0)
        def _():
            low[...] = exact(a[half : 2 * half], w, NT)
            a[2 * half :] -= exact(low[...], low[...], NT)

        return carry

    lax.fori_loop(0, 2, body, 0)
    w_ref[:half, half:] = jnp.zeros((half, half), F32)
    w_ref[half:, :half] = -exact(
        w_ref[half:, half:], exact(low[...], w_ref[:half, :half], NN), NN
    )
    o_ref[...] = exact(p_ref[...], w_ref[...], NT)


def inverse_factor(pieces, place, p):
    rank = p.shape[1]
    return call(
        cholesky_kernel,
        [SM, VM] + [VM] * len(pieces),
        [jax.ShapeDtypeStruct((rank, rank), F32), jax.ShapeDtypeStruct(p.shape, F32)],
        [VM, VM],
        [pltpu.VMEM((3 * LANES, LANES), F32), pltpu.VMEM((LANES, LANES), F32)],
        10**10,
    )(place, p, *pieces)


def ahead_kernel(after_ref, m_ref, g_ref, a_ref, m, g, a, came, sent):
    del after_ref
    width = m.shape[1] // CHUNKS
    wait = fetch(buffer_moves(m_ref, g_ref, m, g), came)
    start, finish = send(
        lambda k: [(a.at[:, :, columns(k, width)], a_ref.at[:, :, columns(k, width)])], sent
    )

    def block(k):
        c = columns(k, width)
        wait(k)
        a[0, :, c], a[1, :, c] = split(buffer_block(m, g, c))
        start(k)

    each(block)
    finish()


def buffer_ahead(after, momentum, grads):
    rows, cols = momentum.shape
    return call(
        ahead_kernel,
        [VM] + [ANY] * 2,
        pair_in_hbm((rows, cols)),
        ANY,
        [
            pltpu.VMEM((rows, cols), F32),
            pltpu.VMEM(grads.shape, BF16),
            pltpu.VMEM((2, rows, cols), BF16),
            dma(CHUNKS, 3),
            dma(CHUNKS, 1),
        ],
        8 * rows * cols,
    )(after, *in_hbm(momentum, grads))


def middle_kernel(o_ref, w_ref, x_ref, a_ref, q_ref, rt_ref, a, q_sum, s_ref, sems):
    wait = fetch(pair_moves(a_ref, a), sems)

    def turn(k):
        c = columns(k, LANES)
        rt_ref[0, :, c], rt_ref[1, :, c] = split(x_ref[k])

    each(turn, x_ref.shape[0])
    rt = (rt_ref[0], rt_ref[1])
    w = split(w_ref[...])
    s_ref[...] = dot3(split(dot3(w, split(dot3(rt, rt, NT)), NN)), w, NT)
    width = a.shape[2] // CHUNKS
    q_sum[...] = jnp.zeros_like(q_sum)

    def block(k):
        c = columns(k, width)
        wait(k)
        q_sum[...] += dot3(
            (a[0, :, c], a[1, :, c]), (rt_ref[0, :, c], rt_ref[1, :, c]), NT
        )

    each(block)
    s = s_ref[...]
    q = dot3(split(q_sum[...]), split(w_ref[...]), NT) - dot3(
        split((1.0 - KEEP_RATE) * o_ref[...]), split(s), NN
    )
    n = s.shape[0]
    squares = jnp.sum(jnp.where(same(n), s, 0.0), axis=0, keepdims=True)
    height = q_ref.shape[1] - 8
    for k in range(q_ref.shape[0]):
        q_ref[k, :height] = q[k * height : (k + 1) * height]
        q_ref[k, height:] = jnp.broadcast_to(squares, (8, n))


def middle(o, w, x, ahead):
    _, rows, cols = ahead.shape
    rank = o.shape[1]
    return call(
        middle_kernel,
        [VM] * 3 + [ANY],
        [jax.ShapeDtypeStruct((4, rows // 4 + 8, rank), F32), pair((rank, cols))],
        [VM] * 2,
        [
            pltpu.VMEM((2, rows, cols), BF16),
            pltpu.VMEM((rows, rank), F32),
            pltpu.VMEM((rank, rank), F32),
            dma(CHUNKS, 1),
        ],
        10 * rows * cols * rank,
    )(o, w, x, *in_hbm(ahead))


def update_kernel(half, o_ref, w_ref, rt_ref, a_ref, *refs):
    raw_ref, b_ref, a, raw, b, came, sent = refs[-7:]
    count = CHUNKS // 2
    width = a.shape[2] // count
    base = half * a.shape[2]

    def placed(k):
        if isinstance(k, int):
            return pl.ds(base + k * width, width)
        return pl.ds(pl.multiple_of(base + k * width, width), width)

    def moves(k):
        return [(a_ref.at[:, :, placed(k)], a.at[:, :, columns(k, width)])]

    wait = fetch(moves, came, count)
    start, finish = send(
        lambda k: [
            (raw.at[:, :, columns(k, width)], raw_ref.at[:, :, placed(k)]),
            (b.at[:, :, columns(k, width)], b_ref.at[:, :, placed(k)]),
        ],
        sent,
        count,
    )
    o = split((1.0 - KEEP_RATE) * o_ref[...])
    w = split(w_ref[...])

    def block(k):
        c, there = columns(k, width), placed(k)
        now = split(dot3(w, (rt_ref[0, :, there], rt_ref[1, :, there]), NN))
        raw[0, :, c], raw[1, :, c] = now
        wait(k)
        b[0, :, c], b[1, :, c] = split(
            a[0, :, c].astype(F32) + a[1, :, c].astype(F32) - dot3(o, now, NN)
        )
        start(k)

    each(block, count)
    finish()


def second_buffer(half, o, w, rt, ahead, begun):
    _, rows, cols = ahead.shape
    rank = o.shape[1]
    part = cols // 2
    return call(
        functools.partial(update_kernel, half),
        [VM] * 3 + [ANY] * (1 + len(begun)),
        [pair_in_hbm((rank, cols)), pair_in_hbm((rows, cols))],
        [ANY] * 2,
        [
            pltpu.VMEM((2, rows, part), BF16),
            pltpu.VMEM((2, rank, part), BF16),
            pltpu.VMEM((2, rows, part), BF16),
            dma(CHUNKS // 2, 1),
            dma(CHUNKS // 2, 2),
        ],
        5 * rows * cols * rank,
        {4: 0, 5: 1} if begun else None,
    )(o, w, rt, *in_hbm(ahead), *in_hbm(*begun))


def write_out(value, out_ref, buffer, sems):
    width = buffer.shape[1] // CHUNKS
    start, finish = send(
        lambda k: [(buffer.at[:, columns(k, width)], out_ref.at[:, columns(k, width)])], sems
    )

    def block(k):
        c = columns(k, width)
        buffer[:, c] = value(k, c).astype(buffer.dtype)
        start(k)

    each(block)
    finish()


def first_change_kernel(
    factor, after_ref, o_ref, rs_ref, raw_ref, c_ref, raw, buffer, came, sent
):
    del after_ref
    wait = fetch(pair_moves(raw_ref, raw), came)
    o = split(o_ref[...] * (factor * rs_ref[:1]))

    def value(k, c):
        wait(k)
        return dot3(o, (raw[0, :, c], raw[1, :, c]), NN)

    write_out(value, c_ref, buffer, sent)


def first_change(factor, after, o, rs, raw):
    rows, rank = o.shape
    cols = raw.shape[2]
    return call(
        functools.partial(first_change_kernel, factor),
        [VM, VM, VM, ANY],
        pltpu.HBM((rows, cols), F32),
        ANY,
        [
            pltpu.VMEM(raw.shape, BF16),
            pltpu.VMEM((rows, cols), F32),
            dma(CHUNKS, 1),
            dma(CHUNKS, 1),
        ],
        6 * rows * cols * rank,
    )(after, o, rs, *in_hbm(raw))


def last_raw_kernel(w_ref, x_ref, raw_ref, sq_ref, x, total, came):
    blocks = x_ref.shape[0] // CHUNKS
    wait = fetch(
        lambda k: [(x_ref.at[columns(k, blocks)], x.at[columns(k, blocks)])], came
    )
    total[...] = jnp.zeros_like(total)
    w = split(w_ref[...])

    def block(k):
        c = columns(k, blocks * LANES)
        wait(k)
        part = jnp.concatenate([x[k * blocks + q] for q in range(blocks)], axis=1)
        raw = dot3(w, split(part), NN)
        raw_ref[0, :, c], raw_ref[1, :, c] = split(raw)
        square = raw * raw
        for q in range(blocks):
            total[...] += square[:, q * LANES : (q + 1) * LANES]

    each(block)
    row = exact(jnp.ones((8, LANES), F32), total[...], NT)
    for k in range(sq_ref.shape[0]):
        sq_ref[k] = row


def last_raw(w, x, peers):
    rank = w.shape[0]
    cols = x.shape[0] * LANES
    return call(
        last_raw_kernel,
        [VM, ANY],
        [pair((rank, cols)), jax.ShapeDtypeStruct((peers, 8, rank), F32)],
        [VM] * 2,
        [
            pltpu.VMEM(x.shape, F32),
            pltpu.VMEM((rank, LANES), F32),
            dma(CHUNKS, 1),
        ],
        6 * rank * cols * rank,
    )(w, *in_hbm(x))


def state_kernel(o_ref, raw_ref, b_ref, s_ref, b, buffer, came, sent):
    wait = fetch(pair_moves(b_ref, b), came)
    o = split((1.0 - KEEP_RATE) * o_ref[...])

    def value(k, c):
        wait(k)
        b_now = b[0, :, c].astype(F32) + b[1, :, c].astype(F32)
        return b_now - dot3(o, (raw_ref[0, :, c], raw_ref[1, :, c]), NN)

    write_out(value, s_ref, buffer, sent)


def last_state(o, raw, b):
    _, rows, cols = b.shape
    return call(
        state_kernel,
        [VM, VM, ANY],
        pltpu.HBM((rows, cols), F32),
        ANY,
        [
            pltpu.VMEM(b.shape, BF16),
            pltpu.VMEM((rows, cols), F32),
            dma(CHUNKS, 1),
            dma(CHUNKS, 1),
        ],
        6 * rows * cols * o.shape[1],
    )(o, raw, *in_hbm(b))


def last_change_kernel(
    factor, o_ref, sq_ref, raw_ref, c_ref, out_ref, held, buffer, came, sent
):
    width = held.shape[1] // CHUNKS
    wait = fetch(
        lambda k: [(c_ref.at[:, columns(k, width)], held.at[:, columns(k, width)])], came
    )
    total = sq_ref[0, :1]
    for k in range(1, sq_ref.shape[0]):
        total = total + sq_ref[k, :1]
    o = split(o_ref[...] * (factor * lax.rsqrt(total + NORM_EPS)))

    def value(k, c):
        wait(k)
        return held[:, c] + dot3(o, (raw_ref[0, :, c], raw_ref[1, :, c]), NN)

    write_out(value, out_ref, buffer, sent)


def last_change(factor, o, sq, raw, change):
    rows, cols = change.shape
    return call(
        functools.partial(last_change_kernel, factor),
        [VM, VM, VM, ANY],
        pltpu.HBM((rows, cols), BF16),
        ANY,
        [
            pltpu.VMEM((rows, cols), F32),
            pltpu.VMEM((rows, cols), BF16),
            dma(CHUNKS, 1),
            dma(CHUNKS, 1),
        ],
        6 * rows * cols * o.shape[1],
    )(o, sq, raw, *in_hbm(change))


SIDE = 4


def chip_permute(x, move):
    pairs = [(2 * k + c, 2 * move(k) + c) for k in range(SIDE) for c in range(2)]
    return lax.ppermute(x, "col", pairs)


def core_permute(x):
    return lax.ppermute(x, "col", [(k, k ^ 1) for k in range(2 * SIDE)])


def near(k):
    return k ^ 1


def far(k):
    return SIDE - 1 - k


def col_sum(parts, beside):
    core = lax.axis_index("col") % 2
    mine = lax.dynamic_slice_in_dim(parts, 2 * core, 2, 0)
    theirs = lax.dynamic_slice_in_dim(parts, 2 - 2 * core, 2, 0)
    mine = mine + core_permute(theirs)
    a, b, done = mine[0], mine[1], []
    for half, moves in enumerate(((near, far), (far, near))):
        from_a, from_b, done = lax.optimization_barrier(
            (chip_permute(a, moves[0]), chip_permute(b, moves[1]), beside(half, done))
        )
        a, b = a + from_a, b + from_b
    mine = jnp.stack([a, b])
    return mine, core_permute(mine), done


def by_chip(part):
    core = lax.axis_index("col") % 2
    other = core_permute(part)
    chip = jnp.where(
        core == 0, jnp.concatenate([part, other]), jnp.concatenate([other, part])
    )
    return [chip] + [
        chip_permute(chip, lambda k, d=d: (k - d) % SIDE) for d in range(1, SIDE)
    ]


def exchange(x, axis):
    return lax.all_to_all(x, axis, 0, 0, tiled=True)


def row_total(blocks, p, place, beside):
    own, part = spread_sum(exchange(blocks, "row"), p.shape[1])
    total, extra = lax.optimization_barrier((exchange(own, "row"), beside(part)))
    return total, *inverse_factor(by_chip(part), place, p), extra


def shards(momentum, grads, basis):
    rows, cols = momentum.shape
    rank = basis.shape[1]
    peers = lax.axis_size("col")
    factor = (rows * lax.axis_size("row") * cols * peers / rank) ** 0.5
    place = lax.axis_index("col").astype(jnp.int32)[None]

    held = [pltpu.VMEM((rows, cols), F32), pltpu.VMEM((1, rows, cols), BF16)]
    part = first_projection(momentum, grads, basis)
    mine, theirs, _ = col_sum(part.reshape(4, rows // 4, rank), lambda half, done: [])
    x1, p1, _ = products(
        first_products_kernel, place, mine, theirs, [momentum, grads], held, peers
    )
    x1, w1, o1, ahead = row_total(
        x1, p1, place, lambda part: buffer_ahead(part, momentum, grads)
    )
    part, rt1 = middle(o1, w1, x1, ahead)
    mine, theirs, (raw1, buffer) = col_sum(
        part, lambda half, done: second_buffer(half, o1, w1, rt1, ahead, done)
    )
    held = [pltpu.VMEM((2, rows, cols), BF16)]
    x2, p2, rs1 = products(
        second_products_kernel, place, mine, theirs, [buffer], held, peers
    )
    x2, w2, o2, change1 = row_total(
        x2, p2, place, lambda part: first_change(factor, part, o1, rs1, raw1)
    )
    raw2, sq2 = last_raw(w2, x2, peers)
    sq2, state = lax.optimization_barrier(
        (exchange(sq2, "col"), last_state(o2, raw2, buffer))
    )
    change = last_change(factor, o2, sq2, raw2, change1)
    return change, state


def solution(mesh):
    return jax.shard_map(
        shards,
        mesh=mesh,
        in_specs=(P("row", "col"), P(None, "row", "col"), P("col", None)),
        out_specs=(P("row", "col"), P("row", "col")),
        check_vma=False,
    )
```

```python
import functools

import jax
import jax.numpy as jnp
from jax import lax
from jax.experimental import pallas as pl
from jax.experimental.pallas import tpu as pltpu
from jax.sharding import PartitionSpec as P

KEEP_RATE = 0.95
NORM_EPS = 1e-06
LANES = 128
CHUNKS = 4
F32 = jnp.float32
BF16 = jnp.bfloat16
VMEM_LIMIT = 20 * 1024 * 1024
NN = (((1,), (0,)), ((), ()))
NT = (((1,), (1,)), ((), ()))


def split(x):
    high = x.astype(BF16)
    return high, (x - high.astype(F32)).astype(BF16)


def mm(a, b, dims):
    return lax.dot_general(a, b, dims, preferred_element_type=F32)


def dot3(a, b, dims):
    return mm(a[0], b[0], dims) + (mm(a[0], b[1], dims) + mm(a[1], b[0], dims))


def exact(a, b, dims):
    return lax.dot_general(
        a, b, dims, precision=lax.Precision.HIGHEST, preferred_element_type=F32
    )


def call(kernel, in_specs, out_shape, out_specs, scratch, cost, aliases=None):
    return pl.pallas_call(
        kernel,
        in_specs=in_specs,
        out_specs=out_specs,
        out_shape=out_shape,
        scratch_shapes=scratch,
        input_output_aliases=aliases or {},
        compiler_params=pltpu.CompilerParams(vmem_limit_bytes=VMEM_LIMIT),
        cost_estimate=pl.CostEstimate(
            flops=cost, transcendentals=0, bytes_accessed=8 * 1024 * 1024
        ),
    )


VM = pl.BlockSpec(memory_space=pltpu.VMEM)
SM = pl.BlockSpec(memory_space=pltpu.SMEM)
ANY = pl.BlockSpec(memory_space=pl.ANY)


def in_hbm(*arrays):
    return [pltpu.with_memory_space_constraint(a, pltpu.HBM) for a in arrays]


def pair(shape):
    return jax.ShapeDtypeStruct((2, *shape), BF16)


def pair_in_hbm(shape):
    return pltpu.HBM((2, *shape), BF16)


def dma(*shape):
    return pltpu.SemaphoreType.DMA(shape)


def fetch(moves, sems, count=CHUNKS):
    def copies(k):
        return [
            pltpu.make_async_copy(a, b, sems.at[k, n]) for n, (a, b) in enumerate(moves(k))
        ]

    for k in range(count):
        for copy in copies(k):
            copy.start()

    def wait(k):
        for copy in copies(k):
            copy.wait()

    return wait


def send(moves, sems, count=CHUNKS):
    def copies(k):
        return [
            pltpu.make_async_copy(a, b, sems.at[k, n]) for n, (a, b) in enumerate(moves(k))
        ]

    def start(k):
        for copy in copies(k):
            copy.start()

    def finish():
        for k in range(count):
            for copy in copies(k):
                copy.wait()

    return start, finish


def columns(k, width):
    if isinstance(k, int):
        return pl.ds(k * width, width)
    return pl.ds(pl.multiple_of(k * width, width), width)


def each(block, count=CHUNKS):
    lax.fori_loop(0, count, lambda k, _: (block(k), 0)[1], 0)


def lower(n):
    i = lax.broadcasted_iota(jnp.int32, (n, n), 0)
    return i >= lax.broadcasted_iota(jnp.int32, (n, n), 1)


def same(n):
    i = lax.broadcasted_iota(jnp.int32, (n, n), 0)
    return i == lax.broadcasted_iota(jnp.int32, (n, n), 1)


def buffer_moves(m_ref, g_ref, m, g):
    width = m.shape[1] // CHUNKS

    def moves(k):
        c = columns(k, width)
        pairs = [(m_ref.at[:, c], m.at[:, c])]
        for n in range(g.shape[0]):
            pairs.append((g_ref.at[n, :, c], g.at[n, :, c]))
        return pairs

    return moves


def buffer_block(m, g, c):
    b = m[:, c]
    for n in range(g.shape[0]):
        b = b + g[n, :, c].astype(F32)
    return b


def first_kernel(m_ref, g_ref, v_ref, p_ref, m, g, v, sems):
    width = m.shape[1] // CHUNKS
    moves = buffer_moves(m_ref, g_ref, m, g)
    wait = fetch(
        lambda k: moves(k) + [(v_ref.at[columns(k, width)], v.at[columns(k, width)])], sems
    )
    p_ref[...] = jnp.zeros_like(p_ref)

    def block(k):
        c = columns(k, width)
        wait(k)
        p_ref[...] += dot3(split(buffer_block(m, g, c)), split(v[c]), NN)

    each(block)


def first_projection(momentum, grads, basis):
    rows, cols = momentum.shape
    rank = basis.shape[1]
    return call(
        first_kernel,
        [ANY] * 3,
        jax.ShapeDtypeStruct((rows, rank), F32),
        VM,
        [
            pltpu.VMEM((rows, cols), F32),
            pltpu.VMEM((1, rows, cols), BF16),
            pltpu.VMEM((cols, rank), F32),
            dma(CHUNKS, 3),
        ],
        6 * rows * cols * rank,
    )(*in_hbm(momentum, grads, basis))


def store_products(inputs, outputs, scratch, block, scaled):
    n_ref, mine_ref, theirs_ref = inputs
    x_ref, p_ref, rs_ref = outputs
    parts, t, shares, pair_of_p = scratch
    core = lax.rem(n_ref[0], 2)
    parts[pl.ds(2 * core, 2)] = mine_ref[...]
    parts[pl.ds(2 - 2 * core, 2)] = theirs_ref[...]
    rows, rank = p_ref.shape
    height = rows // 4
    p = jnp.concatenate([parts[k, :height] for k in range(4)], axis=0)
    if scaled:
        rs = lax.rsqrt(parts[0, height : height + 8] + NORM_EPS)
        p = p * rs[:1]
    else:
        rs = jnp.ones(rs_ref.shape, F32)
    rs_ref[...] = rs
    p_ref[...] = p
    turned, half = p.T, LANES
    gram = exact(turned, p, NN)
    head, last = gram[:half, :half], gram[half:, half:]
    t[:half] = jnp.where(lower(half), head, last)
    t[half : 2 * half] = gram[half:, :half]
    diagonal = jnp.sum(jnp.where(same(half), last, 0.0), axis=0, keepdims=True)
    t[2 * half :] = jnp.broadcast_to(diagonal, (t.shape[0] - 2 * half, half))
    size = x_ref.shape[1] - rank
    share = t[pl.ds(pl.multiple_of(n_ref[0] * size, size), size), :]
    pt = split(turned)
    blocks = x_ref.shape[0] // CHUNKS
    shares[...] = share
    pair_of_p[0], pair_of_p[1] = pt

    def fill(k):
        r = dot3((pair_of_p[0], pair_of_p[1]), block(k), NN)
        for q in range(blocks):
            x_ref[k * blocks + q, :rank] = r[:, q * LANES : (q + 1) * LANES]
            x_ref[k * blocks + q, rank:] = shares[...]

    each(fill)


def first_products_kernel(
    n_ref, mine_ref, theirs_ref, m_ref, g_ref, x_ref, p_ref, rs_ref, m, g, came, *scratch
):
    wait = fetch(buffer_moves(m_ref, g_ref, m, g), came)

    def block(k):
        wait(k)
        return split(buffer_block(m, g, columns(k, m.shape[1] // CHUNKS)))

    store_products(
        (n_ref, mine_ref, theirs_ref), (x_ref, p_ref, rs_ref), scratch, block, False
    )


def pair_moves(b_ref, b):
    width = b.shape[2] // CHUNKS

    def moves(k):
        c = columns(k, width)
        return [(b_ref.at[:, :, c], b.at[:, :, c])]

    return moves


def second_products_kernel(
    n_ref, mine_ref, theirs_ref, b_ref, x_ref, p_ref, rs_ref, b, came, *scratch
):
    wait = fetch(pair_moves(b_ref, b), came)

    def block(k):
        wait(k)
        c = columns(k, b.shape[2] // CHUNKS)
        return b[0, :, c], b[1, :, c]

    store_products(
        (n_ref, mine_ref, theirs_ref), (x_ref, p_ref, rs_ref), scratch, block, True
    )


def products(kernel, place, mine, theirs, bigs, held, peers):
    rows, cols = bigs[0].shape[-2:]
    _, height, rank = mine.shape
    tail = -(-(2 * LANES + 8) // (8 * peers)) * 8
    shape = (cols // LANES, rank + tail, LANES)
    return call(
        kernel,
        [SM, VM, VM] + [ANY] * len(bigs),
        [
            jax.ShapeDtypeStruct(shape, F32),
            jax.ShapeDtypeStruct((rows, rank), F32),
            jax.ShapeDtypeStruct((8, rank), F32),
        ],
        [VM, VM, VM],
        held
        + [
            dma(CHUNKS, len(bigs)),
            pltpu.VMEM((4, height, rank), F32),
            pltpu.VMEM((peers * tail, LANES), F32),
            pltpu.VMEM((tail, LANES), F32),
            pltpu.VMEM((2, rank, rows), BF16),
        ],
        6 * rows * cols * rank,
    )(place, mine, theirs, *in_hbm(*bigs))


def spread_kernel(x_ref, y_ref, t_ref, y, sems):
    count = x_ref.shape[0]
    rank = y.shape[0]
    total = x_ref[0]
    for k in range(1, count):
        total = total + x_ref[k]
    y[...] = total[:rank]
    copies = [
        pltpu.make_async_copy(y, y_ref.at[k], sems.at[k]) for k in range(count)
    ]
    for copy in copies:
        copy.start()
    t_ref[...] = total[rank:]
    for copy in copies:
        copy.wait()


def spread_sum(x, rank):
    count, height, width = x.shape
    return call(
        spread_kernel,
        [VM],
        [
            pltpu.HBM((count, rank, width), F32),
            jax.ShapeDtypeStruct((height - rank, width), F32),
        ],
        [ANY, VM],
        [pltpu.VMEM((rank, width), F32), pltpu.SemaphoreType.DMA((count,))],
        count * height * width,
    )(x)


def two_columns(a, b, d, row0, row1, first, second):
    inv = 1.0 / (a * d - b * b)
    i00, i01, i11 = d * inv, -b * inv, a * inv
    e0 = jnp.where(first, 1.0, jnp.where(second, 0.0, row0))
    e1 = jnp.where(first, 0.0, jnp.where(second, 1.0, row1))
    ratio = b / a
    kept = jnp.where(first, -ratio, row1 - ratio * row0)
    return (i00, i01, i11), i00 * e0 + i01 * e1, i01 * e0 + i11 * e1, kept


def eliminated(m):
    n = m.shape[0]
    eye = same(n)
    across = lax.rsqrt(jnp.sum(jnp.where(eye, m, 0.0), axis=0, keepdims=True))
    down = lax.rsqrt(jnp.sum(jnp.where(eye, m, 0.0), axis=1, keepdims=True))
    m = m * down * across
    lane = lax.broadcasted_iota(jnp.int32, (8, n), 1)
    sub = lax.broadcasted_iota(jnp.int32, (8, n), 0)
    tiles = [m[8 * t : 8 * t + 8] for t in range(n // 8)]
    for j in range(0, n, 4):
        t, r = divmod(j, 8)
        here = [lane[:1] == j + k for k in range(4)]
        left, right = here[0] | here[1], here[2] | here[3]
        all_four = (lane >= j) & (lane < j + 4)
        c = [
            [jnp.broadcast_to(x[:, j + k : j + k + 1], (8, n)) for x in tiles[t:]]
            for k in range(4)
        ]
        rows = [tiles[t][r + k : r + k + 1] for k in range(4)]

        def at(k, l):
            return c[l][0][r + k : r + k + 1]

        (i00, i01, i11), use0, use1, kept1 = two_columns(
            at(0, 0), at(1, 0), at(1, 1), rows[0], rows[1], here[0], here[1]
        )
        f2, g2 = i00 * at(2, 0) + i01 * at(2, 1), i01 * at(2, 0) + i11 * at(2, 1)
        f3, g3 = i00 * at(3, 0) + i01 * at(3, 1), i01 * at(3, 0) + i11 * at(3, 1)
        row2 = jnp.where(left, 0.0, rows[2]) - at(2, 0) * use0 - at(2, 1) * use1
        row3 = jnp.where(left, 0.0, rows[3]) - at(3, 0) * use0 - at(3, 1) * use1
        _, use2, use3, kept3 = two_columns(
            at(2, 2) - at(2, 0) * f2 - at(2, 1) * g2,
            at(3, 2) - at(3, 0) * f2 - at(3, 1) * g2,
            at(3, 3) - at(3, 0) * f3 - at(3, 1) * g3,
            row2,
            row3,
            here[2],
            here[3],
        )
        use0, use1 = jnp.where(right, 0.0, use0), jnp.where(right, 0.0, use1)
        for s in range(t, n // 8):
            c0, c1, c2, c3 = (c[k][s - t] for k in range(4))
            c2 = c2 - c0 * f2 - c1 * g2
            c3 = c3 - c0 * f3 - c1 * g3
            new = jnp.where(all_four, 0.0, tiles[s]) - c0 * use0 - c1 * use1
            new = new - c2 * use2 - c3 * use3
            if s == t:
                own = jnp.where(sub == r + 1, kept1, tiles[s])
                own = jnp.where(sub == r + 2, row2, own)
                own = jnp.where(sub == r + 3, kept3, own)
                new = jnp.where(sub > r + 3, new, own)
            tiles[s] = new
    m = jnp.concatenate(tiles, axis=0)
    i = lax.broadcasted_iota(jnp.int32, (n, n), 0)
    j = lax.broadcasted_iota(jnp.int32, (n, n), 1)
    pivots = jnp.sum(jnp.where(eye, m, 0.0), axis=1, keepdims=True)
    unit = jnp.where(i > j, m, jnp.where(eye, 1.0, 0.0))
    return unit * lax.rsqrt(pivots) * across


def cholesky_kernel(n_ref, p_ref, *refs):
    pieces, (w_ref, o_ref, packed, a, low) = refs[:-5], refs[-5:]
    size = pieces[0].shape[0]
    count = len(pieces)
    for k, piece in enumerate(pieces):
        place = lax.rem(n_ref[0] // 2 + k, count)
        packed[pl.ds(pl.multiple_of(place * size, size), size), :] = piece[...]
    half = LANES
    both = packed[:half]
    turned = both.T
    a[:half] = jnp.where(lower(half), both, turned)
    a[half : 2 * half] = packed[half : 2 * half]
    a[2 * half :] = jnp.where(
        same(half), packed[2 * half : 2 * half + 1], jnp.where(lower(half), turned, both)
    )

    def body(b, carry):
        w = eliminated(a[pl.ds(pl.multiple_of(2 * b * half, half), half), :])
        first = pl.multiple_of(b * half, half)
        w_ref[pl.ds(first, half), pl.ds(first, half)] = w

        @pl.when(b == 0)
        def _():
            low[...] = exact(a[half : 2 * half], w, NT)
            a[2 * half :] -= exact(low[...], low[...], NT)

        return carry

    lax.fori_loop(0, 2, body, 0)
    w_ref[:half, half:] = jnp.zeros((half, half), F32)
    w_ref[half:, :half] = -exact(
        w_ref[half:, half:], exact(low[...], w_ref[:half, :half], NN), NN
    )
    o_ref[...] = exact(p_ref[...], w_ref[...], NT)


def inverse_factor(pieces, place, p):
    rank = p.shape[1]
    return call(
        cholesky_kernel,
        [SM, VM] + [VM] * len(pieces),
        [jax.ShapeDtypeStruct((rank, rank), F32), jax.ShapeDtypeStruct(p.shape, F32)],
        [VM, VM],
        [
            pltpu.VMEM((len(pieces) * pieces[0].shape[0], LANES), F32),
            pltpu.VMEM((3 * LANES, LANES), F32),
            pltpu.VMEM((LANES, LANES), F32),
        ],
        10**10,
    )(place, p, *pieces)


def ahead_kernel(after_ref, m_ref, g_ref, a_ref, m, g, a, came, sent):
    del after_ref
    width = m.shape[1] // CHUNKS
    wait = fetch(buffer_moves(m_ref, g_ref, m, g), came)
    start, finish = send(
        lambda k: [(a.at[:, :, columns(k, width)], a_ref.at[:, :, columns(k, width)])], sent
    )

    def block(k):
        c = columns(k, width)
        wait(k)
        a[0, :, c], a[1, :, c] = split(buffer_block(m, g, c))
        start(k)

    each(block)
    finish()


def buffer_ahead(after, momentum, grads):
    rows, cols = momentum.shape
    return call(
        ahead_kernel,
        [VM] + [ANY] * 2,
        pair_in_hbm((rows, cols)),
        ANY,
        [
            pltpu.VMEM((rows, cols), F32),
            pltpu.VMEM(grads.shape, BF16),
            pltpu.VMEM((2, rows, cols), BF16),
            dma(CHUNKS, 3),
            dma(CHUNKS, 1),
        ],
        8 * rows * cols,
    )(after, *in_hbm(momentum, grads))


def middle_kernel(o_ref, w_ref, x_ref, a_ref, q_ref, rt_ref, a, q_sum, s_ref, sems):
    wait = fetch(pair_moves(a_ref, a), sems)

    def turn(k):
        c = columns(k, LANES)
        rt_ref[0, :, c], rt_ref[1, :, c] = split(x_ref[k])

    each(turn, x_ref.shape[0])
    rt = (rt_ref[0], rt_ref[1])
    w = split(w_ref[...])
    s_ref[...] = dot3(split(dot3(w, split(dot3(rt, rt, NT)), NN)), w, NT)
    width = a.shape[2] // CHUNKS
    q_sum[...] = jnp.zeros_like(q_sum)

    def block(k):
        c = columns(k, width)
        wait(k)
        q_sum[...] += dot3(
            (a[0, :, c], a[1, :, c]), (rt_ref[0, :, c], rt_ref[1, :, c]), NT
        )

    each(block)
    s = s_ref[...]
    q = dot3(split(q_sum[...]), split(w_ref[...]), NT) - dot3(
        split((1.0 - KEEP_RATE) * o_ref[...]), split(s), NN
    )
    n = s.shape[0]
    squares = jnp.sum(jnp.where(same(n), s, 0.0), axis=0, keepdims=True)
    height = q_ref.shape[1] - 8
    for k in range(q_ref.shape[0]):
        q_ref[k, :height] = q[k * height : (k + 1) * height]
        q_ref[k, height:] = jnp.broadcast_to(squares, (8, n))


def middle(o, w, x, ahead):
    _, rows, cols = ahead.shape
    rank = o.shape[1]
    return call(
        middle_kernel,
        [VM] * 3 + [ANY],
        [jax.ShapeDtypeStruct((4, rows // 4 + 8, rank), F32), pair((rank, cols))],
        [VM] * 2,
        [
            pltpu.VMEM((2, rows, cols), BF16),
            pltpu.VMEM((rows, rank), F32),
            pltpu.VMEM((rank, rank), F32),
            dma(CHUNKS, 1),
        ],
        10 * rows * cols * rank,
    )(o, w, x, *in_hbm(ahead))


def update_kernel(half, o_ref, w_ref, rt_ref, a_ref, *refs):
    raw_ref, b_ref, a, raw, b, came, sent = refs[-7:]
    count = CHUNKS // 2
    width = a.shape[2] // count
    base = half * a.shape[2]

    def placed(k):
        if isinstance(k, int):
            return pl.ds(base + k * width, width)
        return pl.ds(pl.multiple_of(base + k * width, width), width)

    def moves(k):
        return [(a_ref.at[:, :, placed(k)], a.at[:, :, columns(k, width)])]

    wait = fetch(moves, came, count)
    start, finish = send(
        lambda k: [
            (raw.at[:, :, columns(k, width)], raw_ref.at[:, :, placed(k)]),
            (b.at[:, :, columns(k, width)], b_ref.at[:, :, placed(k)]),
        ],
        sent,
        count,
    )
    o = split((1.0 - KEEP_RATE) * o_ref[...])
    w = split(w_ref[...])

    def block(k):
        c, there = columns(k, width), placed(k)
        now = split(dot3(w, (rt_ref[0, :, there], rt_ref[1, :, there]), NN))
        raw[0, :, c], raw[1, :, c] = now
        wait(k)
        b[0, :, c], b[1, :, c] = split(
            a[0, :, c].astype(F32) + a[1, :, c].astype(F32) - dot3(o, now, NN)
        )
        start(k)

    each(block, count)
    finish()


def second_buffer(half, o, w, rt, ahead, begun):
    _, rows, cols = ahead.shape
    rank = o.shape[1]
    part = cols // 2
    return call(
        functools.partial(update_kernel, half),
        [VM] * 3 + [ANY] * (1 + len(begun)),
        [pair_in_hbm((rank, cols)), pair_in_hbm((rows, cols))],
        [ANY] * 2,
        [
            pltpu.VMEM((2, rows, part), BF16),
            pltpu.VMEM((2, rank, part), BF16),
            pltpu.VMEM((2, rows, part), BF16),
            dma(CHUNKS // 2, 1),
            dma(CHUNKS // 2, 2),
        ],
        5 * rows * cols * rank,
        {4: 0, 5: 1} if begun else None,
    )(o, w, rt, *in_hbm(ahead), *in_hbm(*begun))


def write_out(value, out_ref, buffer, sems):
    width = buffer.shape[1] // CHUNKS
    start, finish = send(
        lambda k: [(buffer.at[:, columns(k, width)], out_ref.at[:, columns(k, width)])], sems
    )

    def block(k):
        c = columns(k, width)
        buffer[:, c] = value(k, c).astype(buffer.dtype)
        start(k)

    each(block)
    finish()


def first_change_kernel(
    factor, after_ref, o_ref, rs_ref, raw_ref, c_ref, raw, buffer, came, sent
):
    del after_ref
    wait = fetch(pair_moves(raw_ref, raw), came)
    o = split(o_ref[...] * (factor * rs_ref[:1]))

    def value(k, c):
        wait(k)
        return dot3(o, (raw[0, :, c], raw[1, :, c]), NN)

    write_out(value, c_ref, buffer, sent)


def first_change(factor, after, o, rs, raw):
    rows, rank = o.shape
    cols = raw.shape[2]
    return call(
        functools.partial(first_change_kernel, factor),
        [VM, VM, VM, ANY],
        pltpu.HBM((rows, cols), F32),
        ANY,
        [
            pltpu.VMEM(raw.shape, BF16),
            pltpu.VMEM((rows, cols), F32),
            dma(CHUNKS, 1),
            dma(CHUNKS, 1),
        ],
        6 * rows * cols * rank,
    )(after, o, rs, *in_hbm(raw))


def last_raw_kernel(w_ref, x_ref, raw_ref, sq_ref, x, total, came):
    blocks = x_ref.shape[0] // CHUNKS
    wait = fetch(
        lambda k: [(x_ref.at[columns(k, blocks)], x.at[columns(k, blocks)])], came
    )
    total[...] = jnp.zeros_like(total)
    w = split(w_ref[...])

    def block(k):
        c = columns(k, blocks * LANES)
        wait(k)
        part = jnp.concatenate([x[k * blocks + q] for q in range(blocks)], axis=1)
        raw = dot3(w, split(part), NN)
        raw_ref[0, :, c], raw_ref[1, :, c] = split(raw)
        square = raw * raw
        for q in range(blocks):
            total[...] += square[:, q * LANES : (q + 1) * LANES]

    each(block)
    row = exact(jnp.ones((8, LANES), F32), total[...], NT)
    for k in range(sq_ref.shape[0]):
        sq_ref[k] = row


def last_raw(w, x, peers):
    rank = w.shape[0]
    cols = x.shape[0] * LANES
    return call(
        last_raw_kernel,
        [VM, ANY],
        [pair((rank, cols)), jax.ShapeDtypeStruct((peers, 8, rank), F32)],
        [VM] * 2,
        [
            pltpu.VMEM(x.shape, F32),
            pltpu.VMEM((rank, LANES), F32),
            dma(CHUNKS, 1),
        ],
        6 * rank * cols * rank,
    )(w, *in_hbm(x))


def state_kernel(o_ref, raw_ref, b_ref, s_ref, b, buffer, came, sent):
    wait = fetch(pair_moves(b_ref, b), came)
    o = split((1.0 - KEEP_RATE) * o_ref[...])

    def value(k, c):
        wait(k)
        b_now = b[0, :, c].astype(F32) + b[1, :, c].astype(F32)
        return b_now - dot3(o, (raw_ref[0, :, c], raw_ref[1, :, c]), NN)

    write_out(value, s_ref, buffer, sent)


def last_state(o, raw, b):
    _, rows, cols = b.shape
    return call(
        state_kernel,
        [VM, VM, ANY],
        pltpu.HBM((rows, cols), F32),
        ANY,
        [
            pltpu.VMEM(b.shape, BF16),
            pltpu.VMEM((rows, cols), F32),
            dma(CHUNKS, 1),
            dma(CHUNKS, 1),
        ],
        6 * rows * cols * o.shape[1],
    )(o, raw, *in_hbm(b))


def last_change_kernel(
    factor, o_ref, sq_ref, raw_ref, c_ref, out_ref, held, buffer, came, sent
):
    width = held.shape[1] // CHUNKS
    wait = fetch(
        lambda k: [(c_ref.at[:, columns(k, width)], held.at[:, columns(k, width)])], came
    )
    total = sq_ref[0, :1]
    for k in range(1, sq_ref.shape[0]):
        total = total + sq_ref[k, :1]
    o = split(o_ref[...] * (factor * lax.rsqrt(total + NORM_EPS)))

    def value(k, c):
        wait(k)
        return held[:, c] + dot3(o, (raw_ref[0, :, c], raw_ref[1, :, c]), NN)

    write_out(value, out_ref, buffer, sent)


def last_change(factor, o, sq, raw, change):
    rows, cols = change.shape
    return call(
        functools.partial(last_change_kernel, factor),
        [VM, VM, VM, ANY],
        pltpu.HBM((rows, cols), BF16),
        ANY,
        [
            pltpu.VMEM((rows, cols), F32),
            pltpu.VMEM((rows, cols), BF16),
            dma(CHUNKS, 1),
            dma(CHUNKS, 1),
        ],
        6 * rows * cols * o.shape[1],
    )(o, sq, raw, *in_hbm(change))


SIDE = 4


def chip_permute(x, move):
    pairs = [(2 * k + c, 2 * move(k) + c) for k in range(SIDE) for c in range(2)]
    return lax.ppermute(x, "col", pairs)


def core_permute(x):
    return lax.ppermute(x, "col", [(k, k ^ 1) for k in range(2 * SIDE)])


def near(k):
    return k ^ 1


def far(k):
    return SIDE - 1 - k


def col_sum(parts, beside):
    core = lax.axis_index("col") % 2
    mine = lax.dynamic_slice_in_dim(parts, 2 * core, 2, 0)
    theirs = lax.dynamic_slice_in_dim(parts, 2 - 2 * core, 2, 0)
    mine = mine + core_permute(theirs)
    a, b, done = mine[0], mine[1], []
    for half, moves in enumerate(((near, far), (far, near))):
        from_a, from_b, done = lax.optimization_barrier(
            (chip_permute(a, moves[0]), chip_permute(b, moves[1]), beside(half, done))
        )
        a, b = a + from_a, b + from_b
    mine = jnp.stack([a, b])
    return mine, core_permute(mine), done


def by_chip(part):
    core = lax.axis_index("col") % 2
    other = core_permute(part)
    chip = jnp.where(
        core == 0, jnp.concatenate([part, other]), jnp.concatenate([other, part])
    )
    return [chip] + [
        chip_permute(chip, lambda k, d=d: (k - d) % SIDE) for d in range(1, SIDE)
    ]


def exchange(x, axis):
    return lax.all_to_all(x, axis, 0, 0, tiled=True)


def row_total(blocks, p, place, beside):
    own, part = spread_sum(exchange(blocks, "row"), p.shape[1])
    total, extra = lax.optimization_barrier((exchange(own, "row"), beside(part)))
    return total, *inverse_factor(by_chip(part), place, p), extra


def shards(momentum, grads, basis):
    rows, cols = momentum.shape
    rank = basis.shape[1]
    peers = lax.axis_size("col")
    factor = (rows * lax.axis_size("row") * cols * peers / rank) ** 0.5
    place = lax.axis_index("col").astype(jnp.int32)[None]

    held = [pltpu.VMEM((rows, cols), F32), pltpu.VMEM((1, rows, cols), BF16)]
    part = first_projection(momentum, grads, basis)
    mine, theirs, _ = col_sum(part.reshape(4, rows // 4, rank), lambda half, done: [])
    x1, p1, _ = products(
        first_products_kernel, place, mine, theirs, [momentum, grads], held, peers
    )
    x1, w1, o1, ahead = row_total(
        x1, p1, place, lambda part: buffer_ahead(part, momentum, grads)
    )
    part, rt1 = middle(o1, w1, x1, ahead)
    mine, theirs, (raw1, buffer) = col_sum(
        part, lambda half, done: second_buffer(half, o1, w1, rt1, ahead, done)
    )
    held = [pltpu.VMEM((2, rows, cols), BF16)]
    x2, p2, rs1 = products(
        second_products_kernel, place, mine, theirs, [buffer], held, peers
    )
    x2, w2, o2, change1 = row_total(
        x2, p2, place, lambda part: first_change(factor, part, o1, rs1, raw1)
    )
    raw2, sq2 = last_raw(w2, x2, peers)
    sq2, state = lax.optimization_barrier(
        (exchange(sq2, "col"), last_state(o2, raw2, buffer))
    )
    change = last_change(factor, o2, sq2, raw2, change1)
    return change, state


def solution(mesh):
    return jax.shard_map(
        shards,
        mesh=mesh,
        in_specs=(P("row", "col"), P(None, "row", "col"), P("col", None)),
        out_specs=(P("row", "col"), P("row", "col")),
        check_vma=False,
    )
```

```python
import functools

import jax
import jax.numpy as jnp
from jax import lax
from jax.experimental import pallas as pl
from jax.experimental.pallas import tpu as pltpu
from jax.sharding import PartitionSpec as P

KEEP_RATE = 0.95
NORM_EPS = 1e-06
LANES = 128
CHUNKS = 4
FEW = 2
F32 = jnp.float32
BF16 = jnp.bfloat16
VMEM_LIMIT = 20 * 1024 * 1024
NN = (((1,), (0,)), ((), ()))
NT = (((1,), (1,)), ((), ()))


def split(x):
    high = x.astype(BF16)
    return high, (x - high.astype(F32)).astype(BF16)


def mm(a, b, dims):
    return lax.dot_general(a, b, dims, preferred_element_type=F32)


def dot3(a, b, dims):
    return mm(a[0], b[0], dims) + (mm(a[0], b[1], dims) + mm(a[1], b[0], dims))


def exact(a, b, dims):
    return lax.dot_general(
        a, b, dims, precision=lax.Precision.HIGHEST, preferred_element_type=F32
    )


def call(kernel, in_specs, out_shape, out_specs, scratch, cost, aliases=None):
    return pl.pallas_call(
        kernel,
        in_specs=in_specs,
        out_specs=out_specs,
        out_shape=out_shape,
        scratch_shapes=scratch,
        input_output_aliases=aliases or {},
        compiler_params=pltpu.CompilerParams(vmem_limit_bytes=VMEM_LIMIT),
        cost_estimate=pl.CostEstimate(
            flops=cost, transcendentals=0, bytes_accessed=8 * 1024 * 1024
        ),
    )


VM = pl.BlockSpec(memory_space=pltpu.VMEM)
SM = pl.BlockSpec(memory_space=pltpu.SMEM)
ANY = pl.BlockSpec(memory_space=pl.ANY)


def in_hbm(*arrays):
    return [pltpu.with_memory_space_constraint(a, pltpu.HBM) for a in arrays]


def pair(shape):
    return jax.ShapeDtypeStruct((2, *shape), BF16)


def pair_in_hbm(shape):
    return pltpu.HBM((2, *shape), BF16)


def dma(*shape):
    return pltpu.SemaphoreType.DMA(shape)


def fetch(moves, sems, count=CHUNKS):
    def copies(k):
        return [
            pltpu.make_async_copy(a, b, sems.at[k, n]) for n, (a, b) in enumerate(moves(k))
        ]

    for k in range(count):
        for copy in copies(k):
            copy.start()

    def wait(k):
        for copy in copies(k):
            copy.wait()

    return wait


def send(moves, sems, count=CHUNKS):
    def copies(k):
        return [
            pltpu.make_async_copy(a, b, sems.at[k, n]) for n, (a, b) in enumerate(moves(k))
        ]

    def start(k):
        for copy in copies(k):
            copy.start()

    def finish():
        for k in range(count):
            for copy in copies(k):
                copy.wait()

    return start, finish


def columns(k, width):
    if isinstance(k, int):
        return pl.ds(k * width, width)
    return pl.ds(pl.multiple_of(k * width, width), width)


def each(block, count=CHUNKS):
    lax.fori_loop(0, count, lambda k, _: (block(k), 0)[1], 0)


def lower(n):
    i = lax.broadcasted_iota(jnp.int32, (n, n), 0)
    return i >= lax.broadcasted_iota(jnp.int32, (n, n), 1)


def same(n):
    i = lax.broadcasted_iota(jnp.int32, (n, n), 0)
    return i == lax.broadcasted_iota(jnp.int32, (n, n), 1)


def buffer_moves(m_ref, g_ref, m, g):
    width = m.shape[1] // CHUNKS

    def moves(k):
        c = columns(k, width)
        pairs = [(m_ref.at[:, c], m.at[:, c])]
        for n in range(g.shape[0]):
            pairs.append((g_ref.at[n, :, c], g.at[n, :, c]))
        return pairs

    return moves


def buffer_block(m, g, c):
    b = m[:, c]
    for n in range(g.shape[0]):
        b = b + g[n, :, c].astype(F32)
    return b


def first_kernel(m_ref, g_ref, v_ref, p_ref, m, g, v, sems):
    width = m.shape[1] // CHUNKS
    moves = buffer_moves(m_ref, g_ref, m, g)
    wait = fetch(
        lambda k: moves(k) + [(v_ref.at[columns(k, width)], v.at[columns(k, width)])], sems
    )
    p_ref[...] = jnp.zeros_like(p_ref)

    def block(k):
        c = columns(k, width)
        wait(k)
        p_ref[...] += dot3(split(buffer_block(m, g, c)), split(v[c]), NN)

    each(block)


def first_projection(momentum, grads, basis):
    rows, cols = momentum.shape
    rank = basis.shape[1]
    return call(
        first_kernel,
        [ANY] * 3,
        jax.ShapeDtypeStruct((rows, rank), F32),
        VM,
        [
            pltpu.VMEM((rows, cols), F32),
            pltpu.VMEM((1, rows, cols), BF16),
            pltpu.VMEM((cols, rank), F32),
            dma(CHUNKS, 3),
        ],
        6 * rows * cols * rank,
    )(*in_hbm(momentum, grads, basis))


def store_products(inputs, outputs, scratch, block, scaled):
    n_ref, mine_ref, theirs_ref = inputs
    x_ref, p_ref, rs_ref = outputs
    parts, t, shares, pair_of_p = scratch
    core = lax.rem(n_ref[0], 2)
    parts[pl.ds(2 * core, 2)] = mine_ref[...]
    parts[pl.ds(2 - 2 * core, 2)] = theirs_ref[...]
    rows, rank = p_ref.shape
    height = rows // 4
    p = jnp.concatenate([parts[k, :height] for k in range(4)], axis=0)
    if scaled:
        rs = lax.rsqrt(parts[0, height : height + 8] + NORM_EPS)
        p = p * rs[:1]
    else:
        rs = jnp.ones(rs_ref.shape, F32)
    rs_ref[...] = rs
    p_ref[...] = p
    turned, half = p.T, LANES
    gram = exact(turned, p, NN)
    head, last = gram[:half, :half], gram[half:, half:]
    t[:half] = jnp.where(lower(half), head, last)
    t[half : 2 * half] = gram[half:, :half]
    diagonal = jnp.sum(jnp.where(same(half), last, 0.0), axis=0, keepdims=True)
    t[2 * half :] = jnp.broadcast_to(diagonal, (t.shape[0] - 2 * half, half))
    size = x_ref.shape[1] - rank
    share = t[pl.ds(pl.multiple_of(n_ref[0] * size, size), size), :]
    pt = split(turned)
    blocks = x_ref.shape[0] // CHUNKS
    shares[...] = share
    pair_of_p[0], pair_of_p[1] = pt

    def fill(k):
        r = dot3((pair_of_p[0], pair_of_p[1]), block(k), NN)
        for q in range(blocks):
            x_ref[k * blocks + q, :rank] = r[:, q * LANES : (q + 1) * LANES]
            x_ref[k * blocks + q, rank:] = shares[...]

    each(fill)


def first_products_kernel(
    n_ref, mine_ref, theirs_ref, m_ref, g_ref, x_ref, p_ref, rs_ref, m, g, came, *scratch
):
    wait = fetch(buffer_moves(m_ref, g_ref, m, g), came)

    def block(k):
        wait(k)
        return split(buffer_block(m, g, columns(k, m.shape[1] // CHUNKS)))

    store_products(
        (n_ref, mine_ref, theirs_ref), (x_ref, p_ref, rs_ref), scratch, block, False
    )


def pair_moves(b_ref, b, count=CHUNKS):
    width = b.shape[2] // count

    def moves(k):
        c = columns(k, width)
        return [(b_ref.at[:, :, c], b.at[:, :, c])]

    return moves


def second_products_kernel(
    n_ref, mine_ref, theirs_ref, b_ref, x_ref, p_ref, rs_ref, b, came, *scratch
):
    wait = fetch(pair_moves(b_ref, b), came)

    def block(k):
        wait(k)
        c = columns(k, b.shape[2] // CHUNKS)
        return b[0, :, c], b[1, :, c]

    store_products(
        (n_ref, mine_ref, theirs_ref), (x_ref, p_ref, rs_ref), scratch, block, True
    )


def products(kernel, place, mine, theirs, bigs, held, peers):
    rows, cols = bigs[0].shape[-2:]
    _, height, rank = mine.shape
    tail = -(-(2 * LANES + 8) // (8 * peers)) * 8
    shape = (cols // LANES, rank + tail, LANES)
    return call(
        kernel,
        [SM, VM, VM] + [ANY] * len(bigs),
        [
            jax.ShapeDtypeStruct(shape, F32),
            jax.ShapeDtypeStruct((rows, rank), F32),
            jax.ShapeDtypeStruct((8, rank), F32),
        ],
        [VM, VM, VM],
        held
        + [
            dma(CHUNKS, len(bigs)),
            pltpu.VMEM((4, height, rank), F32),
            pltpu.VMEM((peers * tail, LANES), F32),
            pltpu.VMEM((tail, LANES), F32),
            pltpu.VMEM((2, rank, rows), BF16),
        ],
        6 * rows * cols * rank,
    )(place, mine, theirs, *in_hbm(*bigs))


def spread_kernel(x_ref, y_ref, t_ref, y, sems):
    count = x_ref.shape[0]
    rank = y.shape[0]
    total = x_ref[0]
    for k in range(1, count):
        total = total + x_ref[k]
    y[...] = total[:rank]
    copies = [
        pltpu.make_async_copy(y, y_ref.at[k], sems.at[k]) for k in range(count)
    ]
    for copy in copies:
        copy.start()
    t_ref[...] = total[rank:]
    for copy in copies:
        copy.wait()


def spread_sum(x, rank):
    count, height, width = x.shape
    return call(
        spread_kernel,
        [VM],
        [
            pltpu.HBM((count, rank, width), F32),
            jax.ShapeDtypeStruct((height - rank, width), F32),
        ],
        [ANY, VM],
        [pltpu.VMEM((rank, width), F32), pltpu.SemaphoreType.DMA((count,))],
        count * height * width,
    )(x)


def two_columns(a, b, d, row0, row1, first, second):
    inv = 1.0 / (a * d - b * b)
    i00, i01, i11 = d * inv, -b * inv, a * inv
    e0 = jnp.where(first, 1.0, jnp.where(second, 0.0, row0))
    e1 = jnp.where(first, 0.0, jnp.where(second, 1.0, row1))
    ratio = b / a
    kept = jnp.where(first, -ratio, row1 - ratio * row0)
    return (i00, i01, i11), i00 * e0 + i01 * e1, i01 * e0 + i11 * e1, kept


def eliminated(m):
    n = m.shape[0]
    eye = same(n)
    across = lax.rsqrt(jnp.sum(jnp.where(eye, m, 0.0), axis=0, keepdims=True))
    down = lax.rsqrt(jnp.sum(jnp.where(eye, m, 0.0), axis=1, keepdims=True))
    m = m * down * across
    lane = lax.broadcasted_iota(jnp.int32, (8, n), 1)
    sub = lax.broadcasted_iota(jnp.int32, (8, n), 0)
    tiles = [m[8 * t : 8 * t + 8] for t in range(n // 8)]
    for j in range(0, n, 4):
        t, r = divmod(j, 8)
        here = [lane[:1] == j + k for k in range(4)]
        left, right = here[0] | here[1], here[2] | here[3]
        all_four = (lane >= j) & (lane < j + 4)
        c = [
            [jnp.broadcast_to(x[:, j + k : j + k + 1], (8, n)) for x in tiles[t:]]
            for k in range(4)
        ]
        rows = [tiles[t][r + k : r + k + 1] for k in range(4)]

        def at(k, l):
            return c[l][0][r + k : r + k + 1]

        (i00, i01, i11), use0, use1, kept1 = two_columns(
            at(0, 0), at(1, 0), at(1, 1), rows[0], rows[1], here[0], here[1]
        )
        f2, g2 = i00 * at(2, 0) + i01 * at(2, 1), i01 * at(2, 0) + i11 * at(2, 1)
        f3, g3 = i00 * at(3, 0) + i01 * at(3, 1), i01 * at(3, 0) + i11 * at(3, 1)
        row2 = jnp.where(left, 0.0, rows[2]) - at(2, 0) * use0 - at(2, 1) * use1
        row3 = jnp.where(left, 0.0, rows[3]) - at(3, 0) * use0 - at(3, 1) * use1
        _, use2, use3, kept3 = two_columns(
            at(2, 2) - at(2, 0) * f2 - at(2, 1) * g2,
            at(3, 2) - at(3, 0) * f2 - at(3, 1) * g2,
            at(3, 3) - at(3, 0) * f3 - at(3, 1) * g3,
            row2,
            row3,
            here[2],
            here[3],
        )
        use0, use1 = jnp.where(right, 0.0, use0), jnp.where(right, 0.0, use1)
        for s in range(t, n // 8):
            c0, c1, c2, c3 = (c[k][s - t] for k in range(4))
            c2 = c2 - c0 * f2 - c1 * g2
            c3 = c3 - c0 * f3 - c1 * g3
            new = jnp.where(all_four, 0.0, tiles[s]) - c0 * use0 - c1 * use1
            new = new - c2 * use2 - c3 * use3
            if s == t:
                own = jnp.where(sub == r + 1, kept1, tiles[s])
                own = jnp.where(sub == r + 2, row2, own)
                own = jnp.where(sub == r + 3, kept3, own)
                new = jnp.where(sub > r + 3, new, own)
            tiles[s] = new
    m = jnp.concatenate(tiles, axis=0)
    i = lax.broadcasted_iota(jnp.int32, (n, n), 0)
    j = lax.broadcasted_iota(jnp.int32, (n, n), 1)
    pivots = jnp.sum(jnp.where(eye, m, 0.0), axis=1, keepdims=True)
    unit = jnp.where(i > j, m, jnp.where(eye, 1.0, 0.0))
    return unit * lax.rsqrt(pivots) * across


def cholesky_kernel(n_ref, p_ref, *refs):
    pieces, (w_ref, o_ref, packed, a, low) = refs[:-5], refs[-5:]
    size = pieces[0].shape[0]
    count = len(pieces)
    for k, piece in enumerate(pieces):
        place = lax.rem(n_ref[0] // 2 + k, count)
        packed[pl.ds(pl.multiple_of(place * size, size), size), :] = piece[...]
    half = LANES
    both = packed[:half]
    turned = both.T
    a[:half] = jnp.where(lower(half), both, turned)
    a[half : 2 * half] = packed[half : 2 * half]
    a[2 * half :] = jnp.where(
        same(half), packed[2 * half : 2 * half + 1], jnp.where(lower(half), turned, both)
    )

    def body(b, carry):
        w = eliminated(a[pl.ds(pl.multiple_of(2 * b * half, half), half), :])
        first = pl.multiple_of(b * half, half)
        w_ref[pl.ds(first, half), pl.ds(first, half)] = w

        @pl.when(b == 0)
        def _():
            low[...] = exact(a[half : 2 * half], w, NT)
            a[2 * half :] -= exact(low[...], low[...], NT)

        return carry

    lax.fori_loop(0, 2, body, 0)
    w_ref[:half, half:] = jnp.zeros((half, half), F32)
    w_ref[half:, :half] = -exact(
        w_ref[half:, half:], exact(low[...], w_ref[:half, :half], NN), NN
    )
    o_ref[...] = exact(p_ref[...], w_ref[...], NT)


def inverse_factor(pieces, place, p):
    rank = p.shape[1]
    return call(
        cholesky_kernel,
        [SM, VM] + [VM] * len(pieces),
        [jax.ShapeDtypeStruct((rank, rank), F32), jax.ShapeDtypeStruct(p.shape, F32)],
        [VM, VM],
        [
            pltpu.VMEM((len(pieces) * pieces[0].shape[0], LANES), F32),
            pltpu.VMEM((3 * LANES, LANES), F32),
            pltpu.VMEM((LANES, LANES), F32),
        ],
        10**10,
    )(place, p, *pieces)


def ahead_kernel(after_ref, m_ref, g_ref, a_ref, m, g, a, came, sent):
    del after_ref
    width = m.shape[1] // CHUNKS
    wait = fetch(buffer_moves(m_ref, g_ref, m, g), came)
    start, finish = send(
        lambda k: [(a.at[:, :, columns(k, width)], a_ref.at[:, :, columns(k, width)])], sent
    )

    def block(k):
        c = columns(k, width)
        wait(k)
        a[0, :, c], a[1, :, c] = split(buffer_block(m, g, c))
        start(k)

    each(block)
    finish()


def buffer_ahead(after, momentum, grads):
    rows, cols = momentum.shape
    return call(
        ahead_kernel,
        [VM] + [ANY] * 2,
        pair_in_hbm((rows, cols)),
        ANY,
        [
            pltpu.VMEM((rows, cols), F32),
            pltpu.VMEM(grads.shape, BF16),
            pltpu.VMEM((2, rows, cols), BF16),
            dma(CHUNKS, 3),
            dma(CHUNKS, 1),
        ],
        8 * rows * cols,
    )(after, *in_hbm(momentum, grads))


def middle_kernel(o_ref, w_ref, x_ref, a_ref, q_ref, rt_ref, a, q_sum, s_ref, sems):
    wait = fetch(pair_moves(a_ref, a, FEW), sems, FEW)

    def turn(k):
        c = columns(k, LANES)
        rt_ref[0, :, c], rt_ref[1, :, c] = split(x_ref[k])

    each(turn, x_ref.shape[0])
    rt = (rt_ref[0], rt_ref[1])
    w = split(w_ref[...])
    s_ref[...] = dot3(split(dot3(w, split(dot3(rt, rt, NT)), NN)), w, NT)
    width = a.shape[2] // FEW
    q_sum[...] = jnp.zeros_like(q_sum)

    def block(k):
        c = columns(k, width)
        wait(k)
        q_sum[...] += dot3(
            (a[0, :, c], a[1, :, c]), (rt_ref[0, :, c], rt_ref[1, :, c]), NT
        )

    each(block, FEW)
    s = s_ref[...]
    q = dot3(split(q_sum[...]), split(w_ref[...]), NT) - dot3(
        split((1.0 - KEEP_RATE) * o_ref[...]), split(s), NN
    )
    n = s.shape[0]
    squares = jnp.sum(jnp.where(same(n), s, 0.0), axis=0, keepdims=True)
    height = q_ref.shape[1] - 8
    for k in range(q_ref.shape[0]):
        q_ref[k, :height] = q[k * height : (k + 1) * height]
        q_ref[k, height:] = jnp.broadcast_to(squares, (8, n))


def middle(o, w, x, ahead):
    _, rows, cols = ahead.shape
    rank = o.shape[1]
    return call(
        middle_kernel,
        [VM] * 3 + [ANY],
        [jax.ShapeDtypeStruct((4, rows // 4 + 8, rank), F32), pair((rank, cols))],
        [VM] * 2,
        [
            pltpu.VMEM((2, rows, cols), BF16),
            pltpu.VMEM((rows, rank), F32),
            pltpu.VMEM((rank, rank), F32),
            dma(FEW, 1),
        ],
        10 * rows * cols * rank,
    )(o, w, x, *in_hbm(ahead))


def update_kernel(half, o_ref, w_ref, rt_ref, a_ref, *refs):
    raw_ref, b_ref, a, raw, b, came, sent = refs[-7:]
    count = CHUNKS // 2
    width = a.shape[2] // count
    base = half * a.shape[2]

    def placed(k):
        if isinstance(k, int):
            return pl.ds(base + k * width, width)
        return pl.ds(pl.multiple_of(base + k * width, width), width)

    def moves(k):
        return [(a_ref.at[:, :, placed(k)], a.at[:, :, columns(k, width)])]

    wait = fetch(moves, came, count)
    start, finish = send(
        lambda k: [
            (raw.at[:, :, columns(k, width)], raw_ref.at[:, :, placed(k)]),
            (b.at[:, :, columns(k, width)], b_ref.at[:, :, placed(k)]),
        ],
        sent,
        count,
    )
    o = split((1.0 - KEEP_RATE) * o_ref[...])
    w = split(w_ref[...])

    def block(k):
        c, there = columns(k, width), placed(k)
        now = split(dot3(w, (rt_ref[0, :, there], rt_ref[1, :, there]), NN))
        raw[0, :, c], raw[1, :, c] = now
        wait(k)
        b[0, :, c], b[1, :, c] = split(
            a[0, :, c].astype(F32) + a[1, :, c].astype(F32) - dot3(o, now, NN)
        )
        start(k)

    each(block, count)
    finish()


def second_buffer(half, o, w, rt, ahead, begun):
    _, rows, cols = ahead.shape
    rank = o.shape[1]
    part = cols // 2
    return call(
        functools.partial(update_kernel, half),
        [VM] * 3 + [ANY] * (1 + len(begun)),
        [pair_in_hbm((rank, cols)), pair_in_hbm((rows, cols))],
        [ANY] * 2,
        [
            pltpu.VMEM((2, rows, part), BF16),
            pltpu.VMEM((2, rank, part), BF16),
            pltpu.VMEM((2, rows, part), BF16),
            dma(CHUNKS // 2, 1),
            dma(CHUNKS // 2, 2),
        ],
        5 * rows * cols * rank,
        {4: 0, 5: 1} if begun else None,
    )(o, w, rt, *in_hbm(ahead), *in_hbm(*begun))


def write_out(value, out_ref, buffer, sems, count=CHUNKS):
    width = buffer.shape[1] // count
    start, finish = send(
        lambda k: [(buffer.at[:, columns(k, width)], out_ref.at[:, columns(k, width)])],
        sems,
        count,
    )

    def block(k):
        c = columns(k, width)
        buffer[:, c] = value(k, c).astype(buffer.dtype)
        start(k)

    each(block, count)
    finish()


def first_change_kernel(
    factor, after_ref, o_ref, rs_ref, raw_ref, c_ref, raw, buffer, came, sent
):
    del after_ref
    wait = fetch(pair_moves(raw_ref, raw), came)
    o = split(o_ref[...] * (factor * rs_ref[:1]))

    def value(k, c):
        wait(k)
        return dot3(o, (raw[0, :, c], raw[1, :, c]), NN)

    write_out(value, c_ref, buffer, sent)


def first_change(factor, after, o, rs, raw):
    rows, rank = o.shape
    cols = raw.shape[2]
    return call(
        functools.partial(first_change_kernel, factor),
        [VM, VM, VM, ANY],
        pltpu.HBM((rows, cols), F32),
        ANY,
        [
            pltpu.VMEM(raw.shape, BF16),
            pltpu.VMEM((rows, cols), F32),
            dma(CHUNKS, 1),
            dma(CHUNKS, 1),
        ],
        6 * rows * cols * rank,
    )(after, o, rs, *in_hbm(raw))


def last_raw_kernel(w_ref, x_ref, raw_ref, sq_ref, x, total, came):
    blocks = x_ref.shape[0] // FEW
    wait = fetch(
        lambda k: [(x_ref.at[columns(k, blocks)], x.at[columns(k, blocks)])],
        came,
        FEW,
    )
    total[...] = jnp.zeros_like(total)
    w = split(w_ref[...])

    def block(k):
        c = columns(k, blocks * LANES)
        wait(k)
        part = jnp.concatenate([x[k * blocks + q] for q in range(blocks)], axis=1)
        raw = dot3(w, split(part), NN)
        raw_ref[0, :, c], raw_ref[1, :, c] = split(raw)
        square = raw * raw
        for q in range(blocks):
            total[...] += square[:, q * LANES : (q + 1) * LANES]

    each(block, FEW)
    row = exact(jnp.ones((8, LANES), F32), total[...], NT)
    for k in range(sq_ref.shape[0]):
        sq_ref[k] = row


def last_raw(w, x, peers):
    rank = w.shape[0]
    cols = x.shape[0] * LANES
    return call(
        last_raw_kernel,
        [VM, ANY],
        [pair((rank, cols)), jax.ShapeDtypeStruct((peers, 8, rank), F32)],
        [VM] * 2,
        [
            pltpu.VMEM(x.shape, F32),
            pltpu.VMEM((rank, LANES), F32),
            dma(FEW, 1),
        ],
        6 * rank * cols * rank,
    )(w, *in_hbm(x))


def state_kernel(o_ref, raw_ref, b_ref, s_ref, b, buffer, came, sent):
    wait = fetch(pair_moves(b_ref, b), came)
    o = split((1.0 - KEEP_RATE) * o_ref[...])

    def value(k, c):
        wait(k)
        b_now = b[0, :, c].astype(F32) + b[1, :, c].astype(F32)
        return b_now - dot3(o, (raw_ref[0, :, c], raw_ref[1, :, c]), NN)

    write_out(value, s_ref, buffer, sent)


def last_state(o, raw, b):
    _, rows, cols = b.shape
    return call(
        state_kernel,
        [VM, VM, ANY],
        pltpu.HBM((rows, cols), F32),
        ANY,
        [
            pltpu.VMEM(b.shape, BF16),
            pltpu.VMEM((rows, cols), F32),
            dma(CHUNKS, 1),
            dma(CHUNKS, 1),
        ],
        6 * rows * cols * o.shape[1],
    )(o, raw, *in_hbm(b))


def last_change_kernel(
    factor, o_ref, sq_ref, raw_ref, c_ref, out_ref, held, buffer, came, sent
):
    width = held.shape[1] // CHUNKS
    wait = fetch(
        lambda k: [(c_ref.at[:, columns(k, width)], held.at[:, columns(k, width)])], came
    )
    total = sq_ref[0, :1]
    for k in range(1, sq_ref.shape[0]):
        total = total + sq_ref[k, :1]
    o = split(o_ref[...] * (factor * lax.rsqrt(total + NORM_EPS)))

    def value(k, c):
        wait(k)
        return held[:, c] + dot3(o, (raw_ref[0, :, c], raw_ref[1, :, c]), NN)

    write_out(value, out_ref, buffer, sent)


def last_change(factor, o, sq, raw, change):
    rows, cols = change.shape
    return call(
        functools.partial(last_change_kernel, factor),
        [VM, VM, VM, ANY],
        pltpu.HBM((rows, cols), BF16),
        ANY,
        [
            pltpu.VMEM((rows, cols), F32),
            pltpu.VMEM((rows, cols), BF16),
            dma(CHUNKS, 1),
            dma(CHUNKS, 1),
        ],
        6 * rows * cols * o.shape[1],
    )(o, sq, raw, *in_hbm(change))


SIDE = 4


def chip_permute(x, move):
    pairs = [(2 * k + c, 2 * move(k) + c) for k in range(SIDE) for c in range(2)]
    return lax.ppermute(x, "col", pairs)


def core_permute(x):
    return lax.ppermute(x, "col", [(k, k ^ 1) for k in range(2 * SIDE)])


def near(k):
    return k ^ 1


def far(k):
    return SIDE - 1 - k


def col_sum(parts, beside):
    core = lax.axis_index("col") % 2
    mine = lax.dynamic_slice_in_dim(parts, 2 * core, 2, 0)
    theirs = lax.dynamic_slice_in_dim(parts, 2 - 2 * core, 2, 0)
    mine = mine + core_permute(theirs)
    a, b, done = mine[0], mine[1], []
    for half, moves in enumerate(((near, far), (far, near))):
        from_a, from_b, done = lax.optimization_barrier(
            (chip_permute(a, moves[0]), chip_permute(b, moves[1]), beside(half, done))
        )
        a, b = a + from_a, b + from_b
    mine = jnp.stack([a, b])
    return mine, core_permute(mine), done


def by_chip(part):
    core = lax.axis_index("col") % 2
    other = core_permute(part)
    chip = jnp.where(
        core == 0, jnp.concatenate([part, other]), jnp.concatenate([other, part])
    )
    return [chip] + [
        chip_permute(chip, lambda k, d=d: (k - d) % SIDE) for d in range(1, SIDE)
    ]


def exchange(x, axis):
    return lax.all_to_all(x, axis, 0, 0, tiled=True)


def row_total(blocks, p, place, beside):
    own, part = spread_sum(exchange(blocks, "row"), p.shape[1])
    total, extra = lax.optimization_barrier((exchange(own, "row"), beside(part)))
    return total, *inverse_factor(by_chip(part), place, p), extra


def shards(momentum, grads, basis):
    rows, cols = momentum.shape
    rank = basis.shape[1]
    peers = lax.axis_size("col")
    factor = (rows * lax.axis_size("row") * cols * peers / rank) ** 0.5
    place = lax.axis_index("col").astype(jnp.int32)[None]

    held = [pltpu.VMEM((rows, cols), F32), pltpu.VMEM((1, rows, cols), BF16)]
    part = first_projection(momentum, grads, basis)
    mine, theirs, _ = col_sum(part.reshape(4, rows // 4, rank), lambda half, done: [])
    x1, p1, _ = products(
        first_products_kernel, place, mine, theirs, [momentum, grads], held, peers
    )
    x1, w1, o1, ahead = row_total(
        x1, p1, place, lambda part: buffer_ahead(part, momentum, grads)
    )
    part, rt1 = middle(o1, w1, x1, ahead)
    mine, theirs, (raw1, buffer) = col_sum(
        part, lambda half, done: second_buffer(half, o1, w1, rt1, ahead, done)
    )
    held = [pltpu.VMEM((2, rows, cols), BF16)]
    x2, p2, rs1 = products(
        second_products_kernel, place, mine, theirs, [buffer], held, peers
    )
    x2, w2, o2, change1 = row_total(
        x2, p2, place, lambda part: first_change(factor, part, o1, rs1, raw1)
    )
    raw2, sq2 = last_raw(w2, x2, peers)
    sq2, state = lax.optimization_barrier(
        (exchange(sq2, "col"), last_state(o2, raw2, buffer))
    )
    change = last_change(factor, o2, sq2, raw2, change1)
    return change, state


def solution(mesh):
    return jax.shard_map(
        shards,
        mesh=mesh,
        in_specs=(P("row", "col"), P(None, "row", "col"), P("col", None)),
        out_specs=(P("row", "col"), P("row", "col")),
        check_vma=False,
    )
```

```python
import functools

import jax
import jax.numpy as jnp
from jax import lax
from jax.experimental import pallas as pl
from jax.experimental.pallas import tpu as pltpu
from jax.sharding import PartitionSpec as P

KEEP_RATE = 0.95
NORM_EPS = 1e-06
LANES = 128
CHUNKS = 4
FEW = 2
F32 = jnp.float32
BF16 = jnp.bfloat16
VMEM_LIMIT = 20 * 1024 * 1024
NN = (((1,), (0,)), ((), ()))
NT = (((1,), (1,)), ((), ()))


def split(x):
    high = x.astype(BF16)
    return high, (x - high.astype(F32)).astype(BF16)


def mm(a, b, dims):
    return lax.dot_general(a, b, dims, preferred_element_type=F32)


def dot3(a, b, dims):
    return mm(a[0], b[0], dims) + (mm(a[0], b[1], dims) + mm(a[1], b[0], dims))


def exact(a, b, dims):
    return lax.dot_general(
        a, b, dims, precision=lax.Precision.HIGHEST, preferred_element_type=F32
    )


def call(kernel, in_specs, out_shape, out_specs, scratch, cost, aliases=None):
    return pl.pallas_call(
        kernel,
        in_specs=in_specs,
        out_specs=out_specs,
        out_shape=out_shape,
        scratch_shapes=scratch,
        input_output_aliases=aliases or {},
        compiler_params=pltpu.CompilerParams(vmem_limit_bytes=VMEM_LIMIT),
        cost_estimate=pl.CostEstimate(
            flops=cost, transcendentals=0, bytes_accessed=8 * 1024 * 1024
        ),
    )


VM = pl.BlockSpec(memory_space=pltpu.VMEM)
SM = pl.BlockSpec(memory_space=pltpu.SMEM)
ANY = pl.BlockSpec(memory_space=pl.ANY)


def in_hbm(*arrays):
    return [pltpu.with_memory_space_constraint(a, pltpu.HBM) for a in arrays]


def pair(shape):
    return jax.ShapeDtypeStruct((2, *shape), BF16)


def pair_in_hbm(shape):
    return pltpu.HBM((2, *shape), BF16)


def dma(*shape):
    return pltpu.SemaphoreType.DMA(shape)


def fetch(moves, sems, count=CHUNKS):
    def copies(k):
        return [
            pltpu.make_async_copy(a, b, sems.at[k, n]) for n, (a, b) in enumerate(moves(k))
        ]

    for k in range(count):
        for copy in copies(k):
            copy.start()

    def wait(k):
        for copy in copies(k):
            copy.wait()

    return wait


def send(moves, sems, count=CHUNKS):
    def copies(k):
        return [
            pltpu.make_async_copy(a, b, sems.at[k, n]) for n, (a, b) in enumerate(moves(k))
        ]

    def start(k):
        for copy in copies(k):
            copy.start()

    def finish():
        for k in range(count):
            for copy in copies(k):
                copy.wait()

    return start, finish


def columns(k, width):
    if isinstance(k, int):
        return pl.ds(k * width, width)
    return pl.ds(pl.multiple_of(k * width, width), width)


def each(block, count=CHUNKS):
    lax.fori_loop(0, count, lambda k, _: (block(k), 0)[1], 0)


def lower(n):
    i = lax.broadcasted_iota(jnp.int32, (n, n), 0)
    return i >= lax.broadcasted_iota(jnp.int32, (n, n), 1)


def same(n):
    i = lax.broadcasted_iota(jnp.int32, (n, n), 0)
    return i == lax.broadcasted_iota(jnp.int32, (n, n), 1)


def buffer_moves(m_ref, g_ref, m, g):
    width = m.shape[1] // CHUNKS

    def moves(k):
        c = columns(k, width)
        pairs = [(m_ref.at[:, c], m.at[:, c])]
        for n in range(g.shape[0]):
            pairs.append((g_ref.at[n, :, c], g.at[n, :, c]))
        return pairs

    return moves


def buffer_block(m, g, c):
    b = m[:, c]
    for n in range(g.shape[0]):
        b = b + g[n, :, c].astype(F32)
    return b


def first_kernel(m_ref, g_ref, v_ref, p_ref, m, g, v, sems):
    width = m.shape[1] // CHUNKS
    moves = buffer_moves(m_ref, g_ref, m, g)
    wait = fetch(
        lambda k: moves(k) + [(v_ref.at[columns(k, width)], v.at[columns(k, width)])], sems
    )
    p_ref[...] = jnp.zeros_like(p_ref)

    def block(k):
        c = columns(k, width)
        wait(k)
        p_ref[...] += dot3(split(buffer_block(m, g, c)), split(v[c]), NN)

    each(block)


def first_projection(momentum, grads, basis):
    rows, cols = momentum.shape
    rank = basis.shape[1]
    return call(
        first_kernel,
        [ANY] * 3,
        jax.ShapeDtypeStruct((rows, rank), F32),
        VM,
        [
            pltpu.VMEM((rows, cols), F32),
            pltpu.VMEM((1, rows, cols), BF16),
            pltpu.VMEM((cols, rank), F32),
            dma(CHUNKS, 3),
        ],
        6 * rows * cols * rank,
    )(*in_hbm(momentum, grads, basis))


def store_products(inputs, outputs, scratch, block, scaled, count):
    n_ref, mine_ref, theirs_ref = inputs
    x_ref, p_ref, rs_ref = outputs
    parts, t, shares, pair_of_p = scratch
    core = lax.rem(n_ref[0], 2)
    parts[pl.ds(2 * core, 2)] = mine_ref[...]
    parts[pl.ds(2 - 2 * core, 2)] = theirs_ref[...]
    rows, rank = p_ref.shape
    height = rows // 4
    p = jnp.concatenate([parts[k, :height] for k in range(4)], axis=0)
    if scaled:
        rs = lax.rsqrt(parts[0, height : height + 8] + NORM_EPS)
        p = p * rs[:1]
    else:
        rs = jnp.ones(rs_ref.shape, F32)
    rs_ref[...] = rs
    p_ref[...] = p
    turned, half = p.T, LANES
    gram = exact(turned, p, NN)
    head, last = gram[:half, :half], gram[half:, half:]
    t[:half] = jnp.where(lower(half), head, last)
    t[half : 2 * half] = gram[half:, :half]
    diagonal = jnp.sum(jnp.where(same(half), last, 0.0), axis=0, keepdims=True)
    t[2 * half :] = jnp.broadcast_to(diagonal, (t.shape[0] - 2 * half, half))
    size = x_ref.shape[1] - rank
    share = t[pl.ds(pl.multiple_of(n_ref[0] * size, size), size), :]
    pt = split(turned)
    blocks = x_ref.shape[0] // count
    shares[...] = share
    pair_of_p[0], pair_of_p[1] = pt

    def fill(k):
        r = dot3((pair_of_p[0], pair_of_p[1]), block(k), NN)
        for q in range(blocks):
            x_ref[k * blocks + q, :rank] = r[:, q * LANES : (q + 1) * LANES]
            x_ref[k * blocks + q, rank:] = shares[...]

    each(fill, count)


def first_products_kernel(
    n_ref, mine_ref, theirs_ref, m_ref, g_ref, x_ref, p_ref, rs_ref, m, g, came, *scratch
):
    wait = fetch(buffer_moves(m_ref, g_ref, m, g), came)

    def block(k):
        wait(k)
        return split(buffer_block(m, g, columns(k, m.shape[1] // CHUNKS)))

    store_products(
        (n_ref, mine_ref, theirs_ref), (x_ref, p_ref, rs_ref), scratch, block, False, CHUNKS
    )


def pair_moves(b_ref, b, count=CHUNKS):
    width = b.shape[2] // count

    def moves(k):
        c = columns(k, width)
        return [(b_ref.at[:, :, c], b.at[:, :, c])]

    return moves


def second_products_kernel(
    n_ref, mine_ref, theirs_ref, b_ref, x_ref, p_ref, rs_ref, b, came, *scratch
):
    wait = fetch(pair_moves(b_ref, b, FEW), came, FEW)

    def block(k):
        wait(k)
        c = columns(k, b.shape[2] // FEW)
        return b[0, :, c], b[1, :, c]

    store_products(
        (n_ref, mine_ref, theirs_ref), (x_ref, p_ref, rs_ref), scratch, block, True, FEW
    )


def products(kernel, place, mine, theirs, bigs, held, peers):
    rows, cols = bigs[0].shape[-2:]
    _, height, rank = mine.shape
    tail = -(-(2 * LANES + 8) // (8 * peers)) * 8
    shape = (cols // LANES, rank + tail, LANES)
    return call(
        kernel,
        [SM, VM, VM] + [ANY] * len(bigs),
        [
            jax.ShapeDtypeStruct(shape, F32),
            jax.ShapeDtypeStruct((rows, rank), F32),
            jax.ShapeDtypeStruct((8, rank), F32),
        ],
        [VM, VM, VM],
        held
        + [
            dma(CHUNKS, len(bigs)),
            pltpu.VMEM((4, height, rank), F32),
            pltpu.VMEM((peers * tail, LANES), F32),
            pltpu.VMEM((tail, LANES), F32),
            pltpu.VMEM((2, rank, rows), BF16),
        ],
        6 * rows * cols * rank,
    )(place, mine, theirs, *in_hbm(*bigs))


def spread_kernel(x_ref, y_ref, t_ref, y, sems):
    count = x_ref.shape[0]
    rank = y.shape[0]
    total = x_ref[0]
    for k in range(1, count):
        total = total + x_ref[k]
    y[...] = total[:rank]
    copies = [
        pltpu.make_async_copy(y, y_ref.at[k], sems.at[k]) for k in range(count)
    ]
    for copy in copies:
        copy.start()
    t_ref[...] = total[rank:]
    for copy in copies:
        copy.wait()


def spread_sum(x, rank):
    count, height, width = x.shape
    return call(
        spread_kernel,
        [VM],
        [
            pltpu.HBM((count, rank, width), F32),
            jax.ShapeDtypeStruct((height - rank, width), F32),
        ],
        [ANY, VM],
        [pltpu.VMEM((rank, width), F32), pltpu.SemaphoreType.DMA((count,))],
        count * height * width,
    )(x)


def two_columns(a, b, d, row0, row1, first, second):
    inv = 1.0 / (a * d - b * b)
    i00, i01, i11 = d * inv, -b * inv, a * inv
    e0 = jnp.where(first, 1.0, jnp.where(second, 0.0, row0))
    e1 = jnp.where(first, 0.0, jnp.where(second, 1.0, row1))
    ratio = b / a
    kept = jnp.where(first, -ratio, row1 - ratio * row0)
    return (i00, i01, i11), i00 * e0 + i01 * e1, i01 * e0 + i11 * e1, kept


def eliminated(m):
    n = m.shape[0]
    eye = same(n)
    across = lax.rsqrt(jnp.sum(jnp.where(eye, m, 0.0), axis=0, keepdims=True))
    down = lax.rsqrt(jnp.sum(jnp.where(eye, m, 0.0), axis=1, keepdims=True))
    m = m * down * across
    lane = lax.broadcasted_iota(jnp.int32, (8, n), 1)
    sub = lax.broadcasted_iota(jnp.int32, (8, n), 0)
    tiles = [m[8 * t : 8 * t + 8] for t in range(n // 8)]
    for j in range(0, n, 4):
        t, r = divmod(j, 8)
        here = [lane[:1] == j + k for k in range(4)]
        left, right = here[0] | here[1], here[2] | here[3]
        all_four = (lane >= j) & (lane < j + 4)
        c = [
            [jnp.broadcast_to(x[:, j + k : j + k + 1], (8, n)) for x in tiles[t:]]
            for k in range(4)
        ]
        rows = [tiles[t][r + k : r + k + 1] for k in range(4)]

        def at(k, l):
            return c[l][0][r + k : r + k + 1]

        (i00, i01, i11), use0, use1, kept1 = two_columns(
            at(0, 0), at(1, 0), at(1, 1), rows[0], rows[1], here[0], here[1]
        )
        f2, g2 = i00 * at(2, 0) + i01 * at(2, 1), i01 * at(2, 0) + i11 * at(2, 1)
        f3, g3 = i00 * at(3, 0) + i01 * at(3, 1), i01 * at(3, 0) + i11 * at(3, 1)
        row2 = jnp.where(left, 0.0, rows[2]) - at(2, 0) * use0 - at(2, 1) * use1
        row3 = jnp.where(left, 0.0, rows[3]) - at(3, 0) * use0 - at(3, 1) * use1
        _, use2, use3, kept3 = two_columns(
            at(2, 2) - at(2, 0) * f2 - at(2, 1) * g2,
            at(3, 2) - at(3, 0) * f2 - at(3, 1) * g2,
            at(3, 3) - at(3, 0) * f3 - at(3, 1) * g3,
            row2,
            row3,
            here[2],
            here[3],
        )
        use0, use1 = jnp.where(right, 0.0, use0), jnp.where(right, 0.0, use1)
        for s in range(t, n // 8):
            c0, c1, c2, c3 = (c[k][s - t] for k in range(4))
            c2 = c2 - c0 * f2 - c1 * g2
            c3 = c3 - c0 * f3 - c1 * g3
            new = jnp.where(all_four, 0.0, tiles[s]) - c0 * use0 - c1 * use1
            new = new - c2 * use2 - c3 * use3
            if s == t:
                own = jnp.where(sub == r + 1, kept1, tiles[s])
                own = jnp.where(sub == r + 2, row2, own)
                own = jnp.where(sub == r + 3, kept3, own)
                new = jnp.where(sub > r + 3, new, own)
            tiles[s] = new
    m = jnp.concatenate(tiles, axis=0)
    i = lax.broadcasted_iota(jnp.int32, (n, n), 0)
    j = lax.broadcasted_iota(jnp.int32, (n, n), 1)
    pivots = jnp.sum(jnp.where(eye, m, 0.0), axis=1, keepdims=True)
    unit = jnp.where(i > j, m, jnp.where(eye, 1.0, 0.0))
    return unit * lax.rsqrt(pivots) * across


def cholesky_kernel(n_ref, p_ref, *refs):
    pieces, (w_ref, o_ref, packed, a, low) = refs[:-5], refs[-5:]
    size = pieces[0].shape[0]
    count = len(pieces)
    for k, piece in enumerate(pieces):
        place = lax.rem(n_ref[0] // 2 + k, count)
        packed[pl.ds(pl.multiple_of(place * size, size), size), :] = piece[...]
    half = LANES
    both = packed[:half]
    turned = both.T
    a[:half] = jnp.where(lower(half), both, turned)
    a[half : 2 * half] = packed[half : 2 * half]
    a[2 * half :] = jnp.where(
        same(half), packed[2 * half : 2 * half + 1], jnp.where(lower(half), turned, both)
    )

    def body(b, carry):
        w = eliminated(a[pl.ds(pl.multiple_of(2 * b * half, half), half), :])
        first = pl.multiple_of(b * half, half)
        w_ref[pl.ds(first, half), pl.ds(first, half)] = w

        @pl.when(b == 0)
        def _():
            low[...] = exact(a[half : 2 * half], w, NT)
            a[2 * half :] -= exact(low[...], low[...], NT)

        return carry

    lax.fori_loop(0, 2, body, 0)
    w_ref[:half, half:] = jnp.zeros((half, half), F32)
    w_ref[half:, :half] = -exact(
        w_ref[half:, half:], exact(low[...], w_ref[:half, :half], NN), NN
    )
    o_ref[...] = exact(p_ref[...], w_ref[...], NT)


def inverse_factor(pieces, place, p):
    rank = p.shape[1]
    return call(
        cholesky_kernel,
        [SM, VM] + [VM] * len(pieces),
        [jax.ShapeDtypeStruct((rank, rank), F32), jax.ShapeDtypeStruct(p.shape, F32)],
        [VM, VM],
        [
            pltpu.VMEM((len(pieces) * pieces[0].shape[0], LANES), F32),
            pltpu.VMEM((3 * LANES, LANES), F32),
            pltpu.VMEM((LANES, LANES), F32),
        ],
        10**10,
    )(place, p, *pieces)


def ahead_kernel(after_ref, m_ref, g_ref, a_ref, m, g, a, came, sent):
    del after_ref
    width = m.shape[1] // CHUNKS
    wait = fetch(buffer_moves(m_ref, g_ref, m, g), came)
    start, finish = send(
        lambda k: [(a.at[:, :, columns(k, width)], a_ref.at[:, :, columns(k, width)])], sent
    )

    def block(k):
        c = columns(k, width)
        wait(k)
        a[0, :, c], a[1, :, c] = split(buffer_block(m, g, c))
        start(k)

    each(block)
    finish()


def buffer_ahead(after, momentum, grads):
    rows, cols = momentum.shape
    return call(
        ahead_kernel,
        [VM] + [ANY] * 2,
        pair_in_hbm((rows, cols)),
        ANY,
        [
            pltpu.VMEM((rows, cols), F32),
            pltpu.VMEM(grads.shape, BF16),
            pltpu.VMEM((2, rows, cols), BF16),
            dma(CHUNKS, 3),
            dma(CHUNKS, 1),
        ],
        8 * rows * cols,
    )(after, *in_hbm(momentum, grads))


def middle_kernel(o_ref, w_ref, x_ref, a_ref, q_ref, rt_ref, a, q_sum, s_ref, sems):
    wait = fetch(pair_moves(a_ref, a, FEW), sems, FEW)

    def turn(k):
        c = columns(k, LANES)
        rt_ref[0, :, c], rt_ref[1, :, c] = split(x_ref[k])

    each(turn, x_ref.shape[0])
    rt = (rt_ref[0], rt_ref[1])
    w = split(w_ref[...])
    s_ref[...] = dot3(split(dot3(w, split(dot3(rt, rt, NT)), NN)), w, NT)
    width = a.shape[2] // FEW
    q_sum[...] = jnp.zeros_like(q_sum)

    def block(k):
        c = columns(k, width)
        wait(k)
        q_sum[...] += dot3(
            (a[0, :, c], a[1, :, c]), (rt_ref[0, :, c], rt_ref[1, :, c]), NT
        )

    each(block, FEW)
    s = s_ref[...]
    q = dot3(split(q_sum[...]), split(w_ref[...]), NT) - dot3(
        split((1.0 - KEEP_RATE) * o_ref[...]), split(s), NN
    )
    n = s.shape[0]
    squares = jnp.sum(jnp.where(same(n), s, 0.0), axis=0, keepdims=True)
    height = q_ref.shape[1] - 8
    for k in range(q_ref.shape[0]):
        q_ref[k, :height] = q[k * height : (k + 1) * height]
        q_ref[k, height:] = jnp.broadcast_to(squares, (8, n))


def middle(o, w, x, ahead):
    _, rows, cols = ahead.shape
    rank = o.shape[1]
    return call(
        middle_kernel,
        [VM] * 3 + [ANY],
        [jax.ShapeDtypeStruct((4, rows // 4 + 8, rank), F32), pair((rank, cols))],
        [VM] * 2,
        [
            pltpu.VMEM((2, rows, cols), BF16),
            pltpu.VMEM((rows, rank), F32),
            pltpu.VMEM((rank, rank), F32),
            dma(FEW, 1),
        ],
        10 * rows * cols * rank,
    )(o, w, x, *in_hbm(ahead))


def update_kernel(half, o_ref, w_ref, rt_ref, a_ref, *refs):
    raw_ref, b_ref, a, raw, b, came, sent = refs[-7:]
    count = CHUNKS // 2
    width = a.shape[2] // count
    base = half * a.shape[2]

    def placed(k):
        if isinstance(k, int):
            return pl.ds(base + k * width, width)
        return pl.ds(pl.multiple_of(base + k * width, width), width)

    def moves(k):
        return [(a_ref.at[:, :, placed(k)], a.at[:, :, columns(k, width)])]

    wait = fetch(moves, came, count)
    start, finish = send(
        lambda k: [
            (raw.at[:, :, columns(k, width)], raw_ref.at[:, :, placed(k)]),
            (b.at[:, :, columns(k, width)], b_ref.at[:, :, placed(k)]),
        ],
        sent,
        count,
    )
    o = split((1.0 - KEEP_RATE) * o_ref[...])
    w = split(w_ref[...])

    def block(k):
        c, there = columns(k, width), placed(k)
        now = split(dot3(w, (rt_ref[0, :, there], rt_ref[1, :, there]), NN))
        raw[0, :, c], raw[1, :, c] = now
        wait(k)
        b[0, :, c], b[1, :, c] = split(
            a[0, :, c].astype(F32) + a[1, :, c].astype(F32) - dot3(o, now, NN)
        )
        start(k)

    each(block, count)
    finish()


def second_buffer(half, o, w, rt, ahead, begun):
    _, rows, cols = ahead.shape
    rank = o.shape[1]
    part = cols // 2
    return call(
        functools.partial(update_kernel, half),
        [VM] * 3 + [ANY] * (1 + len(begun)),
        [pair_in_hbm((rank, cols)), pair_in_hbm((rows, cols))],
        [ANY] * 2,
        [
            pltpu.VMEM((2, rows, part), BF16),
            pltpu.VMEM((2, rank, part), BF16),
            pltpu.VMEM((2, rows, part), BF16),
            dma(CHUNKS // 2, 1),
            dma(CHUNKS // 2, 2),
        ],
        5 * rows * cols * rank,
        {4: 0, 5: 1} if begun else None,
    )(o, w, rt, *in_hbm(ahead), *in_hbm(*begun))


def write_out(value, out_ref, buffer, sems, count=CHUNKS):
    width = buffer.shape[1] // count
    start, finish = send(
        lambda k: [(buffer.at[:, columns(k, width)], out_ref.at[:, columns(k, width)])],
        sems,
        count,
    )

    def block(k):
        c = columns(k, width)
        buffer[:, c] = value(k, c).astype(buffer.dtype)
        start(k)

    each(block, count)
    finish()


def first_change_kernel(
    factor, after_ref, o_ref, rs_ref, raw_ref, c_ref, raw, buffer, came, sent
):
    del after_ref
    wait = fetch(pair_moves(raw_ref, raw), came)
    o = split(o_ref[...] * (factor * rs_ref[:1]))

    def value(k, c):
        wait(k)
        return dot3(o, (raw[0, :, c], raw[1, :, c]), NN)

    write_out(value, c_ref, buffer, sent)


def first_change(factor, after, o, rs, raw):
    rows, rank = o.shape
    cols = raw.shape[2]
    return call(
        functools.partial(first_change_kernel, factor),
        [VM, VM, VM, ANY],
        pltpu.HBM((rows, cols), F32),
        ANY,
        [
            pltpu.VMEM(raw.shape, BF16),
            pltpu.VMEM((rows, cols), F32),
            dma(CHUNKS, 1),
            dma(CHUNKS, 1),
        ],
        6 * rows * cols * rank,
    )(after, o, rs, *in_hbm(raw))


def last_raw_kernel(w_ref, x_ref, raw_ref, sq_ref, x, total, came):
    blocks = x_ref.shape[0] // FEW
    wait = fetch(
        lambda k: [(x_ref.at[columns(k, blocks)], x.at[columns(k, blocks)])],
        came,
        FEW,
    )
    total[...] = jnp.zeros_like(total)
    w = split(w_ref[...])

    def block(k):
        c = columns(k, blocks * LANES)
        wait(k)
        part = jnp.concatenate([x[k * blocks + q] for q in range(blocks)], axis=1)
        raw = dot3(w, split(part), NN)
        raw_ref[0, :, c], raw_ref[1, :, c] = split(raw)
        square = raw * raw
        for q in range(blocks):
            total[...] += square[:, q * LANES : (q + 1) * LANES]

    each(block, FEW)
    row = exact(jnp.ones((8, LANES), F32), total[...], NT)
    for k in range(sq_ref.shape[0]):
        sq_ref[k] = row


def last_raw(w, x, peers):
    rank = w.shape[0]
    cols = x.shape[0] * LANES
    return call(
        last_raw_kernel,
        [VM, ANY],
        [pair((rank, cols)), jax.ShapeDtypeStruct((peers, 8, rank), F32)],
        [VM] * 2,
        [
            pltpu.VMEM(x.shape, F32),
            pltpu.VMEM((rank, LANES), F32),
            dma(FEW, 1),
        ],
        6 * rank * cols * rank,
    )(w, *in_hbm(x))


def state_kernel(o_ref, raw_ref, b_ref, s_ref, b, buffer, came, sent):
    wait = fetch(pair_moves(b_ref, b), came)
    o = split((1.0 - KEEP_RATE) * o_ref[...])

    def value(k, c):
        wait(k)
        b_now = b[0, :, c].astype(F32) + b[1, :, c].astype(F32)
        return b_now - dot3(o, (raw_ref[0, :, c], raw_ref[1, :, c]), NN)

    write_out(value, s_ref, buffer, sent)


def last_state(o, raw, b):
    _, rows, cols = b.shape
    return call(
        state_kernel,
        [VM, VM, ANY],
        pltpu.HBM((rows, cols), F32),
        ANY,
        [
            pltpu.VMEM(b.shape, BF16),
            pltpu.VMEM((rows, cols), F32),
            dma(CHUNKS, 1),
            dma(CHUNKS, 1),
        ],
        6 * rows * cols * o.shape[1],
    )(o, raw, *in_hbm(b))


def last_change_kernel(
    factor, o_ref, sq_ref, raw_ref, c_ref, out_ref, held, buffer, came, sent
):
    width = held.shape[1] // CHUNKS
    wait = fetch(
        lambda k: [(c_ref.at[:, columns(k, width)], held.at[:, columns(k, width)])], came
    )
    total = sq_ref[0, :1]
    for k in range(1, sq_ref.shape[0]):
        total = total + sq_ref[k, :1]
    o = split(o_ref[...] * (factor * lax.rsqrt(total + NORM_EPS)))

    def value(k, c):
        wait(k)
        return held[:, c] + dot3(o, (raw_ref[0, :, c], raw_ref[1, :, c]), NN)

    write_out(value, out_ref, buffer, sent)


def last_change(factor, o, sq, raw, change):
    rows, cols = change.shape
    return call(
        functools.partial(last_change_kernel, factor),
        [VM, VM, VM, ANY],
        pltpu.HBM((rows, cols), BF16),
        ANY,
        [
            pltpu.VMEM((rows, cols), F32),
            pltpu.VMEM((rows, cols), BF16),
            dma(CHUNKS, 1),
            dma(CHUNKS, 1),
        ],
        6 * rows * cols * o.shape[1],
    )(o, sq, raw, *in_hbm(change))


SIDE = 4


def chip_permute(x, move):
    pairs = [(2 * k + c, 2 * move(k) + c) for k in range(SIDE) for c in range(2)]
    return lax.ppermute(x, "col", pairs)


def core_permute(x):
    return lax.ppermute(x, "col", [(k, k ^ 1) for k in range(2 * SIDE)])


def near(k):
    return k ^ 1


def far(k):
    return SIDE - 1 - k


def col_sum(parts, beside):
    core = lax.axis_index("col") % 2
    mine = lax.dynamic_slice_in_dim(parts, 2 * core, 2, 0)
    theirs = lax.dynamic_slice_in_dim(parts, 2 - 2 * core, 2, 0)
    mine = mine + core_permute(theirs)
    a, b, done = mine[0], mine[1], []
    for half, moves in enumerate(((near, far), (far, near))):
        from_a, from_b, done = lax.optimization_barrier(
            (chip_permute(a, moves[0]), chip_permute(b, moves[1]), beside(half, done))
        )
        a, b = a + from_a, b + from_b
    mine = jnp.stack([a, b])
    return mine, core_permute(mine), done


def by_chip(part):
    core = lax.axis_index("col") % 2
    other = core_permute(part)
    chip = jnp.where(
        core == 0, jnp.concatenate([part, other]), jnp.concatenate([other, part])
    )
    return [chip] + [
        chip_permute(chip, lambda k, d=d: (k - d) % SIDE) for d in range(1, SIDE)
    ]


def exchange(x, axis):
    return lax.all_to_all(x, axis, 0, 0, tiled=True)


def row_total(blocks, p, place, beside):
    own, part = spread_sum(exchange(blocks, "row"), p.shape[1])
    total, extra = lax.optimization_barrier((exchange(own, "row"), beside(part)))
    return total, *inverse_factor(by_chip(part), place, p), extra


def shards(momentum, grads, basis):
    rows, cols = momentum.shape
    rank = basis.shape[1]
    peers = lax.axis_size("col")
    factor = (rows * lax.axis_size("row") * cols * peers / rank) ** 0.5
    place = lax.axis_index("col").astype(jnp.int32)[None]

    held = [pltpu.VMEM((rows, cols), F32), pltpu.VMEM((1, rows, cols), BF16)]
    part = first_projection(momentum, grads, basis)
    mine, theirs, _ = col_sum(part.reshape(4, rows // 4, rank), lambda half, done: [])
    x1, p1, _ = products(
        first_products_kernel, place, mine, theirs, [momentum, grads], held, peers
    )
    x1, w1, o1, ahead = row_total(
        x1, p1, place, lambda part: buffer_ahead(part, momentum, grads)
    )
    part, rt1 = middle(o1, w1, x1, ahead)
    mine, theirs, (raw1, buffer) = col_sum(
        part, lambda half, done: second_buffer(half, o1, w1, rt1, ahead, done)
    )
    held = [pltpu.VMEM((2, rows, cols), BF16)]
    x2, p2, rs1 = products(
        second_products_kernel, place, mine, theirs, [buffer], held, peers
    )
    x2, w2, o2, change1 = row_total(
        x2, p2, place, lambda part: first_change(factor, part, o1, rs1, raw1)
    )
    raw2, sq2 = last_raw(w2, x2, peers)
    sq2, state = lax.optimization_barrier(
        (exchange(sq2, "col"), last_state(o2, raw2, buffer))
    )
    change = last_change(factor, o2, sq2, raw2, change1)
    return change, state


def solution(mesh):
    return jax.shard_map(
        shards,
        mesh=mesh,
        in_specs=(P("row", "col"), P(None, "row", "col"), P("col", None)),
        out_specs=(P("row", "col"), P("row", "col")),
        check_vma=False,
    )
```
